32 devices in a mesh: grp: 2 (over x), gz: 8 (over z, y), col: 2 (over core).
Axes of the slice: x: 2, y: 2, z: 4, core: 2. Of those that a mesh axis runs over, the one named last changes fastest.
Arguments:
- noisy_image: float32 [4, 1024, 768], P('grp', 'gz', 'col'), parts along dimension 0, may hold values from -6 to 6
- fresh_noise: float32 [4, 1024, 768], P('grp', 'gz', 'col'), parts along dimension 0, may hold values from -6 to 6
- coil_maps: float32 [8, 4, 1024, 768], P('col', 'grp', 'gz'), parts along dimension 1, may hold values from -1.5 to 1.5
- measured: float32 [4, 768, 8, 1024], P('grp', 'gz', 'col'), parts along dimension 0, may hold values from -2.4 to 2.4
- sampled: int32 [768, 2048], P('gz', 'grp'), parts along dimension 1, may hold values 0 or 1
- first_kernel: bfloat16 [9, 64, 2], replicated, may hold values from -1.5 to 1.5
- inner_kernels: bfloat16 [1, 9, 64, 64], replicated, may hold values from -0.25 to 0.25
- last_kernel: bfloat16 [9, 2, 64], replicated, may hold values from -0.25 to 0.25
Outputs:
- next_image: float32 [4, 1024, 768], P('grp', 'gz', 'col'), parts along dimension 0
The draws below stay inside these ranges and needn't reach their ends.
There are 2 independent parts, one for each index of `grp`. The reference program is written for one: setup_inputs(seed, part) draws one part's arguments, and reference() takes and returns one part's arrays. A program takes and returns all parts, laid end to end along the dimension named above; an argument that names none is the same for every part. Nothing has to cross between parts.
All inputs are finite; a program needn't handle non-finite values. No bound on the sum of `sampled` on one device may be relied on, other than what follows from the above.
Results may differ from the reference program's by a relative error of at most 0.00044.
Values may be sent and summed in bfloat16 or wider, within the bound.
No kernel may reach another device: no remote copies, remote signals or barrier semaphores. Data moves between devices by JAX's collectives and lax.ppermute only.
A program may use at most 128 MiB of HBM per device.

```python
import jax
import jax.numpy as jnp
from jax import lax

H = 1024
W = 768
CH = 64
COILS = 8
MID_LAYERS = 1


def place_ends(values, stream_key, low, top_value):
    longest = values.shape.index(max(values.shape))
    spots = []
    for shift in (0, 1):
        where = [jax.random.randint(jax.random.fold_in(stream_key, axis), (), 0, length) for axis, length in enumerate(values.shape)]
        where[longest] = (where[longest] + shift) % values.shape[longest]
        spots.append(tuple(where))
    return values.at[spots[0]].set(low).at[spots[1]].set(top_value)


def block_levels(key, dims, shards, smallest, largest):
    factor_of = 1.0
    for dim, shards_of in shards:
        draws = jax.random.uniform(jax.random.fold_in(jax.random.fold_in(key, 6), dim), (shards_of,), jnp.float32, smallest / len(shards), largest / len(shards))
        factor_of = factor_of * jnp.repeat(jnp.exp(draws), dims[dim] // shards_of).reshape((-1,) + (1,) * (len(dims) - 1 - dim))
    return factor_of


def normal_values(own_key, dims, width, reach, shards=(), dtype=jnp.bfloat16):
    gain = block_levels(own_key, dims, shards, -0.22, 0.18) if shards else 1.0
    entries = jax.random.normal(own_key, dims, jnp.float32) * width * gain
    return jnp.minimum(jnp.maximum(entries, -reach), reach).astype(dtype)


def setup_inputs(seed: int = 0, part: int = 0) -> dict:
    splits = jax.random.split(jax.random.key(seed), 9)
    own_keys = jax.random.split(jax.random.fold_in(splits[8], part), 9)
    return {
        "noisy_image": normal_values(own_keys[0], (2, H, W), 1.0, 6.0, ((1, 8), (2, 2)), jnp.float32),
        "fresh_noise": normal_values(own_keys[1], (2, H, W), 1.0, 6.0, ((1, 8), (2, 2)), jnp.float32),
        "coil_maps": normal_values(own_keys[2], (COILS, 2, H, W), 0.25, 1.5, ((0, 2), (2, 8)), jnp.float32),
        "measured": normal_values(own_keys[3], (2, W, COILS, H), 0.4, 2.4, ((1, 8), (2, 2)), jnp.float32),
        "sampled": place_ends((jax.random.randint(own_keys[4], (W, H), 0, 3) < 1).astype(jnp.int32), jax.random.fold_in(own_keys[4], 1), 0, 1),
        "first_kernel": normal_values(splits[5], (9, CH, 2), (9 * 2) ** -0.5, 1.5),
        "inner_kernels": normal_values(splits[6], (MID_LAYERS, 9, CH, CH), (9 * CH) ** -0.5, 0.25),
        "last_kernel": normal_values(splits[7], (9, 2, CH), (9 * CH) ** -0.5, 0.25),
    }


SCALE_NOW = 0.8
SIGMA_NOW = 0.6
STEP_GAIN = 1.0
SCALE_NEXT = 0.9
DIRECT_GAIN = 0.31622776601683794
NOISE_GAIN = 0.3


def convolve(features, kernel):
    kernel_out = kernel.shape[1]
    kernel_in = kernel.shape[2]
    filters = jnp.transpose(kernel.astype(jnp.float32).reshape(3, 3, kernel_out, kernel_in), (2, 3, 0, 1))
    result = lax.conv_general_dilated(features.astype(jnp.float32)[None], filters, (1, 1), ((1, 1), (1, 1)), dimension_numbers=("NCHW", "OIHW", "NCHW"), precision=lax.Precision.HIGHEST)
    return result[0]


def reference(noisy_image, fresh_noise, coil_maps, measured, sampled, first_kernel, inner_kernels, last_kernel):
    hidden = jax.nn.silu(convolve(noisy_image.astype(jnp.bfloat16), first_kernel)).astype(jnp.bfloat16)
    for layer_index in range(MID_LAYERS):
        hidden = jax.nn.silu(convolve(hidden, inner_kernels[layer_index])).astype(jnp.bfloat16)
    predicted = convolve(hidden, last_kernel)
    clean = (noisy_image - SIGMA_NOW * predicted) / SCALE_NOW
    maps_real = coil_maps[:, 0]
    maps_imag = coil_maps[:, 1]
    coil_real = maps_real * clean[0] - maps_imag * clean[1]
    coil_imag = maps_real * clean[1] + maps_imag * clean[0]
    spectra = jnp.fft.fft2(lax.complex(coil_real, coil_imag), norm="ortho")
    target = lax.complex(jnp.transpose(measured[0], (1, 2, 0)), jnp.transpose(measured[1], (1, 2, 0)))
    keeping = jnp.transpose(sampled).astype(jnp.float32)
    residual = (spectra - target) * keeping
    back = jnp.fft.ifft2(residual, norm="ortho")
    back_real = jnp.real(back)
    back_imag = jnp.imag(back)
    grad_real = jnp.sum(maps_real * back_real + maps_imag * back_imag, axis=0)
    grad_imag = jnp.sum(maps_real * back_imag - maps_imag * back_real, axis=0)
    update = clean - STEP_GAIN * jnp.stack([grad_real, grad_imag])
    return SCALE_NEXT * update + DIRECT_GAIN * predicted + NOISE_GAIN * fresh_noise
```

```python
import math

import jax
import jax.numpy as jnp
import ml_dtypes
import numpy as np
from jax import lax
from jax.experimental import pallas as pl
from jax.experimental.pallas import tpu as pltpu
from jax.sharding import PartitionSpec as P

SCALE_NOW = 0.8
SIGMA_NOW = 0.6
STEP_GAIN = 1.0
SCALE_NEXT = 0.9
DIRECT_GAIN = 0.31622776601683794
NOISE_GAIN = 0.3

NOISY_MAX = 6.0
MAPS_MAX = 1.5
MEASURED_MAX = 2.4

F32 = jnp.float32
BF16 = jnp.bfloat16
LANES = 128
EDGE = 8


def ceil_to(value, step):
    return -(-value // step) * step


def tap_choice(rows, cols):
    choice = np.zeros(rows.shape + (9,), np.float32)
    for index in np.ndindex(rows.shape):
        a, b = rows[index], cols[index]
        if 0 <= a < 3 and 0 <= b < 3:
            choice[index + (3 * a + b,)] = 1.0
    return choice


def pick_taps(choice, kernel):
    flat = lax.dot_general(
        jnp.asarray(choice.reshape(-1, 9), BF16),
        kernel.reshape(9, -1),
        (((1,), (0,)), ((), ())),
        preferred_element_type=F32,
    ).astype(BF16)
    return flat.reshape(choice.shape[:-1] + kernel.shape[1:])


def network_weights(first_kernel, inner_kernel, last_kernel):
    s, d, x, c, r = np.meshgrid(*map(np.arange, (4, 4, 16, 2, 2)), indexing="ij")
    first = pick_taps(tap_choice(x - 5 - 2 * s - r, d - c), first_kernel * jnp.asarray(0.5, BF16))
    first = jnp.transpose(first, (0, 1, 6, 2, 3, 4, 5)).reshape(4, 128, -1)
    places = []
    for cols, rows in (((0, 1), (0, 1)), ((-1, 2), (0, 1)), ((0, 1), (2, -1)), ((-1, 2), (2, -1))):
        places += [(gamma, rho) for gamma in cols for rho in rows]
    gamma = np.array([p[0] for p in places])[:, None, None]
    rho = np.array([p[1] for p in places])[:, None, None]
    c, r = np.arange(2)[None, :, None], np.arange(2)[None, None, :]
    rows, cols = np.broadcast_arrays(rho - r + 1, gamma - c + 1)
    inner = pick_taps(tap_choice(rows, cols), inner_kernel * jnp.asarray(0.5, BF16))
    ch = inner_kernel.shape[1]
    inner = jnp.transpose(inner, (0, 4, 1, 2, 3)).reshape(16 * ch, 4 * ch)
    dr, dc, c, r = np.meshgrid(*map(np.arange, (4, 4, 2, 2)), indexing="ij")
    last = pick_taps(tap_choice(r - dr + 2, c - dc + 2), last_kernel)
    last = jnp.transpose(last, (0, 1, 4, 2, 3, 5)).reshape(32, -1)
    return first, inner, last


def split3(value):
    high = value.astype(BF16)
    rest = value - high.astype(F32)
    middle = rest.astype(BF16)
    return high, middle, (rest - middle.astype(F32)).astype(BF16)


def split2(value):
    high = value.astype(BF16)
    return high, (value - high.astype(F32)).astype(BF16)


def mm(lhs, rhs):
    return lax.dot_general(lhs, rhs, (((1,), (0,)), ((), ())), preferred_element_type=F32)


def mm_nt(lhs, rhs):
    return lax.dot_general(lhs, rhs, (((1,), (1,)), ((), ())), preferred_element_type=F32)


def network_kernel(
    flags, top, center, bottom, side, first, inner, last, pred, clean, tile, q, hid, hid_side, mask, acc
):
    rows, cols = center.shape[1:]
    blocks = rows // 2 + 2
    groups = q.shape[1] // 8 - 1
    used = mask.shape[0]

    for ch in range(2):
        tile[ch, 0:8, :] = top[ch]
        tile[ch, 8 : 8 + rows, :] = center[ch]
        tile[ch, 8 + rows : 16 + rows, :] = bottom[ch]
    w = lax.broadcasted_iota(jnp.int32, (cols, 256), 0)
    k = lax.broadcasted_iota(jnp.int32, (cols, 256), 1)
    e = lax.broadcasted_iota(jnp.int32, (2 * EDGE, 256), 0)
    e = jnp.where(e < EDGE, e - EDGE, e - EDGE + cols)
    ke = lax.broadcasted_iota(jnp.int32, (2 * EDGE, 256), 1)
    for d in range(4):
        sel = jnp.where(w == 2 * k - 3 + d, 1.0, 0.0).astype(BF16)
        sel_side = jnp.where(e == 2 * ke - 3 + d, 1.0, 0.0).astype(BF16)
        for ch in range(2):
            q[2 * d + ch] = mm(tile[ch].astype(BF16), sel) + mm(side[ch].astype(BF16), sel_side)

    ks = lax.broadcasted_iota(jnp.int32, (used, 256), 0)
    drop_low = jnp.where(flags[2] != 0, 0, -1)
    drop_high = jnp.where(flags[3] != 0, cols // 2 + 1, -1)
    mask[...] = jnp.where((ks == drop_low) | (ks == drop_high), 0.0, 1.0)
    acc[...] = jnp.zeros(acc.shape, F32)

    def first_layer(t, carry):
        window = q[:, pl.ds(pl.multiple_of(8 * t, 8), 16), :].reshape(128, 256)
        window = jnp.transpose(window)[:used].astype(BF16)
        for s in range(4):
            half = mm(window, first[s])
            h = (half + half * jnp.tanh(half)) * mask[...]
            hid[4 * t + s] = h.astype(BF16)
            hid_side[4 * t + s, :, 0:128] = pltpu.roll(h[:, 128:256], 1, 0).astype(BF16)
            hid_side[4 * t + s, :, 128:256] = pltpu.roll(h[:, 0:128], used - 1, 0).astype(BF16)
        return carry

    lax.fori_loop(0, groups, first_layer, 0)

    for flag, j in ((0, 0), (1, blocks - 1)):

        @pl.when(flags[flag] != 0)
        def _(j=j):
            hid[j] = jnp.zeros(hid.shape[1:], BF16)
            hid_side[j] = jnp.zeros(hid_side.shape[1:], BF16)

    lane = lax.broadcasted_iota(jnp.int32, (used, 256), 1)
    below = lax.rem(lane, 128) < 64

    def next_layers(j, carry):
        up, down = jnp.maximum(j - 1, 0), j + 1
        half = mm(hid[j], inner[0:256, :]) + mm(hid_side[j], inner[256:512, :])
        half += mm(jnp.where(below, hid[down], hid[up]), inner[512:768, :])
        half += mm(jnp.where(below, hid_side[down], hid_side[up]), inner[768:1024, :])
        h = ((half + half * jnp.tanh(half)) * mask[...]).astype(BF16)
        part = mm_nt(last[...], h)
        gone = ((j == 0) & (flags[0] != 0)) | ((j == blocks - 1) & (flags[1] != 0))
        part = part * jnp.where(gone, 0.0, 1.0)
        where = pl.ds(pl.multiple_of(16 * j, 16), 32)
        for c in range(0, used, 128):
            width = min(128, used - c)
            acc[c // 128, where, 0:width] = acc[c // 128, where, 0:width] + part[:, c : c + width]
        return carry

    lax.fori_loop(0, blocks, next_layers, 0)

    k = lax.broadcasted_iota(jnp.int32, (256, cols), 0)
    w = lax.broadcasted_iota(jnp.int32, (256, cols), 1)
    total = [0.0, 0.0]
    for d in range(4):
        sel = jnp.where(w == 2 * k - 3 + d, 1.0, 0.0).astype(BF16)
        for ch in range(2):
            start = 24 + 2 * d + ch
            lines = jnp.concatenate(
                [acc[c, pl.ds(start, rows, stride=8), :] for c in range(2)], axis=1
            )
            for piece in split3(lines):
                total[ch] += mm(piece, sel)
    for ch in range(2):
        pred[ch] = total[ch]
        clean[ch] = (center[ch] - SIGMA_NOW * total[ch]) / SCALE_NOW


def run_network(noisy, top, bottom, side, flags, weights):
    _, rows, cols = noisy.shape
    blocks = rows // 2 + 2
    groups = -(-blocks // 4)
    used = ceil_to(cols // 2 + 2, 16)
    vmem = pl.BlockSpec(memory_space=pltpu.VMEM)
    shape = jax.ShapeDtypeStruct(noisy.shape, F32)
    return pl.pallas_call(
        network_kernel,
        out_shape=(shape, shape),
        in_specs=[pl.BlockSpec(memory_space=pltpu.SMEM)] + [vmem] * 7,
        out_specs=(vmem, vmem),
        scratch_shapes=[
            pltpu.VMEM((2, rows + 16, cols), F32),
            pltpu.VMEM((8, 8 * groups + 8, 256), F32),
            pltpu.VMEM((4 * groups, used, 256), BF16),
            pltpu.VMEM((4 * groups, used, 256), BF16),
            pltpu.VMEM((used, 256), F32),
            pltpu.VMEM((2, 16 * blocks + 16, 128), F32),
        ],
        name="network",
    )(flags, top, noisy, bottom, side, *weights)


def move(value, axis, pairs):
    return lax.ppermute(value, axis, pairs)


def halo(noisy):
    gz, col = lax.axis_size("gz"), lax.axis_size("col")
    _, rows, cols = noisy.shape
    upper, lower = noisy[:, :EDGE, :], noisy[:, rows - EDGE :, :]
    left, right = noisy[:, :, :EDGE], noisy[:, :, cols - EDGE :]
    down = [(i, i + 1) for i in range(gz - 1)]
    top = move(lower, "gz", down)
    bottom = move(upper, "gz", [(b, a) for a, b in down])

    def both(dr, dc):
        return [
            (r * col + c, (r + dr) * col + c + dc)
            for r in range(gz)
            for c in range(col)
            if 0 <= r + dr < gz and 0 <= c + dc < col
        ]

    def side(dc, edge):
        parts = [
            move(edge[:, rows - EDGE :], ("gz", "col"), both(1, dc)),
            move(edge, "col", [(c, c + dc) for c in range(col) if 0 <= c + dc < col]),
            move(edge[:, :EDGE], ("gz", "col"), both(-1, dc)),
        ]
        return parts

    if col == 2:
        first = lax.axis_index("col") == 0
        edge = jnp.where(first, right, left)
        swap = [(0, 1), (1, 0)]

        def cross(dr):
            return [
                (r * 2 + c, (r + dr) * 2 + 1 - c)
                for r in range(gz)
                for c in range(2)
                if 0 <= r + dr < gz
            ]

        got = jnp.concatenate(
            [
                move(edge[:, rows - EDGE :], ("gz", "col"), cross(1)),
                move(edge, "col", swap),
                move(edge[:, :EDGE], ("gz", "col"), cross(-1)),
            ],
            axis=1,
        )
        zero = jnp.zeros_like(got)
        sides = jnp.concatenate(
            [jnp.where(first, zero, got), jnp.where(first, got, zero)], axis=2
        )
    else:
        sides = jnp.concatenate(
            [
                jnp.concatenate(side(1, right), axis=1),
                jnp.concatenate(side(-1, left), axis=1),
            ],
            axis=2,
        )
    return top, bottom, sides


def edge_flags():
    row, col = lax.axis_index("gz"), lax.axis_index("col")
    last_row, last_col = lax.axis_size("gz") - 1, lax.axis_size("col") - 1
    return jnp.stack([row == 0, row == last_row, col == 0, col == last_col]).astype(jnp.int32)


def halves(matrix):
    high = matrix.astype(ml_dtypes.bfloat16)
    low = (matrix - high.astype(np.float64)).astype(ml_dtypes.bfloat16)
    return np.stack([high, low])


def fourier_parts(length, scale):
    index = np.arange(length)
    angle = 2.0 * np.pi * (np.outer(index, index) % length) / length
    return np.cos(angle) * scale, np.sin(angle) * scale


def turn_table(radix, inner):
    angle = 2.0 * np.pi * np.outer(np.arange(radix), np.arange(inner)) / (radix * inner)
    return np.stack([np.cos(angle), np.sin(angle)]).astype(np.float32)


def small_dft(values, sign):
    n = len(values)
    if n == 1:
        return values
    if n % 2 == 0:
        even = small_dft(values[0::2], sign)
        odd = small_dft(values[1::2], sign)
        low, high = [], []
        for q in range(n // 2):
            re, im = times_unit(odd[q], q, n, sign)
            low.append((even[q][0] + re, even[q][1] + im))
            high.append((even[q][0] - re, even[q][1] - im))
        return low + high
    if n == 3:
        (r0, i0), (r1, i1), (r2, i2) = values
        sr, si = r1 + r2, i1 + i2
        half = math.sqrt(3.0) / 2.0 * sign
        dr, di = half * (r1 - r2), half * (i1 - i2)
        tr, ti = r0 - 0.5 * sr, i0 - 0.5 * si
        return [(r0 + sr, i0 + si), (tr - di, ti + dr), (tr + di, ti - dr)]
    out = []
    for q in range(n):
        terms = [times_unit(v, a * q, n, sign) for a, v in enumerate(values)]
        out.append((sum(t[0] for t in terms), sum(t[1] for t in terms)))
    return out


def times_unit(value, power, n, sign):
    re, im = value
    power %= n
    if power == 0:
        return re, im
    if 4 * power == n:
        return (-im, re) if sign > 0 else (im, -re)
    if 2 * power == n:
        return -re, -im
    if 4 * power == 3 * n:
        return (im, -re) if sign > 0 else (-im, re)
    c = math.cos(2.0 * math.pi * power / n)
    s = sign * math.sin(2.0 * math.pi * power / n)
    return c * re - s * im, c * im + s * re


def turn(value, cos, sin, sign):
    re, im = value
    if sign > 0:
        return re * cos - im * sin, im * cos + re * sin
    return re * cos + im * sin, im * cos - re * sin


def mm3(lhs, rhs, dot):
    return dot(lhs[0], rhs[0]) + (dot(lhs[0], rhs[1]) + dot(lhs[1], rhs[0]))


def columns_forward_kernel(first, mine, other, maps, matrix, table, out):
    radix, inner = table.shape[1:]
    rows, cols = mine.shape[1:]
    groups = out.shape[0]
    per = inner // groups
    lead = first[0] != 0
    image = [
        jnp.concatenate(
            [jnp.where(lead, mine[p], other[p]), jnp.where(lead, other[p], mine[p])], axis=1
        )
        for p in range(2)
    ]
    maps_real, maps_imag = maps[0, 0], maps[0, 1]
    coil = (
        maps_real * image[0] - maps_imag * image[1],
        maps_real * image[1] + maps_imag * image[0],
    )
    parts = [
        tuple(v[:, a * inner : (a + 1) * inner] for v in coil) for a in range(radix)
    ]
    for q, part in enumerate(small_dft(parts, -1)):
        if q:
            part = turn(part, table[0, q : q + 1, :], table[1, q : q + 1, :], -1)
        data = split2(jnp.concatenate(part, axis=1))
        result = mm3((matrix[0], matrix[1]), data, mm_nt)
        for p in range(2):
            for g in range(groups):
                start = p * inner + g * per
                out[g, p, 0, q] = result[start : start + per]


def columns_forward(mine, other, maps, groups):
    coils, _, rows, cols = maps.shape
    inner = 256
    radix = cols // inner
    c, s = fourier_parts(inner, 1.0 / math.sqrt(cols))
    matrix = halves(np.block([[c, s], [-s, c]]))
    table = turn_table(radix, inner)
    first = (lax.axis_index("col") == 0).astype(jnp.int32)[None]
    vmem = pl.BlockSpec(memory_space=pltpu.VMEM)
    per = inner // groups
    return pl.pallas_call(
        columns_forward_kernel,
        out_shape=jax.ShapeDtypeStruct((groups, 2, coils, radix, per, rows), F32),
        grid=(coils,),
        in_specs=[
            pl.BlockSpec(memory_space=pltpu.SMEM),
            vmem,
            vmem,
            pl.BlockSpec((1, 2, rows, cols), lambda i: (i, 0, 0, 0)),
            vmem,
            vmem,
        ],
        out_specs=pl.BlockSpec(
            (groups, 2, 1, radix, per, rows), lambda i: (0, 0, i, 0, 0, 0)
        ),
        name="columns_forward",
    )(first, mine, other, maps, jnp.asarray(matrix), jnp.asarray(table))


def rows_kernel(data, kept, target, forward, inverse, table, out):
    radix = table.shape[1]
    parts = small_dft([(data[a, 0], data[a, 1]) for a in range(radix)], -1)
    back = []
    for q, part in enumerate(parts):
        cos, sin = table[0, q : q + 1, :], table[1, q : q + 1, :]
        if q:
            part = turn(part, cos, sin, -1)
        spectrum = mm3(split2(jnp.concatenate(part, axis=1)), (forward[0], forward[1]), mm)
        keep = kept[q]
        residual = jnp.concatenate(
            [
                keep * (spectrum[:, p * LANES : (p + 1) * LANES] - target[p, q])
                for p in range(2)
            ],
            axis=1,
        )
        lines = mm3(split2(residual), (inverse[0], inverse[1]), mm)
        part = (lines[:, :LANES], lines[:, LANES:])
        if q:
            part = turn(part, cos, sin, 1)
        back.append(part)
    for a, (re, im) in enumerate(small_dft(back, 1)):
        out[a, 0] = re
        out[a, 1] = im


def rows_both_ways(data, kept, target):
    radix, _, count, _ = data.shape
    c, s = fourier_parts(LANES, 1.0 / math.sqrt(radix * LANES))
    forward = halves(np.block([[c, -s], [s, c]]))
    inverse = halves(np.block([[c, s], [-s, c]]))
    table = turn_table(radix, LANES)
    block = 48 if count % 48 == 0 else 8
    vmem = pl.BlockSpec(memory_space=pltpu.VMEM)
    spec = pl.BlockSpec((radix, 2, block, LANES), lambda i: (0, 0, i, 0))
    return pl.pallas_call(
        rows_kernel,
        out_shape=jax.ShapeDtypeStruct(data.shape, F32),
        grid=(count // block,),
        in_specs=[
            spec,
            pl.BlockSpec((radix, block, LANES), lambda i: (0, i, 0)),
            pl.BlockSpec((2, radix, block, LANES), lambda i: (0, 0, i, 0)),
            vmem,
            vmem,
            vmem,
        ],
        out_specs=spec,
        name="rows_both_ways",
    )(data, kept, target, jnp.asarray(forward), jnp.asarray(inverse), jnp.asarray(table))


def columns_inverse_kernel(data, maps, matrix, table, out):
    radix, inner = table.shape[1:]
    groups = data.shape[0]
    rows = out.shape[1]
    parts = []
    for q in range(radix):
        lines = jnp.concatenate(
            [data[g, p, 0, q] for p in range(2) for g in range(groups)], axis=0
        )
        lines = split2(jnp.transpose(lines))
        result = mm3(lines, (matrix[0], matrix[1]), mm)
        part = (result[:, :inner], result[:, inner:])
        if q:
            part = turn(part, table[0, q : q + 1, :], table[1, q : q + 1, :], 1)
        parts.append(part)
    back = small_dft(parts, 1)
    step = pl.program_id(0)
    for a, (re, im) in enumerate(back):
        where = slice(a * inner, (a + 1) * inner)
        maps_real, maps_imag = maps[0, 0, :, where], maps[0, 1, :, where]
        sums = (
            maps_real * re + maps_imag * im,
            maps_real * im - maps_imag * re,
        )
        for p in range(2):

            @pl.when(step == 0)
            def _(p=p, sums=sums, where=where):
                out[p, :, where] = sums[p]

            @pl.when(step != 0)
            def _(p=p, sums=sums, where=where):
                out[p, :, where] = out[p, :, where] + sums[p]


def columns_inverse(data, maps):
    groups, _, coils, radix, per, rows = data.shape
    cols = maps.shape[3]
    inner = cols // radix
    c, s = fourier_parts(inner, 1.0 / math.sqrt(cols))
    matrix = halves(np.block([[c, s], [-s, c]]))
    table = turn_table(radix, inner)
    vmem = pl.BlockSpec(memory_space=pltpu.VMEM)
    return pl.pallas_call(
        columns_inverse_kernel,
        out_shape=jax.ShapeDtypeStruct((2, rows, cols), F32),
        grid=(coils,),
        in_specs=[
            pl.BlockSpec((groups, 2, 1, radix, per, rows), lambda i: (0, 0, i, 0, 0, 0)),
            pl.BlockSpec((1, 2, rows, cols), lambda i: (i, 0, 0, 0)),
            vmem,
            vmem,
        ],
        out_specs=pl.BlockSpec((2, rows, cols), lambda i: (0, 0, 0)),
        name="columns_inverse",
    )(data, maps, jnp.asarray(matrix), jnp.asarray(table))


def send_bounds(first_kernel, inner_kernel, last_kernel, cols, height):
    def gain(kernel):
        return jnp.max(jnp.sum(jnp.abs(kernel.astype(F32)), axis=(0, 2))) * 1.02

    predicted = NOISY_MAX * gain(first_kernel) * gain(inner_kernel) * gain(last_kernel)
    clean = (NOISY_MAX + SIGMA_NOW * predicted) / SCALE_NOW
    spectra = 1.1 * math.sqrt(cols) * 2.0 * MAPS_MAX * clean
    lines = 1.1 * math.sqrt(height) * (spectra + math.sqrt(2.0) * MEASURED_MAX)
    return spectra, lines


def exchange(value, bound):
    half = (value * (60000.0 / bound)).astype(jnp.float16)
    half = lax.all_to_all(half, "gz", split_axis=0, concat_axis=0, tiled=True)
    return half.astype(F32) * (bound / 60000.0)


def local(
    noisy_image, fresh_noise, coil_maps, measured, sampled, first_kernel, inner_kernels, last_kernel
):
    groups = lax.axis_size("gz")
    coils, _, rows, cols = coil_maps.shape
    height = measured.shape[3]
    radix, inner = cols // 256, 256
    per = inner // groups
    row_radix = height // LANES

    weights = network_weights(first_kernel, inner_kernels[0], last_kernel)
    top, bottom, side = halo(noisy_image)
    predicted, clean = run_network(noisy_image, top, bottom, side, edge_flags(), weights)
    other = lax.ppermute(clean, "col", [(0, 1), (1, 0)])

    spectra_bound, lines_bound = send_bounds(
        first_kernel, inner_kernels[0], last_kernel, cols, height
    )
    spectra = columns_forward(clean, other, coil_maps, groups)
    spectra = spectra.reshape(groups, 2, coils * radix * per, rows)
    arrived = exchange(spectra, spectra_bound)
    if rows != LANES:
        arrived = jnp.transpose(arrived, (1, 2, 0, 3)).reshape(2, -1, row_radix, LANES)
        arrived = jnp.transpose(arrived, (2, 0, 1, 3))
    target = measured.reshape(2, per, radix, coils, LANES, row_radix)
    target = jnp.transpose(target, (0, 5, 3, 2, 1, 4)).reshape(2, row_radix, -1, LANES)
    kept = sampled.reshape(per, radix, LANES, row_radix).astype(F32)
    kept = jnp.transpose(kept, (3, 1, 0, 2))[:, None]
    kept = jnp.broadcast_to(kept, (row_radix, coils, radix, per, LANES))
    kept = kept.reshape(row_radix, -1, LANES)
    lines = rows_both_ways(arrived, kept, target)
    if rows != LANES:
        lines = jnp.transpose(lines, (1, 2, 0, 3)).reshape(2, -1, groups, rows)
        lines = jnp.transpose(lines, (2, 0, 1, 3))
    lines = exchange(lines, lines_bound)
    lines = lines.reshape(groups, 2, coils, radix, per, rows)
    gradient = columns_inverse(lines, coil_maps)

    first = lax.axis_index("col") == 0
    width = noisy_image.shape[2]
    own = jnp.where(first, gradient[:, :, :width], gradient[:, :, width:])
    away = jnp.where(first, gradient[:, :, width:], gradient[:, :, :width])
    own = own + lax.ppermute(away, "col", [(0, 1), (1, 0)])
    update = clean - STEP_GAIN * own
    return SCALE_NEXT * update + DIRECT_GAIN * predicted + NOISE_GAIN * fresh_noise


def solution(mesh):
    in_specs = (
        P("grp", "gz", "col"),
        P("grp", "gz", "col"),
        P("col", "grp", "gz", None),
        P("grp", "gz", "col", None),
        P("gz", "grp"),
        P(),
        P(),
        P(),
    )
    out_specs = P("grp", "gz", "col")
    return jax.shard_map(local, mesh=mesh, in_specs=in_specs, out_specs=out_specs, check_vma=False)
```

```python
import math
from functools import partial

import jax
import jax.numpy as jnp
import ml_dtypes
import numpy as np
from jax import lax
from jax.experimental import pallas as pl
from jax.experimental.pallas import tpu as pltpu
from jax.sharding import PartitionSpec as P

SCALE_NOW = 0.8
SIGMA_NOW = 0.6
STEP_GAIN = 1.0
SCALE_NEXT = 0.9
DIRECT_GAIN = 0.31622776601683794
NOISE_GAIN = 0.3

NOISY_MAX = 6.0
MAPS_MAX = 1.5
MEASURED_MAX = 2.4

F32 = jnp.float32
BF16 = jnp.bfloat16
LANES = 128
EDGE = 8
INNER = 256


def ceil_to(value, step):
    return -(-value // step) * step


def tap_choice(rows, cols):
    choice = np.zeros(rows.shape + (9,), np.float32)
    for index in np.ndindex(rows.shape):
        a, b = rows[index], cols[index]
        if 0 <= a < 3 and 0 <= b < 3:
            choice[index + (3 * a + b,)] = 1.0
    return choice


def tap_choices():
    pair = np.eye(2, dtype=np.float32)
    first, last = [], []
    for c, r in np.ndindex(2, 2):
        s, d, x = np.meshgrid(*map(np.arange, (4, 4, 16)), indexing="ij")
        chosen = tap_choice(x - 5 - 2 * s - r, d - c)
        first.append(np.einsum("sdxt,hk->shdxtk", chosen, pair).reshape(512, 18))
        dr, dc = np.meshgrid(np.arange(4), np.arange(4), indexing="ij")
        chosen = tap_choice(r - dr + 2, c - dc + 2)
        last.append(np.einsum("yxt,hk->yxhtk", chosen, pair).reshape(32, 18))
    middle = []
    for cols, rows in (((0, 1), (0, 1)), ((-1, 2), (0, 1)), ((0, 1), (2, -1)), ((-1, 2), (2, -1))):
        for gamma in cols:
            for rho in rows:
                taps = []
                for c, r in np.ndindex(2, 2):
                    a, b = rho - r + 1, gamma - c + 1
                    taps.append(3 * a + b if 0 <= a < 3 and 0 <= b < 3 else None)
                middle.append(taps)
    return np.stack(first), middle, np.stack(last)


def weights_kernel(cols, height, k1, k2, k3, choice1, choice3, first, inner, last, bounds):
    _, middle, _ = tap_choices()
    ch = k1.shape[1]
    parts = [mm(choice1[i], k1[...]) for i in range(4)]
    first[...] = (0.5 * jnp.concatenate(parts, axis=1)).astype(BF16).reshape(first.shape)
    turned = [(0.5 * jnp.transpose(k2[t].astype(F32))).astype(BF16) for t in range(9)]
    zero = jnp.zeros((ch, ch), BF16)
    for p, taps in enumerate(middle):
        row = [zero if t is None else turned[t] for t in taps]
        inner[p * ch : (p + 1) * ch, :] = jnp.concatenate(row, axis=1)
    parts = [mm(choice3[i], k3[...]) for i in range(4)]
    last[...] = jnp.concatenate(parts, axis=1).astype(BF16)

    def top(value, axes):
        for axis in axes:
            value = jnp.max(value, axis=axis, keepdims=True)
        return value

    gain1 = top(jnp.sum(jnp.abs(k1[...].astype(F32)), axis=0, keepdims=True), (1,))
    gain2 = sum(jnp.abs(k2[t].astype(F32)) for t in range(9))
    gain2 = top(jnp.sum(gain2, axis=1, keepdims=True), (0,))
    gain3 = jnp.sum(jnp.abs(k3[...].astype(F32)), axis=1, keepdims=True)
    odd = lax.rem(lax.broadcasted_iota(jnp.int32, gain3.shape, 0), 2) == 1
    gain3 = jnp.maximum(
        jnp.sum(jnp.where(odd, gain3, 0.0), axis=0, keepdims=True),
        jnp.sum(jnp.where(odd, 0.0, gain3), axis=0, keepdims=True),
    )
    predicted = 1.1 * NOISY_MAX * gain1 * gain2 * gain3
    clean = (NOISY_MAX + SIGMA_NOW * predicted) / SCALE_NOW
    spectra = 1.1 * math.sqrt(cols) * 2.0 * MAPS_MAX * clean
    lines = 1.1 * math.sqrt(height) * (spectra + math.sqrt(2.0) * MEASURED_MAX)
    bounds[...] = jnp.concatenate(
        [jnp.broadcast_to(spectra, (4, LANES)), jnp.broadcast_to(lines, (4, LANES))], axis=0
    )


def network_weights(first_kernel, inner_kernel, last_kernel, cols, height):
    ch = inner_kernel.shape[1]
    choice1, _, choice3 = tap_choices()
    k1 = jnp.transpose(first_kernel, (0, 2, 1)).reshape(18, ch)
    shapes = ((4, 128, 4 * ch), (16 * ch, 4 * ch), (32, 4 * ch))
    first, inner, last, bounds = pl.pallas_call(
        partial(weights_kernel, cols, height),
        out_shape=[jax.ShapeDtypeStruct(d, BF16) for d in shapes]
        + [jax.ShapeDtypeStruct((8, LANES), F32)],
        cost_estimate=pl.CostEstimate(flops=10**7, bytes_accessed=10**6, transcendentals=0),
        name="weights",
    )(
        k1,
        inner_kernel,
        last_kernel.reshape(18, ch),
        jnp.asarray(choice1, BF16),
        jnp.asarray(choice3, BF16),
    )
    return (first, inner, last), bounds[0, 0], bounds[4, 0]


def split3(value):
    high = value.astype(BF16)
    rest = value - high.astype(F32)
    middle = rest.astype(BF16)
    return high, middle, (rest - middle.astype(F32)).astype(BF16)


def split2(value):
    high = value.astype(BF16)
    return high, (value - high.astype(F32)).astype(BF16)


def mm(lhs, rhs):
    return lax.dot_general(lhs, rhs, (((1,), (0,)), ((), ())), preferred_element_type=F32)


def mm_nt(lhs, rhs):
    return lax.dot_general(lhs, rhs, (((1,), (1,)), ((), ())), preferred_element_type=F32)


def network_kernel(
    flags, top, center, bottom, side, first, inner, last, pred, clean, tile, q, hid, hid_side, mask, acc
):
    rows, cols = center.shape[1:]
    blocks = rows // 2 + 2
    groups = q.shape[1] // 8 - 1
    used = mask.shape[0]

    for ch in range(2):
        tile[ch, 0:8, :] = top[ch]
        tile[ch, 8 : 8 + rows, :] = center[ch]
        tile[ch, 8 + rows : 16 + rows, :] = bottom[ch]
    w = lax.broadcasted_iota(jnp.int32, (cols, 256), 0)
    k = lax.broadcasted_iota(jnp.int32, (cols, 256), 1)
    e = lax.broadcasted_iota(jnp.int32, (2 * EDGE, 256), 0)
    e = jnp.where(e < EDGE, e - EDGE, e - EDGE + cols)
    ke = lax.broadcasted_iota(jnp.int32, (2 * EDGE, 256), 1)
    for d in range(4):
        sel = jnp.where(w == 2 * k - 3 + d, 1.0, 0.0).astype(BF16)
        sel_side = jnp.where(e == 2 * ke - 3 + d, 1.0, 0.0).astype(BF16)
        for ch in range(2):
            q[4 * ch + d] = mm(tile[ch].astype(BF16), sel) + mm(side[ch].astype(BF16), sel_side)

    ks = lax.broadcasted_iota(jnp.int32, (used, 256), 0)
    drop_low = jnp.where(flags[2] != 0, 0, -1)
    drop_high = jnp.where(flags[3] != 0, cols // 2 + 1, -1)
    mask[...] = jnp.where((ks == drop_low) | (ks == drop_high), 0.0, 1.0)
    acc[...] = jnp.zeros(acc.shape, F32)

    def first_layer(t, carry):
        window = q[:, pl.ds(pl.multiple_of(8 * t, 8), 16), :].reshape(128, 256)
        window = jnp.transpose(window)[:used].astype(BF16)
        for s in range(4):
            half = mm(window, first[s])
            h = (half + half * jnp.tanh(half)) * mask[...]
            hid[4 * t + s] = h.astype(BF16)
            hid_side[4 * t + s, :, 0:128] = pltpu.roll(h[:, 128:256], 1, 0).astype(BF16)
            hid_side[4 * t + s, :, 128:256] = pltpu.roll(h[:, 0:128], used - 1, 0).astype(BF16)
        return carry

    lax.fori_loop(0, groups, first_layer, 0)

    for flag, j in ((0, 0), (1, blocks - 1)):

        @pl.when(flags[flag] != 0)
        def _(j=j):
            hid[j] = jnp.zeros(hid.shape[1:], BF16)
            hid_side[j] = jnp.zeros(hid_side.shape[1:], BF16)

    lane = lax.broadcasted_iota(jnp.int32, (used, 256), 1)
    below = lax.rem(lane, 128) < 64

    def next_layers(j, carry):
        up, down = jnp.maximum(j - 1, 0), j + 1
        half = mm(hid[j], inner[0:256, :]) + mm(hid_side[j], inner[256:512, :])
        half += mm(jnp.where(below, hid[down], hid[up]), inner[512:768, :])
        half += mm(jnp.where(below, hid_side[down], hid_side[up]), inner[768:1024, :])
        h = ((half + half * jnp.tanh(half)) * mask[...]).astype(BF16)
        part = mm_nt(last[...], h)
        gone = ((j == 0) & (flags[0] != 0)) | ((j == blocks - 1) & (flags[1] != 0))
        part = part * jnp.where(gone, 0.0, 1.0)
        where = pl.ds(pl.multiple_of(16 * j, 16), 32)
        for c in range(0, used, 128):
            width = min(128, used - c)
            acc[c // 128, where, 0:width] = acc[c // 128, where, 0:width] + part[:, c : c + width]
        return carry

    lax.fori_loop(0, blocks, next_layers, 0)

    k = lax.broadcasted_iota(jnp.int32, (256, cols), 0)
    w = lax.broadcasted_iota(jnp.int32, (256, cols), 1)
    total = [0.0, 0.0]
    for d in range(4):
        sel = jnp.where(w == 2 * k - 3 + d, 1.0, 0.0).astype(BF16)
        for ch in range(2):
            start = 24 + 2 * d + ch
            lines = jnp.concatenate(
                [acc[c, pl.ds(start, rows, stride=8), :] for c in range(2)], axis=1
            )
            for piece in split3(lines):
                total[ch] += mm(piece, sel)
    for ch in range(2):
        pred[ch] = total[ch]
        clean[ch] = (center[ch] - SIGMA_NOW * total[ch]) / SCALE_NOW


def run_network(noisy, top, bottom, side, flags, weights):
    _, rows, cols = noisy.shape
    blocks = rows // 2 + 2
    groups = -(-blocks // 4)
    used = ceil_to(cols // 2 + 2, 16)
    vmem = pl.BlockSpec(memory_space=pltpu.VMEM)
    shape = jax.ShapeDtypeStruct(noisy.shape, F32)
    return pl.pallas_call(
        network_kernel,
        out_shape=(shape, shape),
        in_specs=[pl.BlockSpec(memory_space=pltpu.SMEM)] + [vmem] * 7,
        out_specs=(vmem, vmem),
        scratch_shapes=[
            pltpu.VMEM((2, rows + 16, cols), F32),
            pltpu.VMEM((8, 8 * groups + 8, 256), F32),
            pltpu.VMEM((4 * groups, used, 256), BF16),
            pltpu.VMEM((4 * groups, used, 256), BF16),
            pltpu.VMEM((used, 256), F32),
            pltpu.VMEM((2, 16 * blocks + 16, 128), F32),
        ],
        name="network",
    )(flags, top, noisy, bottom, side, *weights)


def move(value, axis, pairs):
    return lax.ppermute(value, axis, pairs)


def halo(noisy):
    gz, col = lax.axis_size("gz"), lax.axis_size("col")
    _, rows, cols = noisy.shape
    upper, lower = noisy[:, :EDGE, :], noisy[:, rows - EDGE :, :]
    left, right = noisy[:, :, :EDGE], noisy[:, :, cols - EDGE :]
    down = [(i, i + 1) for i in range(gz - 1)]
    top = move(lower, "gz", down)
    bottom = move(upper, "gz", [(b, a) for a, b in down])

    def both(dr, dc):
        return [
            (r * col + c, (r + dr) * col + c + dc)
            for r in range(gz)
            for c in range(col)
            if 0 <= r + dr < gz and 0 <= c + dc < col
        ]

    def side(dc, edge):
        parts = [
            move(edge[:, rows - EDGE :], ("gz", "col"), both(1, dc)),
            move(edge, "col", [(c, c + dc) for c in range(col) if 0 <= c + dc < col]),
            move(edge[:, :EDGE], ("gz", "col"), both(-1, dc)),
        ]
        return parts

    if col == 2:
        first = lax.axis_index("col") == 0
        edge = jnp.where(first, right, left)
        swap = [(0, 1), (1, 0)]

        def cross(dr):
            return [
                (r * 2 + c, (r + dr) * 2 + 1 - c)
                for r in range(gz)
                for c in range(2)
                if 0 <= r + dr < gz
            ]

        got = jnp.concatenate(
            [
                move(edge[:, rows - EDGE :], ("gz", "col"), cross(1)),
                move(edge, "col", swap),
                move(edge[:, :EDGE], ("gz", "col"), cross(-1)),
            ],
            axis=1,
        )
        zero = jnp.zeros_like(got)
        sides = jnp.concatenate(
            [jnp.where(first, zero, got), jnp.where(first, got, zero)], axis=2
        )
    else:
        sides = jnp.concatenate(
            [
                jnp.concatenate(side(1, right), axis=1),
                jnp.concatenate(side(-1, left), axis=1),
            ],
            axis=2,
        )
    return top, bottom, sides


def edge_flags():
    row, col = lax.axis_index("gz"), lax.axis_index("col")
    last_row, last_col = lax.axis_size("gz") - 1, lax.axis_size("col") - 1
    return jnp.stack([row == 0, row == last_row, col == 0, col == last_col]).astype(jnp.int32)


def halves(matrix):
    high = matrix.astype(ml_dtypes.bfloat16)
    low = (matrix - high.astype(np.float64)).astype(ml_dtypes.bfloat16)
    return np.stack([high, low])


def fourier_parts(length, scale):
    index = np.arange(length)
    angle = 2.0 * np.pi * (np.outer(index, index) % length) / length
    return np.cos(angle) * scale, np.sin(angle) * scale


def turn_table(radix, inner):
    angle = 2.0 * np.pi * np.outer(np.arange(radix), np.arange(inner)) / (radix * inner)
    return np.stack([np.cos(angle), np.sin(angle)]).astype(np.float32)


def small_dft(values, sign):
    n = len(values)
    if n == 1:
        return values
    if n % 2 == 0:
        even = small_dft(values[0::2], sign)
        odd = small_dft(values[1::2], sign)
        low, high = [], []
        for q in range(n // 2):
            re, im = times_unit(odd[q], q, n, sign)
            low.append((even[q][0] + re, even[q][1] + im))
            high.append((even[q][0] - re, even[q][1] - im))
        return low + high
    if n == 3:
        (r0, i0), (r1, i1), (r2, i2) = values
        sr, si = r1 + r2, i1 + i2
        half = math.sqrt(3.0) / 2.0 * sign
        dr, di = half * (r1 - r2), half * (i1 - i2)
        tr, ti = r0 - 0.5 * sr, i0 - 0.5 * si
        return [(r0 + sr, i0 + si), (tr - di, ti + dr), (tr + di, ti - dr)]
    out = []
    for q in range(n):
        terms = [times_unit(v, a * q, n, sign) for a, v in enumerate(values)]
        out.append((sum(t[0] for t in terms), sum(t[1] for t in terms)))
    return out


def times_unit(value, power, n, sign):
    re, im = value
    power %= n
    if power == 0:
        return re, im
    if 4 * power == n:
        return (-im, re) if sign > 0 else (im, -re)
    if 2 * power == n:
        return -re, -im
    if 4 * power == 3 * n:
        return (im, -re) if sign > 0 else (-im, re)
    c = math.cos(2.0 * math.pi * power / n)
    s = sign * math.sin(2.0 * math.pi * power / n)
    return c * re - s * im, c * im + s * re


def turn(value, cos, sin, sign):
    re, im = value
    if sign > 0:
        return re * cos - im * sin, im * cos + re * sin
    return re * cos + im * sin, im * cos - re * sin


def mm3(lhs, rhs, dot):
    return dot(lhs[0], rhs[0]) + (dot(lhs[0], rhs[1]) + dot(lhs[1], rhs[0]))


def columns_forward_kernel(first, mine, other, maps, matrix, table, out):
    radix, inner = table.shape[1:]
    rows, cols = mine.shape[1:]
    groups = out.shape[0]
    per = inner // groups
    lead = first[0] != 0
    image = [
        jnp.concatenate(
            [jnp.where(lead, mine[p], other[p]), jnp.where(lead, other[p], mine[p])], axis=1
        )
        for p in range(2)
    ]
    maps_real, maps_imag = maps[0, 0], maps[0, 1]
    coil = (
        maps_real * image[0] - maps_imag * image[1],
        maps_real * image[1] + maps_imag * image[0],
    )
    parts = [
        tuple(v[:, a * inner : (a + 1) * inner] for v in coil) for a in range(radix)
    ]
    for q, part in enumerate(small_dft(parts, -1)):
        if q:
            part = turn(part, table[0, q : q + 1, :], table[1, q : q + 1, :], -1)
        data = split2(jnp.concatenate(part, axis=1))
        result = mm3((matrix[0], matrix[1]), data, mm_nt)
        for p in range(2):
            for g in range(groups):
                start = p * inner + g * per
                out[g, p, 0, q] = result[start : start + per]


def columns_forward(mine, other, maps, groups):
    coils, _, rows, cols = maps.shape
    inner = 256
    radix = cols // inner
    c, s = fourier_parts(inner, 1.0 / math.sqrt(cols))
    matrix = halves(np.block([[c, s], [-s, c]]))
    table = turn_table(radix, inner)
    first = (lax.axis_index("col") == 0).astype(jnp.int32)[None]
    vmem = pl.BlockSpec(memory_space=pltpu.VMEM)
    per = inner // groups
    return pl.pallas_call(
        columns_forward_kernel,
        out_shape=jax.ShapeDtypeStruct((groups, 2, coils, radix, per, rows), F32),
        grid=(coils,),
        in_specs=[
            pl.BlockSpec(memory_space=pltpu.SMEM),
            vmem,
            vmem,
            pl.BlockSpec((1, 2, rows, cols), lambda i: (i, 0, 0, 0)),
            vmem,
            vmem,
        ],
        out_specs=pl.BlockSpec(
            (groups, 2, 1, radix, per, rows), lambda i: (0, 0, i, 0, 0, 0)
        ),
        name="columns_forward",
    )(first, mine, other, maps, jnp.asarray(matrix), jnp.asarray(table))


def rows_kernel(data, kept, target, forward, inverse, table, out):
    radix = table.shape[1]
    parts = small_dft([(data[a, 0], data[a, 1]) for a in range(radix)], -1)
    back = []
    for q, part in enumerate(parts):
        cos, sin = table[0, q : q + 1, :], table[1, q : q + 1, :]
        if q:
            part = turn(part, cos, sin, -1)
        spectrum = mm3(split2(jnp.concatenate(part, axis=1)), (forward[0], forward[1]), mm)
        keep = kept[q]
        residual = jnp.concatenate(
            [
                keep * (spectrum[:, p * LANES : (p + 1) * LANES] - target[p, q])
                for p in range(2)
            ],
            axis=1,
        )
        lines = mm3(split2(residual), (inverse[0], inverse[1]), mm)
        part = (lines[:, :LANES], lines[:, LANES:])
        if q:
            part = turn(part, cos, sin, 1)
        back.append(part)
    for a, (re, im) in enumerate(small_dft(back, 1)):
        out[a, 0] = re
        out[a, 1] = im


def rows_both_ways(data, kept, target, first_line):
    radix, _, count, _ = data.shape
    pencil = kept.shape[1]
    c, s = fourier_parts(LANES, 1.0 / math.sqrt(radix * LANES))
    forward = halves(np.block([[c, -s], [s, c]]))
    inverse = halves(np.block([[c, s], [-s, c]]))
    table = turn_table(radix, LANES)
    block = max(b for b in range(8, 56, 8) if pencil % b == 0)
    offset, repeat = first_line // block, pencil // block
    vmem = pl.BlockSpec(memory_space=pltpu.VMEM)
    spec = pl.BlockSpec((radix, 2, block, LANES), lambda i: (0, 0, i, 0))
    return pl.pallas_call(
        rows_kernel,
        out_shape=jax.ShapeDtypeStruct(data.shape, F32),
        grid=(count // block,),
        in_specs=[
            spec,
            pl.BlockSpec((radix, block, LANES), lambda i: (0, lax.rem(i + offset, repeat), 0)),
            pl.BlockSpec((2, radix, block, LANES), lambda i: (0, 0, i + offset, 0)),
            vmem,
            vmem,
            vmem,
        ],
        out_specs=spec,
        name="rows_both_ways",
    )(data, kept, target, jnp.asarray(forward), jnp.asarray(inverse), jnp.asarray(table))


def columns_inverse_kernel(data, maps, matrix, table, out):
    radix, inner = table.shape[1:]
    groups = data.shape[0]
    rows = out.shape[1]
    parts = []
    for q in range(radix):
        lines = jnp.concatenate(
            [data[g, p, 0, q] for p in range(2) for g in range(groups)], axis=0
        )
        lines = split2(jnp.transpose(lines))
        result = mm3(lines, (matrix[0], matrix[1]), mm)
        part = (result[:, :inner], result[:, inner:])
        if q:
            part = turn(part, table[0, q : q + 1, :], table[1, q : q + 1, :], 1)
        parts.append(part)
    back = small_dft(parts, 1)
    step = pl.program_id(0)
    for a, (re, im) in enumerate(back):
        where = slice(a * inner, (a + 1) * inner)
        maps_real, maps_imag = maps[0, 0, :, where], maps[0, 1, :, where]
        sums = (
            maps_real * re + maps_imag * im,
            maps_real * im - maps_imag * re,
        )
        for p in range(2):

            @pl.when(step == 0)
            def _(p=p, sums=sums, where=where):
                out[p, :, where] = sums[p]

            @pl.when(step != 0)
            def _(p=p, sums=sums, where=where):
                out[p, :, where] = out[p, :, where] + sums[p]


def columns_inverse(data, maps):
    groups, _, coils, radix, per, rows = data.shape
    cols = maps.shape[3]
    inner = cols // radix
    c, s = fourier_parts(inner, 1.0 / math.sqrt(cols))
    matrix = halves(np.block([[c, s], [-s, c]]))
    table = turn_table(radix, inner)
    vmem = pl.BlockSpec(memory_space=pltpu.VMEM)
    return pl.pallas_call(
        columns_inverse_kernel,
        out_shape=jax.ShapeDtypeStruct((2, rows, cols), F32),
        grid=(coils,),
        in_specs=[
            pl.BlockSpec((groups, 2, 1, radix, per, rows), lambda i: (0, 0, i, 0, 0, 0)),
            pl.BlockSpec((1, 2, rows, cols), lambda i: (i, 0, 0, 0)),
            vmem,
            vmem,
        ],
        out_specs=pl.BlockSpec((2, rows, cols), lambda i: (0, 0, 0)),
        name="columns_inverse",
    )(data, maps, jnp.asarray(matrix), jnp.asarray(table))


def target_kernel(radix3, *refs):
    tiles = (len(refs) - 4) // 2
    measured, sampled = refs[:tiles], refs[tiles : 2 * tiles]
    target, kept, lines, order = refs[2 * tiles :]
    radix, pencil, _ = kept.shape
    count, height = lines.shape
    coils = count // pencil
    per = pencil // radix3

    @pl.when(pl.program_id(0) == 0)
    def _():
        source = lax.broadcasted_iota(jnp.int32, (height, LANES), 0)
        place = lax.broadcasted_iota(jnp.int32, (height, LANES), 1)
        for q in range(radix):
            order[:, q * LANES : (q + 1) * LANES] = jnp.where(
                source == radix * place + q, 1.0, 0.0
            ).astype(BF16)
        for t in range(tiles):
            for q in range(radix3):
                lines[q * per : (q + 1) * per, t * LANES : (t + 1) * LANES] = sampled[t][
                    pl.ds(q, per, stride=radix3), :
                ].astype(F32)
        picked = mm(lines[0:pencil, :].astype(BF16), order[...])
        for q in range(radix):
            kept[q] = picked[:, q * LANES : (q + 1) * LANES]

    for t in range(tiles):
        for c in range(coils):
            for q in range(radix3):
                start = c * pencil + q * per
                lines[start : start + per, t * LANES : (t + 1) * LANES] = measured[t][
                    0, pl.ds(q * coils + c, per, stride=radix3 * coils), :
                ]
    high, low = split2(lines[...])
    for q in range(0, radix, 2):
        width = min(2, radix - q) * LANES
        part = order[:, q * LANES : q * LANES + width]
        picked = mm(high, part) + mm(low, part)
        for k in range(0, width, LANES):
            target[0, q + k // LANES] = picked[:, k : k + LANES]


def prepare_target(measured, sampled, radix3):
    _, pencil, coils, height = measured.shape
    radix = height // LANES
    count = pencil * coils
    measured = measured.reshape(2, count, height)
    return pl.pallas_call(
        partial(target_kernel, radix3),
        out_shape=(
            jax.ShapeDtypeStruct((2, radix, count, LANES), F32),
            jax.ShapeDtypeStruct((radix, pencil, LANES), F32),
        ),
        grid=(2,),
        in_specs=[
            pl.BlockSpec((1, count, LANES), lambda i, t=t: (i, 0, t)) for t in range(radix)
        ]
        + [pl.BlockSpec((pencil, LANES), lambda i, t=t: (0, t)) for t in range(radix)],
        out_specs=(
            pl.BlockSpec((1, radix, count, LANES), lambda i: (i, 0, 0, 0)),
            pl.BlockSpec((radix, pencil, LANES), lambda i: (0, 0, 0)),
        ),
        scratch_shapes=[pltpu.VMEM((count, height), F32), pltpu.VMEM((height, height), BF16)],
        cost_estimate=pl.CostEstimate(
            flops=8 * count * height * height, bytes_accessed=16 * count * height, transcendentals=0
        ),
        name="target",
    )(*[measured] * radix, *[sampled] * radix)


def exchange(value, bound):
    half = (value * (60000.0 / bound)).astype(jnp.float16)
    half = lax.all_to_all(half, "gz", split_axis=0, concat_axis=0, tiled=True)
    return half.astype(F32) * (bound / 60000.0)


def local(
    noisy_image, fresh_noise, coil_maps, measured, sampled, first_kernel, inner_kernels, last_kernel
):
    groups = lax.axis_size("gz")
    coils, _, rows, cols = coil_maps.shape
    height = measured.shape[3]
    radix, inner = cols // INNER, INNER
    per = inner // groups
    row_radix = height // LANES

    weights, spectra_bound, lines_bound = network_weights(
        first_kernel, inner_kernels[0], last_kernel, cols, height
    )
    top, bottom, side = halo(noisy_image)
    predicted, clean = run_network(noisy_image, top, bottom, side, edge_flags(), weights)
    other = lax.ppermute(clean, "col", [(0, 1), (1, 0)])

    spectra = columns_forward(clean, other, coil_maps, groups)
    spectra = spectra.reshape(groups, 2, coils * radix * per, rows)
    arrived = exchange(spectra, spectra_bound)
    if rows != LANES:
        arrived = jnp.transpose(arrived, (1, 2, 0, 3)).reshape(2, -1, row_radix, LANES)
        arrived = jnp.transpose(arrived, (2, 0, 1, 3))
    target, kept = prepare_target(measured, sampled, radix)
    lines = rows_both_ways(arrived, kept, target, 0)
    if rows != LANES:
        lines = jnp.transpose(lines, (1, 2, 0, 3)).reshape(2, -1, groups, rows)
        lines = jnp.transpose(lines, (2, 0, 1, 3))
    lines = exchange(lines, lines_bound)
    lines = lines.reshape(groups, 2, coils, radix, per, rows)
    gradient = columns_inverse(lines, coil_maps)

    first = lax.axis_index("col") == 0
    width = noisy_image.shape[2]
    own = jnp.where(first, gradient[:, :, :width], gradient[:, :, width:])
    away = jnp.where(first, gradient[:, :, width:], gradient[:, :, :width])
    own = own + lax.ppermute(away, "col", [(0, 1), (1, 0)])
    update = clean - STEP_GAIN * own
    return SCALE_NEXT * update + DIRECT_GAIN * predicted + NOISE_GAIN * fresh_noise


def solution(mesh):
    in_specs = (
        P("grp", "gz", "col"),
        P("grp", "gz", "col"),
        P("col", "grp", "gz", None),
        P("grp", "gz", "col", None),
        P("gz", "grp"),
        P(),
        P(),
        P(),
    )
    out_specs = P("grp", "gz", "col")
    return jax.shard_map(local, mesh=mesh, in_specs=in_specs, out_specs=out_specs, check_vma=False)
```

```python
import math
from functools import partial

import jax
import jax.numpy as jnp
import ml_dtypes
import numpy as np
from jax import lax
from jax.experimental import pallas as pl
from jax.experimental.pallas import tpu as pltpu
from jax.sharding import PartitionSpec as P

SCALE_NOW = 0.8
SIGMA_NOW = 0.6
STEP_GAIN = 1.0
SCALE_NEXT = 0.9
DIRECT_GAIN = 0.31622776601683794
NOISE_GAIN = 0.3

NOISY_MAX = 6.0
MAPS_MAX = 1.5
MEASURED_MAX = 2.4

F32 = jnp.float32
BF16 = jnp.bfloat16
LANES = 128
EDGE = 8
INNER = 256


def ceil_to(value, step):
    return -(-value // step) * step


def tap_choice(rows, cols):
    choice = np.zeros(rows.shape + (9,), np.float32)
    for index in np.ndindex(rows.shape):
        a, b = rows[index], cols[index]
        if 0 <= a < 3 and 0 <= b < 3:
            choice[index + (3 * a + b,)] = 1.0
    return choice


def tap_choices():
    pair = np.eye(2, dtype=np.float32)
    first, last = [], []
    for c, r in np.ndindex(2, 2):
        s, d, x = np.meshgrid(*map(np.arange, (4, 4, 16)), indexing="ij")
        chosen = tap_choice(x - 5 - 2 * s - r, d - c)
        first.append(np.einsum("sdxt,hk->shdxtk", chosen, pair).reshape(512, 18))
        dr, dc = np.meshgrid(np.arange(4), np.arange(4), indexing="ij")
        chosen = tap_choice(r - dr + 2, c - dc + 2)
        last.append(np.einsum("yxt,hk->yxhtk", chosen, pair).reshape(32, 18))
    middle = []
    for cols, rows in (((0, 1), (0, 1)), ((-1, 2), (0, 1)), ((0, 1), (2, -1)), ((-1, 2), (2, -1))):
        for gamma in cols:
            for rho in rows:
                taps = []
                for c, r in np.ndindex(2, 2):
                    a, b = rho - r + 1, gamma - c + 1
                    taps.append(3 * a + b if 0 <= a < 3 and 0 <= b < 3 else None)
                middle.append(taps)
    return np.stack(first), middle, np.stack(last)


def weights_kernel(cols, height, first_taps, k2, last_taps, choice1, choice3, first, inner, last, scales):
    _, middle, _ = tap_choices()
    ch = k2.shape[1]
    k1 = jnp.concatenate([first_taps[t].astype(F32) for t in range(9)], axis=0).astype(BF16)
    k3 = jnp.concatenate([last_taps[t].astype(F32) for t in range(9)], axis=0).astype(BF16)
    parts = [mm(choice1[i], k1) for i in range(4)]
    first[...] = (0.5 * jnp.concatenate(parts, axis=1)).astype(BF16).reshape(first.shape)
    turned = [(0.5 * jnp.transpose(k2[t].astype(F32))).astype(BF16) for t in range(9)]
    zero = jnp.zeros((ch, ch), BF16)
    for p, taps in enumerate(middle):
        row = [zero if t is None else turned[t] for t in taps]
        inner[p * ch : (p + 1) * ch, :] = jnp.concatenate(row, axis=1)
    parts = [mm(choice3[i], k3) for i in range(4)]
    last[...] = jnp.concatenate(parts, axis=1).astype(BF16)

    def top(value, axes):
        for axis in axes:
            value = jnp.max(value, axis=axis, keepdims=True)
        return value

    gain1 = top(jnp.sum(jnp.abs(k1.astype(F32)), axis=0, keepdims=True), (1,))
    gain2 = sum(jnp.abs(k2[t].astype(F32)) for t in range(9))
    gain2 = top(jnp.sum(gain2, axis=1, keepdims=True), (0,))
    gain3 = jnp.sum(jnp.abs(k3.astype(F32)), axis=1, keepdims=True)
    odd = lax.rem(lax.broadcasted_iota(jnp.int32, gain3.shape, 0), 2) == 1
    gain3 = jnp.maximum(
        jnp.sum(jnp.where(odd, gain3, 0.0), axis=0, keepdims=True),
        jnp.sum(jnp.where(odd, 0.0, gain3), axis=0, keepdims=True),
    )
    predicted = 1.1 * NOISY_MAX * gain1 * gain2 * gain3
    clean = (NOISY_MAX + SIGMA_NOW * predicted) / SCALE_NOW
    spectra = 1.1 * math.sqrt(cols) * 2.0 * MAPS_MAX * clean
    lines = 1.1 * math.sqrt(height) * (spectra + math.sqrt(2.0) * MEASURED_MAX)
    rows = []
    for bound in (spectra, lines):
        rows += [60000.0 / bound, bound / 60000.0]
    scales[...] = jnp.concatenate([jnp.broadcast_to(r, (1, LANES)) for r in rows + rows], axis=0)


def network_weights(first_kernel, inner_kernel, last_kernel, cols, height):
    ch = inner_kernel.shape[1]
    choice1, _, choice3 = tap_choices()
    shapes = ((4, 128, 4 * ch), (16 * ch, 4 * ch), (32, 4 * ch))
    first, inner, last, scales = pl.pallas_call(
        partial(weights_kernel, cols, height),
        out_shape=[jax.ShapeDtypeStruct(d, BF16) for d in shapes]
        + [jax.ShapeDtypeStruct((8, LANES), F32)],
        cost_estimate=pl.CostEstimate(flops=10**7, bytes_accessed=10**6, transcendentals=0),
        name="weights",
    )(
        jnp.transpose(first_kernel, (0, 2, 1)),
        inner_kernel,
        last_kernel,
        jnp.asarray(choice1, BF16),
        jnp.asarray(choice3, BF16),
    )
    return (first, inner, last), scales


def split3(value):
    high = value.astype(BF16)
    rest = value - high.astype(F32)
    middle = rest.astype(BF16)
    return high, middle, (rest - middle.astype(F32)).astype(BF16)


def split2(value):
    high = value.astype(BF16)
    return high, (value - high.astype(F32)).astype(BF16)


def mm(lhs, rhs):
    return lax.dot_general(lhs, rhs, (((1,), (0,)), ((), ())), preferred_element_type=F32)


def mm_nt(lhs, rhs):
    return lax.dot_general(lhs, rhs, (((1,), (1,)), ((), ())), preferred_element_type=F32)


def network_kernel(
    flags, top, center, bottom, side, first, inner, last, pred, clean, tile, q, hid, hid_side, acc
):
    rows, cols = center.shape[1:]
    blocks = rows // 2 + 2
    groups = q.shape[1] // 8 - 1
    used = hid.shape[1]
    step = max(u for u in (1, 2, 3) if blocks % u == 0)

    for ch in range(2):
        tile[ch, 0:8, :] = top[ch, :, 0:cols]
        tile[ch, 8 : 8 + rows, :] = center[ch]
        tile[ch, 8 + rows : 16 + rows, :] = bottom[ch, :, 0:cols]
    edge = jnp.concatenate(
        [
            part
            for ch in range(2)
            for part in (top[ch, :, cols:], side[ch], bottom[ch, :, cols:])
        ],
        axis=0,
    ).astype(BF16)
    w = lax.broadcasted_iota(jnp.int32, (cols, 256), 0)
    k = lax.broadcasted_iota(jnp.int32, (cols, 256), 1)
    e = lax.broadcasted_iota(jnp.int32, (EDGE, 256), 0) + jnp.where(flags[2] != 0, cols, -EDGE)
    ke = lax.broadcasted_iota(jnp.int32, (EDGE, 256), 1)
    for d in range(4):
        sel = jnp.where(w == 2 * k - 3 + d, 1.0, 0.0).astype(BF16)
        sel_side = jnp.where(e == 2 * ke - 3 + d, 1.0, 0.0).astype(BF16)
        both = mm(tile[...].reshape(-1, cols).astype(BF16), sel)
        both += mm(edge, sel_side)
        for ch in range(2):
            q[4 * ch + d] = both[ch * (rows + 16) : (ch + 1) * (rows + 16)]

    end = cols // 2 + 1
    tail = end // 8 * 8
    lines = lax.broadcasted_iota(jnp.int32, (8, 256), 0)
    low = jnp.where((lines == 0) & (flags[2] != 0), 0.0, 1.0)
    high = jnp.where((lines == end - tail) & (flags[3] != 0), 0.0, 1.0)

    def silu_rows(half):
        h = half + half * jnp.tanh(half)
        pieces = []
        for start in range(0, h.shape[0], used):
            pieces += [
                h[start : start + 8] * low,
                h[start + 8 : start + tail],
                h[start + tail : start + tail + 8] * high,
            ]
            if tail + 8 < used:
                pieces.append(h[start + tail + 8 : start + used])
        return jnp.concatenate(pieces, axis=0)

    acc[...] = jnp.zeros(acc.shape, F32)
    hid[0] = jnp.zeros(hid.shape[1:], BF16)
    hid_side[0] = jnp.zeros(hid.shape[1:], BF16)

    def first_layer(t, carry):
        window = q[:, pl.ds(pl.multiple_of(8 * t, 8), 16), :].reshape(128, 256)
        window = jnp.transpose(window)[:used].astype(BF16)
        for s in range(4):
            h = silu_rows(mm(window, first[s]))
            place = 4 * t + s + 1
            hid[place] = h.astype(BF16)
            hid_side[place, :, 0:128] = pltpu.roll(h[:, 128:256], 1, 0).astype(BF16)
            hid_side[place, :, 128:256] = pltpu.roll(h[:, 0:128], used - 1, 0).astype(BF16)
        return carry

    lax.fori_loop(0, groups, first_layer, 0)

    for flag, j in ((0, 0), (1, blocks - 1)):

        @pl.when(flags[flag] != 0)
        def _(j=j):
            hid[j + 1] = jnp.zeros(hid.shape[1:], BF16)
            hid_side[j + 1] = jnp.zeros(hid_side.shape[1:], BF16)

    lane = lax.broadcasted_iota(jnp.int32, (step * used, 256), 1)
    below = lax.rem(lane, 128) < 64

    def next_layers(i, carry):
        j = step * i

        def around(ref, offset):
            return ref[pl.ds(j + offset, step)].reshape(step * used, 256)

        lhs = jnp.concatenate(
            [
                around(hid, 1),
                around(hid_side, 1),
                jnp.where(below, around(hid, 2), around(hid, 0)),
                jnp.where(below, around(hid_side, 2), around(hid_side, 0)),
            ],
            axis=1,
        )
        h = silu_rows(mm(lhs, inner[...])).astype(BF16)
        for u in range(step):
            part = mm_nt(last[...], h[u * used : (u + 1) * used])
            row = j + u
            gone = ((row == 0) & (flags[0] != 0)) | ((row == blocks - 1) & (flags[1] != 0))
            part = part * jnp.where(gone, 0.0, 1.0)
            where = pl.ds(pl.multiple_of(16 * row, 16), 32)
            for c in range(0, used, 128):
                width = min(128, used - c)
                acc[c // 128, where, 0:width] = acc[c // 128, where, 0:width] + part[:, c : c + width]
        return carry

    lax.fori_loop(0, blocks // step, next_layers, 0)

    k = lax.broadcasted_iota(jnp.int32, (256, cols), 0)
    w = lax.broadcasted_iota(jnp.int32, (256, cols), 1)
    total = 0.0
    for d in range(4):
        sel = jnp.where(w == 2 * k - 3 + d, 1.0, 0.0).astype(BF16)
        lines = jnp.concatenate(
            [
                jnp.concatenate(
                    [acc[c, pl.ds(24 + 2 * d + ch, rows, stride=8), :] for c in range(2)], axis=1
                )
                for ch in range(2)
            ],
            axis=0,
        )
        total += mm(jnp.concatenate(split3(lines), axis=1), jnp.concatenate([sel] * 3, axis=0))
    for ch in range(2):
        part = total[ch * rows : (ch + 1) * rows]
        pred[ch] = part
        clean[ch] = (center[ch] - SIGMA_NOW * part) / SCALE_NOW


def run_network(noisy, top, bottom, side, flags, weights):
    _, rows, cols = noisy.shape
    blocks = rows // 2 + 2
    groups = -(-blocks // 4)
    used = ceil_to(cols // 2 + 2, 16)
    vmem = pl.BlockSpec(memory_space=pltpu.VMEM)
    shape = jax.ShapeDtypeStruct(noisy.shape, F32)
    return pl.pallas_call(
        network_kernel,
        out_shape=(shape, shape),
        in_specs=[pl.BlockSpec(memory_space=pltpu.SMEM)] + [vmem] * 7,
        out_specs=(vmem, vmem),
        scratch_shapes=[
            pltpu.VMEM((2, rows + 16, cols), F32),
            pltpu.VMEM((8, 8 * groups + 8, 256), F32),
            pltpu.VMEM((4 * groups + 1, used, 256), BF16),
            pltpu.VMEM((4 * groups + 1, used, 256), BF16),
            pltpu.VMEM((2, 16 * blocks + 16, 128), F32),
        ],
        cost_estimate=pl.CostEstimate(
            flops=20 * rows * cols * 64 * 64, bytes_accessed=24 * rows * cols, transcendentals=0
        ),
        name="network",
    )(flags, top, noisy, bottom, side, *weights)


def halo(noisy):
    gz = lax.axis_size("gz")
    _, rows, cols = noisy.shape
    left, right = noisy[:, :, :EDGE], noisy[:, :, cols - EDGE :]
    side = swap_cores(jnp.where(lax.axis_index("col") == 0, right, left))
    down = [(i, i + 1) for i in range(gz - 1)]
    lower = jnp.concatenate([noisy[:, rows - EDGE :], side[:, rows - EDGE :]], axis=2)
    upper = jnp.concatenate([noisy[:, :EDGE], side[:, :EDGE]], axis=2)
    top = lax.ppermute(lower, "gz", down)
    bottom = lax.ppermute(upper, "gz", [(b, a) for a, b in down])
    return top, bottom, side


def swap_cores(value):
    assert lax.axis_size("col") == 2
    return lax.ppermute(value, "col", [(0, 1), (1, 0)])


def edge_flags():
    row, col = lax.axis_index("gz"), lax.axis_index("col")
    last_row, last_col = lax.axis_size("gz") - 1, lax.axis_size("col") - 1
    return jnp.stack([row == 0, row == last_row, col == 0, col == last_col]).astype(jnp.int32)


def halves(matrix):
    high = matrix.astype(ml_dtypes.bfloat16)
    low = (matrix - high.astype(np.float64)).astype(ml_dtypes.bfloat16)
    return np.stack([high, low])


def fourier_parts(length, scale):
    index = np.arange(length)
    angle = 2.0 * np.pi * (np.outer(index, index) % length) / length
    return np.cos(angle) * scale, np.sin(angle) * scale


def turn_table(radix, inner):
    angle = 2.0 * np.pi * np.outer(np.arange(radix), np.arange(inner)) / (radix * inner)
    return np.stack([np.cos(angle), np.sin(angle)]).astype(np.float32)


def small_dft(values, sign):
    n = len(values)
    if n == 1:
        return values
    if n % 2 == 0:
        even = small_dft(values[0::2], sign)
        odd = small_dft(values[1::2], sign)
        low, high = [], []
        for q in range(n // 2):
            re, im = times_unit(odd[q], q, n, sign)
            low.append((even[q][0] + re, even[q][1] + im))
            high.append((even[q][0] - re, even[q][1] - im))
        return low + high
    if n == 3:
        (r0, i0), (r1, i1), (r2, i2) = values
        sr, si = r1 + r2, i1 + i2
        half = math.sqrt(3.0) / 2.0 * sign
        dr, di = half * (r1 - r2), half * (i1 - i2)
        tr, ti = r0 - 0.5 * sr, i0 - 0.5 * si
        return [(r0 + sr, i0 + si), (tr - di, ti + dr), (tr + di, ti - dr)]
    out = []
    for q in range(n):
        terms = [times_unit(v, a * q, n, sign) for a, v in enumerate(values)]
        out.append((sum(t[0] for t in terms), sum(t[1] for t in terms)))
    return out


def times_unit(value, power, n, sign):
    re, im = value
    power %= n
    if power == 0:
        return re, im
    if 4 * power == n:
        return (-im, re) if sign > 0 else (im, -re)
    if 2 * power == n:
        return -re, -im
    if 4 * power == 3 * n:
        return (im, -re) if sign > 0 else (-im, re)
    c = math.cos(2.0 * math.pi * power / n)
    s = sign * math.sin(2.0 * math.pi * power / n)
    return c * re - s * im, c * im + s * re


def turn(value, cos, sin, sign):
    re, im = value
    if sign > 0:
        return re * cos - im * sin, im * cos + re * sin
    return re * cos + im * sin, im * cos - re * sin


def beside(parts, axis):
    return jnp.concatenate([parts[0], parts[0], parts[1]], axis=axis)


def against(matrix, axis):
    return jnp.concatenate([matrix[0], matrix[1], matrix[0]], axis=axis)


def columns_forward_kernel(first, mine, other, maps, scales, matrix, table, out):
    radix, inner = table.shape[1:]
    coils = maps.shape[0]
    rows, cols = mine.shape[1:]
    groups = out.shape[0]
    per = inner // groups
    lead = first[0] != 0
    image = [
        jnp.concatenate(
            [jnp.where(lead, mine[p], other[p]), jnp.where(lead, other[p], mine[p])], axis=1
        )
        * scales[0:1, 0:1]
        for p in range(2)
    ]
    turned = []
    for coil in range(coils):
        maps_real, maps_imag = maps[coil, 0], maps[coil, 1]
        coil_image = (
            maps_real * image[0] - maps_imag * image[1],
            maps_real * image[1] + maps_imag * image[0],
        )
        parts = [
            tuple(v[:, a * inner : (a + 1) * inner] for v in coil_image) for a in range(radix)
        ]
        parts = small_dft(parts, -1)
        turned.append(
            [
                turn(part, table[0, q : q + 1, :], table[1, q : q + 1, :], -1) if q else part
                for q, part in enumerate(parts)
            ]
        )
    for q in range(radix):
        data = jnp.concatenate([jnp.concatenate(turned[c][q], axis=1) for c in range(coils)], axis=0)
        result = mm_nt(against(matrix, 1), beside(split2(data), 1))
        for p in range(2):
            for g in range(groups):
                start = p * inner + g * per
                for c in range(coils):
                    out[g, p, c, q] = result[start : start + per, c * rows : (c + 1) * rows]


def columns_forward(first, mine, other, maps, scales, groups, chunk, chunks):
    coils, _, rows, cols = maps.shape
    coils //= chunks
    inner = INNER
    radix = cols // inner
    c, s = fourier_parts(inner, 1.0 / math.sqrt(cols))
    matrix = halves(np.block([[c, s], [-s, c]]))
    table = turn_table(radix, inner)
    vmem = pl.BlockSpec(memory_space=pltpu.VMEM)
    per = inner // groups
    return pl.pallas_call(
        columns_forward_kernel,
        out_shape=jax.ShapeDtypeStruct((groups, 2, coils, radix, per, rows), F32),
        grid=(1,),
        in_specs=[
            pl.BlockSpec(memory_space=pltpu.SMEM),
            vmem,
            vmem,
            pl.BlockSpec((coils, 2, rows, cols), lambda i: (chunk, 0, 0, 0)),
            vmem,
            vmem,
            vmem,
        ],
        out_specs=pl.BlockSpec(
            (groups, 2, coils, radix, per, rows), lambda i: (0, 0, 0, 0, 0, 0)
        ),
        cost_estimate=pl.CostEstimate(
            flops=24 * coils * rows * cols * inner,
            bytes_accessed=16 * coils * rows * cols,
            transcendentals=0,
        ),
        name="columns_forward",
    )(first, mine, other, maps, scales, jnp.asarray(matrix), jnp.asarray(table))


def rows_kernel(data, kept, target, scales, forward, inverse, table, out, lines):
    radix = table.shape[1]
    count = data.shape[2]
    parts = small_dft([(data[a, 0], data[a, 1]) for a in range(radix)], -1)
    for q, part in enumerate(parts):
        if q:
            part = turn(part, table[0, q : q + 1, :], table[1, q : q + 1, :], -1)
        for p in range(2):
            lines[q * count : (q + 1) * count, p * LANES : (p + 1) * LANES] = part[p]
    spectrum = mm(beside(split2(lines[...]), 1), against(forward, 0))
    keep = kept[...].reshape(radix * count, LANES) * scales[2:3, :]
    unit = scales[1:2, :]
    residual = jnp.concatenate(
        [
            keep
            * (spectrum[:, p * LANES : (p + 1) * LANES] * unit - target[p].reshape(-1, LANES))
            for p in range(2)
        ],
        axis=1,
    )
    lines[...] = mm(beside(split2(residual), 1), against(inverse, 0))
    back = []
    for q in range(radix):
        part = tuple(
            lines[q * count : (q + 1) * count, p * LANES : (p + 1) * LANES] for p in range(2)
        )
        if q:
            part = turn(part, table[0, q : q + 1, :], table[1, q : q + 1, :], 1)
        back.append(part)
    for a, (re, im) in enumerate(small_dft(back, 1)):
        out[a, 0] = re
        out[a, 1] = im


def rows_both_ways(data, kept, target, scales, first_line):
    radix, _, count, _ = data.shape
    pencil = kept.shape[1]
    c, s = fourier_parts(LANES, 1.0 / math.sqrt(radix * LANES))
    forward = halves(np.block([[c, -s], [s, c]]))
    inverse = halves(np.block([[c, s], [-s, c]]))
    table = turn_table(radix, LANES)
    block = max(b for b in range(8, 56, 8) if pencil % b == 0)
    offset, repeat = first_line // block, pencil // block
    vmem = pl.BlockSpec(memory_space=pltpu.VMEM)
    spec = pl.BlockSpec((radix, 2, block, LANES), lambda i: (0, 0, i, 0))
    return pl.pallas_call(
        rows_kernel,
        out_shape=jax.ShapeDtypeStruct(data.shape, F32),
        grid=(count // block,),
        in_specs=[
            spec,
            pl.BlockSpec((radix, block, LANES), lambda i: (0, lax.rem(i + offset, repeat), 0)),
            pl.BlockSpec((2, radix, block, LANES), lambda i: (0, 0, i + offset, 0)),
            vmem,
            vmem,
            vmem,
            vmem,
        ],
        out_specs=spec,
        scratch_shapes=[pltpu.VMEM((radix * block, 2 * LANES), F32)],
        cost_estimate=pl.CostEstimate(
            flops=24 * radix * count * LANES * LANES,
            bytes_accessed=32 * radix * count * LANES,
            transcendentals=0,
        ),
        name="rows_both_ways",
    )(data, kept, target, scales, jnp.asarray(forward), jnp.asarray(inverse), jnp.asarray(table))


def columns_inverse_kernel(last, first, data, maps, scales, matrix, table, *refs):
    radix, inner = table.shape[1:]
    groups = data.shape[0]
    coils, _, rows, cols = maps.shape
    base, outs = (None, refs) if len(refs) == 1 else (refs[0], refs[1:])
    parts = []
    for q in range(radix):
        lines = jnp.concatenate(
            [
                jnp.transpose(
                    jnp.concatenate(
                        [data[g, p, c, q] for p in range(2) for g in range(groups)], axis=0
                    )
                )
                for c in range(coils)
            ],
            axis=0,
        )
        result = mm(beside(split2(lines), 1), against(matrix, 0))
        part = (result[:, :inner], result[:, inner:])
        if q:
            part = turn(part, table[0, q : q + 1, :], table[1, q : q + 1, :], 1)
        parts.append(part)
    sums = [[], []]
    for a, (re, im) in enumerate(small_dft(parts, 1)):
        where = slice(a * inner, (a + 1) * inner)
        total = [0.0, 0.0]
        for c in range(coils):
            maps_real, maps_imag = maps[c, 0, :, where], maps[c, 1, :, where]
            x, y = re[c * rows : (c + 1) * rows], im[c * rows : (c + 1) * rows]
            total[0] += maps_real * x + maps_imag * y
            total[1] += maps_real * y - maps_imag * x
        for p in range(2):
            part = total[p] * scales[3:4, 0:1]
            sums[p].append(part if base is None else base[p, :, where] + part)
    lead = first[0] != 0
    for p in range(2):
        line = jnp.concatenate(sums[p], axis=1)
        if last:
            own, away = line[:, : cols // 2], line[:, cols // 2 :]
            outs[0][p] = jnp.where(lead, own, away)
            outs[1][p] = jnp.where(lead, away, own)
        else:
            outs[0][p] = line


def columns_inverse(first, data, maps, scales, chunk, chunks, base):
    groups, _, coils, radix, per, rows = data.shape
    cols = maps.shape[3]
    inner = cols // radix
    c, s = fourier_parts(inner, 1.0 / math.sqrt(cols))
    matrix = halves(np.block([[c, s], [-s, c]]))
    table = turn_table(radix, inner)
    vmem = pl.BlockSpec(memory_space=pltpu.VMEM)
    last = chunk == chunks - 1
    if last:
        shape = [jax.ShapeDtypeStruct((2, rows, cols // 2), F32)] * 2
    else:
        shape = [jax.ShapeDtypeStruct((2, rows, cols), F32)]
    return pl.pallas_call(
        partial(columns_inverse_kernel, last),
        out_shape=shape,
        grid=(1,),
        in_specs=[
            pl.BlockSpec(memory_space=pltpu.SMEM),
            vmem,
            pl.BlockSpec((coils, 2, rows, cols), lambda i: (chunk, 0, 0, 0)),
            vmem,
            vmem,
            vmem,
        ]
        + [vmem] * len(base),
        out_specs=[vmem] * len(shape),
        cost_estimate=pl.CostEstimate(
            flops=24 * coils * rows * cols * inner,
            bytes_accessed=16 * coils * rows * cols,
            transcendentals=0,
        ),
        name="columns_inverse",
    )(first, data, maps, scales, jnp.asarray(matrix), jnp.asarray(table), *base)


def target_kernel(radix3, token, *refs):
    tiles = (len(refs) - 4) // 2
    measured, sampled = refs[:tiles], refs[tiles : 2 * tiles]
    target, kept, lines, order = refs[2 * tiles :]
    radix, pencil, _ = kept.shape
    count, height = lines.shape
    coils = count // pencil
    per = pencil // radix3

    @pl.when(pl.program_id(0) == 0)
    def _():
        source = lax.broadcasted_iota(jnp.int32, (height, LANES), 0)
        place = lax.broadcasted_iota(jnp.int32, (height, LANES), 1)
        for q in range(radix):
            order[:, q * LANES : (q + 1) * LANES] = jnp.where(
                source == radix * place + q, 1.0, 0.0
            ).astype(BF16)
        for t in range(tiles):
            for q in range(radix3):
                lines[q * per : (q + 1) * per, t * LANES : (t + 1) * LANES] = sampled[t][
                    pl.ds(q, per, stride=radix3), :
                ].astype(F32)
        picked = mm(lines[0:pencil, :].astype(BF16), order[...])
        for q in range(radix):
            kept[q] = picked[:, q * LANES : (q + 1) * LANES]

    for t in range(tiles):
        source = measured[t].reshape(count, LANES)
        for c in range(coils):
            for q in range(radix3):
                start = c * pencil + q * per
                lines[start : start + per, t * LANES : (t + 1) * LANES] = source[
                    pl.ds(q * coils + c, per, stride=radix3 * coils), :
                ]
    high, low = split2(lines[...])
    for q in range(0, radix, 2):
        width = min(2, radix - q) * LANES
        part = order[:, q * LANES : q * LANES + width]
        picked = mm(high, part) + mm(low, part)
        for k in range(0, width, LANES):
            target[0, q + k // LANES] = picked[:, k : k + LANES]


def prepare_target(token, measured, sampled, radix3):
    _, pencil, coils, height = measured.shape
    radix = height // LANES
    count = pencil * coils
    return pl.pallas_call(
        partial(target_kernel, radix3),
        out_shape=(
            jax.ShapeDtypeStruct((2, radix, count, LANES), F32),
            jax.ShapeDtypeStruct((radix, pencil, LANES), F32),
        ),
        grid=(2,),
        in_specs=[pl.BlockSpec(memory_space=pltpu.SMEM)]
        + [
            pl.BlockSpec((1, pencil, coils, LANES), lambda i, t=t: (i, 0, 0, t))
            for t in range(radix)
        ]
        + [pl.BlockSpec((pencil, LANES), lambda i, t=t: (0, t)) for t in range(radix)],
        out_specs=(
            pl.BlockSpec((1, radix, count, LANES), lambda i: (i, 0, 0, 0)),
            pl.BlockSpec((radix, pencil, LANES), lambda i: (0, 0, 0)),
        ),
        scratch_shapes=[pltpu.VMEM((count, height), F32), pltpu.VMEM((height, height), BF16)],
        cost_estimate=pl.CostEstimate(
            flops=8 * count * height * height, bytes_accessed=16 * count * height, transcendentals=0
        ),
        name="target",
    )(token, *[measured] * radix, *[sampled] * radix)


def exchange(value):
    return lax.all_to_all(value, "gz", split_axis=0, concat_axis=0, tiled=True)


def after(value, *earlier):
    return lax.optimization_barrier((value, *earlier))[0]


def local(
    noisy_image, fresh_noise, coil_maps, measured, sampled, first_kernel, inner_kernels, last_kernel
):
    groups = lax.axis_size("gz")
    coils, _, rows, cols = coil_maps.shape
    height = measured.shape[3]
    radix, inner = cols // INNER, INNER
    per = inner // groups
    row_radix = height // LANES
    chunks = 2
    pencil = radix * per
    count = coils * pencil // chunks
    lead = (lax.axis_index("col") == 0).astype(jnp.int32)[None]

    weights, scales = network_weights(
        first_kernel, inner_kernels[0], last_kernel, cols, height
    )
    top, bottom, side = halo(noisy_image)
    predicted, clean = run_network(noisy_image, top, bottom, side, edge_flags(), weights)
    other = swap_cores(clean)

    token = lead
    arrived = []
    for chunk in range(chunks):
        spectra = columns_forward(token, clean, other, coil_maps, scales, groups, chunk, chunks)
        spectra = spectra.reshape(groups, 2, count, rows).astype(jnp.float16)
        if chunk == 0:
            target, kept = prepare_target(after(lead, spectra), measured, sampled, radix)
            token = after(lead, kept)
        arrived.append(exchange(spectra))

    back = []
    for chunk in range(chunks):
        lines = after(arrived[chunk], *back).astype(F32)
        if rows != LANES:
            lines = jnp.transpose(lines, (1, 2, 0, 3)).reshape(2, -1, row_radix, LANES)
            lines = jnp.transpose(lines, (2, 0, 1, 3))
        lines = rows_both_ways(lines, kept, target, scales, chunk * (coils // chunks) * pencil)
        if rows != LANES:
            lines = jnp.transpose(lines, (1, 2, 0, 3)).reshape(2, -1, groups, rows)
            lines = jnp.transpose(lines, (2, 0, 1, 3))
        back.append(lines.astype(jnp.float16))

    gradient = []
    for chunk in range(chunks):
        lines = after(exchange(back[chunk]), *gradient).astype(F32)
        lines = lines.reshape(groups, 2, coils // chunks, radix, per, rows)
        gradient = columns_inverse(lead, lines, coil_maps, scales, chunk, chunks, gradient)

    own, away = gradient
    own = own + swap_cores(away)
    update = clean - STEP_GAIN * own
    return SCALE_NEXT * update + DIRECT_GAIN * predicted + NOISE_GAIN * fresh_noise


def solution(mesh):
    in_specs = (
        P("grp", "gz", "col"),
        P("grp", "gz", "col"),
        P("col", "grp", "gz", None),
        P("grp", "gz", "col", None),
        P("gz", "grp"),
        P(),
        P(),
        P(),
    )
    out_specs = P("grp", "gz", "col")
    return jax.shard_map(local, mesh=mesh, in_specs=in_specs, out_specs=out_specs, check_vma=False)
```

```python
import math
from functools import partial

import jax
import jax.numpy as jnp
import ml_dtypes
import numpy as np
from jax import lax
from jax.experimental import pallas as pl
from jax.experimental.pallas import tpu as pltpu
from jax.sharding import PartitionSpec as P

SCALE_NOW = 0.8
SIGMA_NOW = 0.6
STEP_GAIN = 1.0
SCALE_NEXT = 0.9
DIRECT_GAIN = 0.31622776601683794
NOISE_GAIN = 0.3

NOISY_MAX = 6.0
MAPS_MAX = 1.5
MEASURED_MAX = 2.4

F32 = jnp.float32
BF16 = jnp.bfloat16
LANES = 128
EDGE = 8
MIB = 1024 * 1024
INNER = 256


def ceil_to(value, step):
    return -(-value // step) * step


def tap_choice(rows, cols):
    choice = np.zeros(rows.shape + (9,), np.float32)
    for index in np.ndindex(rows.shape):
        a, b = rows[index], cols[index]
        if 0 <= a < 3 and 0 <= b < 3:
            choice[index + (3 * a + b,)] = 1.0
    return choice


def tap_choices():
    pair = np.eye(2, dtype=np.float32)
    first, last = [], []
    for c, r in np.ndindex(2, 2):
        s, d, x = np.meshgrid(*map(np.arange, (4, 4, 16)), indexing="ij")
        chosen = tap_choice(x - 5 - 2 * s - r, d - c)
        first.append(np.einsum("sdxt,hk->shdxtk", chosen, pair).reshape(512, 18))
        dr, dc = np.meshgrid(np.arange(4), np.arange(4), indexing="ij")
        chosen = tap_choice(r - dr + 2, c - dc + 2)
        last.append(np.einsum("yxt,hk->yxhtk", chosen, pair).reshape(32, 18))
    middle = []
    for cols, rows in (((0, 1), (0, 1)), ((-1, 2), (0, 1)), ((0, 1), (2, -1)), ((-1, 2), (2, -1))):
        for gamma in cols:
            for rho in rows:
                taps = []
                for c, r in np.ndindex(2, 2):
                    a, b = rho - r + 1, gamma - c + 1
                    taps.append(3 * a + b if 0 <= a < 3 and 0 <= b < 3 else None)
                middle.append(taps)
    return np.stack(first), middle, np.stack(last)


def weights_kernel(cols, height, first_taps, k2, last_taps, choice1, choice3, first, inner, last, scales):
    _, middle, _ = tap_choices()
    ch = k2.shape[1]
    k1 = jnp.concatenate([first_taps[t].astype(F32) for t in range(9)], axis=0).astype(BF16)
    k3 = jnp.concatenate([last_taps[t].astype(F32) for t in range(9)], axis=0).astype(BF16)
    parts = [mm(choice1[i], k1) for i in range(4)]
    first[...] = (0.5 * jnp.concatenate(parts, axis=1)).astype(BF16).reshape(first.shape)
    turned = [(0.5 * jnp.transpose(k2[t].astype(F32))).astype(BF16) for t in range(9)]
    zero = jnp.zeros((ch, ch), BF16)
    for p, taps in enumerate(middle):
        row = [zero if t is None else turned[t] for t in taps]
        inner[p * ch : (p + 1) * ch, :] = jnp.concatenate(row, axis=1)
    parts = [mm(choice3[i], k3) for i in range(4)]
    last[...] = jnp.concatenate(parts, axis=1).astype(BF16)

    def top(value, axes):
        for axis in axes:
            value = jnp.max(value, axis=axis, keepdims=True)
        return value

    gain1 = top(jnp.sum(jnp.abs(k1.astype(F32)), axis=0, keepdims=True), (1,))
    gain2 = sum(jnp.abs(k2[t].astype(F32)) for t in range(9))
    gain2 = top(jnp.sum(gain2, axis=1, keepdims=True), (0,))
    gain3 = jnp.sum(jnp.abs(k3.astype(F32)), axis=1, keepdims=True)
    odd = lax.rem(lax.broadcasted_iota(jnp.int32, gain3.shape, 0), 2) == 1
    gain3 = jnp.maximum(
        jnp.sum(jnp.where(odd, gain3, 0.0), axis=0, keepdims=True),
        jnp.sum(jnp.where(odd, 0.0, gain3), axis=0, keepdims=True),
    )
    predicted = 1.1 * NOISY_MAX * gain1 * gain2 * gain3
    clean = (NOISY_MAX + SIGMA_NOW * predicted) / SCALE_NOW
    spectra = 1.1 * math.sqrt(cols) * 2.0 * MAPS_MAX * clean
    lines = 1.1 * math.sqrt(height) * (spectra + math.sqrt(2.0) * MEASURED_MAX)
    rows = []
    for bound in (spectra, lines):
        rows += [60000.0 / bound, bound / 60000.0]
    scales[...] = jnp.concatenate([jnp.broadcast_to(r, (1, LANES)) for r in rows + rows], axis=0)


def network_weights(first_kernel, inner_kernel, last_kernel, cols, height):
    ch = inner_kernel.shape[1]
    choice1, _, choice3 = tap_choices()
    shapes = ((4, 128, 4 * ch), (16 * ch, 4 * ch), (32, 4 * ch))
    first, inner, last, scales = pl.pallas_call(
        partial(weights_kernel, cols, height),
        out_shape=[jax.ShapeDtypeStruct(d, BF16) for d in shapes]
        + [jax.ShapeDtypeStruct((8, LANES), F32)],
        cost_estimate=pl.CostEstimate(flops=10**7, bytes_accessed=10**6, transcendentals=0),
        name="weights",
    )(
        jnp.transpose(first_kernel, (0, 2, 1)),
        inner_kernel,
        last_kernel,
        jnp.asarray(choice1, BF16),
        jnp.asarray(choice3, BF16),
    )
    return (first, inner, last), scales


def split3(value):
    high = value.astype(BF16)
    rest = value - high.astype(F32)
    middle = rest.astype(BF16)
    return high, middle, (rest - middle.astype(F32)).astype(BF16)


def split2(value):
    high = value.astype(BF16)
    return high, (value - high.astype(F32)).astype(BF16)


def mm(lhs, rhs):
    return lax.dot_general(lhs, rhs, (((1,), (0,)), ((), ())), preferred_element_type=F32)


def mm_nt(lhs, rhs):
    return lax.dot_general(lhs, rhs, (((1,), (1,)), ((), ())), preferred_element_type=F32)


def network_kernel(
    flags, top, center, bottom, side, first, inner, last, pred, clean, tile, q, hid, hid_side, done, acc
):
    rows, cols = center.shape[1:]
    blocks = rows // 2 + 2
    groups = q.shape[1] // 8 - 1
    used = hid.shape[1]
    step = done.shape[0] // used

    for ch in range(2):
        tile[ch, 0:8, :] = top[ch, :, 0:cols]
        tile[ch, 8 : 8 + rows, :] = center[ch]
        tile[ch, 8 + rows : 16 + rows, :] = bottom[ch, :, 0:cols]
    edge = jnp.concatenate(
        [
            part
            for ch in range(2)
            for part in (top[ch, :, cols:], side[ch], bottom[ch, :, cols:])
        ],
        axis=0,
    ).astype(BF16)
    w = lax.broadcasted_iota(jnp.int32, (cols, 256), 0)
    k = lax.broadcasted_iota(jnp.int32, (cols, 256), 1)
    e = lax.broadcasted_iota(jnp.int32, (EDGE, 256), 0) + jnp.where(flags[2] != 0, cols, -EDGE)
    ke = lax.broadcasted_iota(jnp.int32, (EDGE, 256), 1)
    for d in range(4):
        sel = jnp.where(w == 2 * k - 3 + d, 1.0, 0.0).astype(BF16)
        sel_side = jnp.where(e == 2 * ke - 3 + d, 1.0, 0.0).astype(BF16)
        both = mm(tile[...].reshape(-1, cols).astype(BF16), sel)
        both += mm(edge, sel_side)
        for ch in range(2):
            q[4 * ch + d] = both[ch * (rows + 16) : (ch + 1) * (rows + 16)]

    end = cols // 2 + 1
    tail = end // 8 * 8
    lines = lax.broadcasted_iota(jnp.int32, (8, 256), 0)
    low = jnp.where((lines == 0) & (flags[2] != 0), 0.0, 1.0)
    high = jnp.where((lines == end - tail) & (flags[3] != 0), 0.0, 1.0)

    def silu_rows(half):
        h = half + half * jnp.tanh(half)
        pieces = []
        for start in range(0, h.shape[0], used):
            pieces += [
                h[start : start + 8] * low,
                h[start + 8 : start + tail],
                h[start + tail : start + tail + 8] * high,
            ]
            if tail + 8 < used:
                pieces.append(h[start + tail + 8 : start + used])
        return jnp.concatenate(pieces, axis=0)

    acc[...] = jnp.zeros(acc.shape, F32)
    hid[0] = jnp.zeros(hid.shape[1:], BF16)
    hid_side[0] = jnp.zeros(hid.shape[1:], BF16)

    def first_layer(t, carry):
        window = q[:, pl.ds(pl.multiple_of(8 * t, 8), 16), :].reshape(128, 256)
        window = jnp.transpose(window)[:used].astype(BF16)
        for s in range(4):
            h = silu_rows(mm(window, first[s]))
            place = 4 * t + s + 1
            hid[place] = h.astype(BF16)
            hid_side[place, :, 0:128] = pltpu.roll(h[:, 128:256], 1, 0).astype(BF16)
            hid_side[place, :, 128:256] = pltpu.roll(h[:, 0:128], used - 1, 0).astype(BF16)
        return carry

    lax.fori_loop(0, groups, first_layer, 0)

    for flag, j in ((0, 0), (1, blocks - 1)):

        @pl.when(flags[flag] != 0)
        def _(j=j):
            hid[j + 1] = jnp.zeros(hid.shape[1:], BF16)
            hid_side[j + 1] = jnp.zeros(hid_side.shape[1:], BF16)

    lane = lax.broadcasted_iota(jnp.int32, (step * used, 256), 1)
    below = lax.rem(lane, 128) < 64

    def next_layers(i, carry):
        j = step * i

        def around(ref, offset):
            return ref[pl.ds(j + offset, step)].reshape(step * used, 256)

        lhs = jnp.concatenate(
            [
                around(hid, 1),
                around(hid_side, 1),
                jnp.where(below, around(hid, 2), around(hid, 0)),
                jnp.where(below, around(hid_side, 2), around(hid_side, 0)),
            ],
            axis=1,
        )
        add_parts(j - step)
        done[...] = silu_rows(mm(lhs, inner[...])).astype(BF16)
        return carry

    def add_parts(j):
        for u in range(step):
            part = mm_nt(last[...], done[u * used : (u + 1) * used])
            row = j + u
            gone = ((row == 0) & (flags[0] != 0)) | ((row == blocks - 1) & (flags[1] != 0))
            part = part * jnp.where(gone, 0.0, 1.0)
            where = pl.ds(pl.multiple_of(16 * (row + step), 16), 32)
            for c in range(0, used, 128):
                width = min(128, used - c)
                acc[c // 128, where, 0:width] = acc[c // 128, where, 0:width] + part[:, c : c + width]

    done[...] = jnp.zeros(done.shape, BF16)
    lax.fori_loop(0, blocks // step, next_layers, 0)
    add_parts(blocks - step)

    def pixels(d):
        return jnp.concatenate(
            [
                jnp.concatenate(
                    [
                        acc[c, pl.ds(24 + 16 * step + 2 * d + ch, rows, stride=8), :]
                        for c in range(2)
                    ],
                    axis=1,
                )
                for ch in range(2)
            ],
            axis=0,
        )

    k = lax.broadcasted_iota(jnp.int32, (256, cols), 0)
    w = lax.broadcasted_iota(jnp.int32, (256, cols), 1)
    total = 0.0
    for d, other, shift in ((1, 3, 1), (2, 0, 255)):
        line = pixels(d) + pltpu.roll(pixels(other), shift, 1)
        sel = jnp.where(w == 2 * k - 3 + d, 1.0, 0.0).astype(BF16)
        both = mm(jnp.concatenate(split2(line), axis=0), sel)
        total += both[: 2 * rows] + both[2 * rows :]
    for ch in range(2):
        part = total[ch * rows : (ch + 1) * rows]
        pred[ch] = part
        clean[ch] = (center[ch] - SIGMA_NOW * part) / SCALE_NOW


def run_network(noisy, top, bottom, side, flags, weights):
    _, rows, cols = noisy.shape
    blocks = rows // 2 + 2
    groups = -(-blocks // 4)
    used = ceil_to(cols // 2 + 2, 16)
    step = max(u for u in (1, 2, 3, 6) if blocks % u == 0)
    vmem = pl.BlockSpec(memory_space=pltpu.VMEM)
    shape = jax.ShapeDtypeStruct(noisy.shape, F32)
    return pl.pallas_call(
        network_kernel,
        out_shape=(shape, shape),
        in_specs=[pl.BlockSpec(memory_space=pltpu.SMEM)] + [vmem] * 7,
        out_specs=(vmem, vmem),
        scratch_shapes=[
            pltpu.VMEM((2, rows + 16, cols), F32),
            pltpu.VMEM((8, 8 * groups + 8, 256), F32),
            pltpu.VMEM((4 * groups + 1, used, 256), BF16),
            pltpu.VMEM((4 * groups + 1, used, 256), BF16),
            pltpu.VMEM((step * used, 256), BF16),
            pltpu.VMEM((2, 16 * (blocks + step) + 16, 128), F32),
        ],
        cost_estimate=pl.CostEstimate(
            flops=20 * rows * cols * 64 * 64, bytes_accessed=24 * rows * cols, transcendentals=0
        ),
        compiler_params=pltpu.CompilerParams(vmem_limit_bytes=40 * MIB),
        name="network",
    )(flags, top, noisy, bottom, side, *weights)


def halo(noisy):
    gz = lax.axis_size("gz")
    _, rows, cols = noisy.shape
    left, right = noisy[:, :, :EDGE], noisy[:, :, cols - EDGE :]
    side = swap_cores(jnp.where(lax.axis_index("col") == 0, right, left))
    down = [(i, i + 1) for i in range(gz - 1)]
    lower = jnp.concatenate([noisy[:, rows - EDGE :], side[:, rows - EDGE :]], axis=2)
    upper = jnp.concatenate([noisy[:, :EDGE], side[:, :EDGE]], axis=2)
    top = lax.ppermute(lower, "gz", down)
    bottom = lax.ppermute(upper, "gz", [(b, a) for a, b in down])
    return top, bottom, side


def swap_cores(value):
    assert lax.axis_size("col") == 2
    return lax.ppermute(value, "col", [(0, 1), (1, 0)])


def edge_flags():
    row, col = lax.axis_index("gz"), lax.axis_index("col")
    last_row, last_col = lax.axis_size("gz") - 1, lax.axis_size("col") - 1
    return jnp.stack([row == 0, row == last_row, col == 0, col == last_col]).astype(jnp.int32)


def halves(matrix):
    high = matrix.astype(ml_dtypes.bfloat16)
    low = (matrix - high.astype(np.float64)).astype(ml_dtypes.bfloat16)
    return np.stack([high, low])


def fourier_parts(length, scale):
    index = np.arange(length)
    angle = 2.0 * np.pi * (np.outer(index, index) % length) / length
    return np.cos(angle) * scale, np.sin(angle) * scale


def turn_table(radix, inner):
    angle = 2.0 * np.pi * np.outer(np.arange(radix), np.arange(inner)) / (radix * inner)
    return np.stack([np.cos(angle), np.sin(angle)]).astype(np.float32)


def small_dft(values, sign):
    n = len(values)
    if n == 1:
        return values
    if n % 2 == 0:
        even = small_dft(values[0::2], sign)
        odd = small_dft(values[1::2], sign)
        low, high = [], []
        for q in range(n // 2):
            re, im = times_unit(odd[q], q, n, sign)
            low.append((even[q][0] + re, even[q][1] + im))
            high.append((even[q][0] - re, even[q][1] - im))
        return low + high
    if n == 3:
        (r0, i0), (r1, i1), (r2, i2) = values
        sr, si = r1 + r2, i1 + i2
        half = math.sqrt(3.0) / 2.0 * sign
        dr, di = half * (r1 - r2), half * (i1 - i2)
        tr, ti = r0 - 0.5 * sr, i0 - 0.5 * si
        return [(r0 + sr, i0 + si), (tr - di, ti + dr), (tr + di, ti - dr)]
    out = []
    for q in range(n):
        terms = [times_unit(v, a * q, n, sign) for a, v in enumerate(values)]
        out.append((sum(t[0] for t in terms), sum(t[1] for t in terms)))
    return out


def times_unit(value, power, n, sign):
    re, im = value
    power %= n
    if power == 0:
        return re, im
    if 4 * power == n:
        return (-im, re) if sign > 0 else (im, -re)
    if 2 * power == n:
        return -re, -im
    if 4 * power == 3 * n:
        return (im, -re) if sign > 0 else (-im, re)
    c = math.cos(2.0 * math.pi * power / n)
    s = sign * math.sin(2.0 * math.pi * power / n)
    return c * re - s * im, c * im + s * re


def turn(value, cos, sin, sign):
    re, im = value
    if sign > 0:
        return re * cos - im * sin, im * cos + re * sin
    return re * cos + im * sin, im * cos - re * sin


def beside(parts, axis):
    return jnp.concatenate([parts[0], parts[0], parts[1]], axis=axis)


def against(matrix, axis):
    return jnp.concatenate([matrix[0], matrix[1], matrix[0]], axis=axis)


def columns_forward_kernel(first, mine, other, maps, scales, matrix, table, out):
    radix, inner = table.shape[1:]
    coils = maps.shape[0]
    rows, cols = mine.shape[1:]
    groups = out.shape[0]
    per = inner // groups
    lead, me = first[0] != 0, first[1]
    image = [
        jnp.concatenate(
            [jnp.where(lead, mine[p], other[p]), jnp.where(lead, other[p], mine[p])], axis=1
        )
        * scales[0:1, 0:1]
        for p in range(2)
    ]
    turned = []
    for coil in range(coils):
        maps_real, maps_imag = maps[coil, 0], maps[coil, 1]
        coil_image = (
            maps_real * image[0] - maps_imag * image[1],
            maps_real * image[1] + maps_imag * image[0],
        )
        parts = [
            tuple(v[:, a * inner : (a + 1) * inner] for v in coil_image) for a in range(radix)
        ]
        parts = small_dft(parts, -1)
        turned.append(
            [
                turn(part, table[0, q : q + 1, :], table[1, q : q + 1, :], -1) if q else part
                for q, part in enumerate(parts)
            ]
        )
    for q in range(radix):
        data = jnp.concatenate([jnp.concatenate(turned[c][q], axis=1) for c in range(coils)], axis=0)
        result = mm_nt(against(matrix, 1), beside(split2(data), 1))
        for p in range(2):
            for g in range(groups):
                start = p * inner + g * per
                for c in range(coils):
                    out[lax.bitwise_xor(g, me), p, c, q] = result[start : start + per, c * rows : (c + 1) * rows]


def columns_forward(first, mine, other, maps, scales, groups, chunk, chunks):
    coils, _, rows, cols = maps.shape
    coils //= chunks
    inner = INNER
    radix = cols // inner
    c, s = fourier_parts(inner, 1.0 / math.sqrt(cols))
    matrix = halves(np.block([[c, s], [-s, c]]))
    table = turn_table(radix, inner)
    vmem = pl.BlockSpec(memory_space=pltpu.VMEM)
    per = inner // groups
    return pl.pallas_call(
        columns_forward_kernel,
        out_shape=jax.ShapeDtypeStruct((groups, 2, coils, radix, per, rows), F32),
        grid=(1,),
        in_specs=[
            pl.BlockSpec(memory_space=pltpu.SMEM),
            vmem,
            vmem,
            pl.BlockSpec((coils, 2, rows, cols), lambda i: (chunk, 0, 0, 0)),
            vmem,
            vmem,
            vmem,
        ],
        out_specs=pl.BlockSpec(
            (groups, 2, coils, radix, per, rows), lambda i: (0, 0, 0, 0, 0, 0)
        ),
        cost_estimate=pl.CostEstimate(
            flops=24 * coils * rows * cols * inner,
            bytes_accessed=16 * coils * rows * cols,
            transcendentals=0,
        ),
        compiler_params=pltpu.CompilerParams(vmem_limit_bytes=20 * MIB),
        name="columns_forward",
    )(first, mine, other, maps, scales, jnp.asarray(matrix), jnp.asarray(table))


def rows_kernel(place, data, kept, target, scales, forward, inverse, table, out, lines):
    radix = table.shape[1]
    count = data.shape[2]
    spots = [lax.bitwise_xor(a, place[1]) for a in range(radix)]
    parts = small_dft([(data[spot, 0], data[spot, 1]) for spot in spots], -1)
    for q, part in enumerate(parts):
        if q:
            part = turn(part, table[0, q : q + 1, :], table[1, q : q + 1, :], -1)
        for p in range(2):
            lines[q * count : (q + 1) * count, p * LANES : (p + 1) * LANES] = part[p]
    spectrum = mm(beside(split2(lines[...]), 1), against(forward, 0))
    keep = kept[...].reshape(radix * count, LANES) * scales[2:3, :]
    unit = scales[1:2, :]
    residual = jnp.concatenate(
        [
            keep
            * (spectrum[:, p * LANES : (p + 1) * LANES] * unit - target[p].reshape(-1, LANES))
            for p in range(2)
        ],
        axis=1,
    )
    lines[...] = mm(beside(split2(residual), 1), against(inverse, 0))
    back = []
    for q in range(radix):
        part = tuple(
            lines[q * count : (q + 1) * count, p * LANES : (p + 1) * LANES] for p in range(2)
        )
        if q:
            part = turn(part, table[0, q : q + 1, :], table[1, q : q + 1, :], 1)
        back.append(part)
    for spot, (re, im) in zip(spots, small_dft(back, 1)):
        out[spot, 0] = re
        out[spot, 1] = im


def rows_both_ways(place, data, kept, target, scales, first_line):
    radix, _, count, _ = data.shape
    pencil = kept.shape[1]
    c, s = fourier_parts(LANES, 1.0 / math.sqrt(radix * LANES))
    forward = halves(np.block([[c, -s], [s, c]]))
    inverse = halves(np.block([[c, s], [-s, c]]))
    table = turn_table(radix, LANES)
    block = max(b for b in range(8, 56, 8) if pencil % b == 0)
    offset, repeat = first_line // block, pencil // block
    vmem = pl.BlockSpec(memory_space=pltpu.VMEM)
    spec = pl.BlockSpec((radix, 2, block, LANES), lambda i: (0, 0, i, 0))
    return pl.pallas_call(
        rows_kernel,
        out_shape=jax.ShapeDtypeStruct(data.shape, F32),
        grid=(count // block,),
        in_specs=[
            pl.BlockSpec(memory_space=pltpu.SMEM),
            spec,
            pl.BlockSpec((radix, block, LANES), lambda i: (0, lax.rem(i + offset, repeat), 0)),
            pl.BlockSpec((2, radix, block, LANES), lambda i: (0, 0, i + offset, 0)),
            vmem,
            vmem,
            vmem,
            vmem,
        ],
        out_specs=spec,
        scratch_shapes=[pltpu.VMEM((radix * block, 2 * LANES), F32)],
        cost_estimate=pl.CostEstimate(
            flops=24 * radix * count * LANES * LANES,
            bytes_accessed=32 * radix * count * LANES,
            transcendentals=0,
        ),
        compiler_params=pltpu.CompilerParams(vmem_limit_bytes=12 * MIB),
        name="rows_both_ways",
    )(place, data, kept, target, scales, jnp.asarray(forward), jnp.asarray(inverse), jnp.asarray(table))


def columns_inverse_kernel(last, first, data, maps, scales, matrix, table, *refs):
    radix, inner = table.shape[1:]
    groups = data.shape[0]
    coils, _, rows, cols = maps.shape
    base, outs = (None, refs) if len(refs) == 1 else (refs[0], refs[1:])
    parts = []
    for q in range(radix):
        lines = jnp.concatenate(
            [
                jnp.transpose(
                    jnp.concatenate(
                        [
                            data[lax.bitwise_xor(g, first[1]), p, c, q]
                            for p in range(2)
                            for g in range(groups)
                        ], axis=0
                    )
                )
                for c in range(coils)
            ],
            axis=0,
        )
        result = mm(beside(split2(lines), 1), against(matrix, 0))
        part = (result[:, :inner], result[:, inner:])
        if q:
            part = turn(part, table[0, q : q + 1, :], table[1, q : q + 1, :], 1)
        parts.append(part)
    sums = [[], []]
    for a, (re, im) in enumerate(small_dft(parts, 1)):
        where = slice(a * inner, (a + 1) * inner)
        total = [0.0, 0.0]
        for c in range(coils):
            maps_real, maps_imag = maps[c, 0, :, where], maps[c, 1, :, where]
            x, y = re[c * rows : (c + 1) * rows], im[c * rows : (c + 1) * rows]
            total[0] += maps_real * x + maps_imag * y
            total[1] += maps_real * y - maps_imag * x
        for p in range(2):
            part = total[p] * scales[3:4, 0:1]
            sums[p].append(part if base is None else base[p, :, where] + part)
    lead = first[0] != 0
    for p in range(2):
        line = jnp.concatenate(sums[p], axis=1)
        if last:
            own, away = line[:, : cols // 2], line[:, cols // 2 :]
            outs[0][p] = jnp.where(lead, own, away)
            outs[1][p] = jnp.where(lead, away, own)
        else:
            outs[0][p] = line


def columns_inverse(first, data, maps, scales, chunk, chunks, base):
    groups, _, coils, radix, per, rows = data.shape
    cols = maps.shape[3]
    inner = cols // radix
    c, s = fourier_parts(inner, 1.0 / math.sqrt(cols))
    matrix = halves(np.block([[c, s], [-s, c]]))
    table = turn_table(radix, inner)
    vmem = pl.BlockSpec(memory_space=pltpu.VMEM)
    last = chunk == chunks - 1
    if last:
        shape = [jax.ShapeDtypeStruct((2, rows, cols // 2), F32)] * 2
    else:
        shape = [jax.ShapeDtypeStruct((2, rows, cols), F32)]
    return pl.pallas_call(
        partial(columns_inverse_kernel, last),
        out_shape=shape,
        grid=(1,),
        in_specs=[
            pl.BlockSpec(memory_space=pltpu.SMEM),
            vmem,
            pl.BlockSpec((coils, 2, rows, cols), lambda i: (chunk, 0, 0, 0)),
            vmem,
            vmem,
            vmem,
        ]
        + [vmem] * len(base),
        out_specs=[vmem] * len(shape),
        cost_estimate=pl.CostEstimate(
            flops=24 * coils * rows * cols * inner,
            bytes_accessed=16 * coils * rows * cols,
            transcendentals=0,
        ),
        compiler_params=pltpu.CompilerParams(vmem_limit_bytes=20 * MIB),
        name="columns_inverse",
    )(first, data, maps, scales, jnp.asarray(matrix), jnp.asarray(table), *base)


def target_kernel(radix3, token, *refs):
    tiles = (len(refs) - 4) // 2
    measured, sampled = refs[:tiles], refs[tiles : 2 * tiles]
    target, kept, lines, order = refs[2 * tiles :]
    radix, pencil, _ = kept.shape
    count, height = lines.shape
    coils = count // pencil
    per = pencil // radix3

    @pl.when(pl.program_id(0) == 0)
    def _():
        source = lax.broadcasted_iota(jnp.int32, (height, LANES), 0)
        place = lax.broadcasted_iota(jnp.int32, (height, LANES), 1)
        for q in range(radix):
            order[:, q * LANES : (q + 1) * LANES] = jnp.where(
                source == radix * place + q, 1.0, 0.0
            ).astype(BF16)
        for t in range(tiles):
            for q in range(radix3):
                lines[q * per : (q + 1) * per, t * LANES : (t + 1) * LANES] = sampled[t][
                    pl.ds(q, per, stride=radix3), :
                ].astype(F32)
        picked = mm(lines[0:pencil, :].astype(BF16), order[...])
        for q in range(radix):
            kept[q] = picked[:, q * LANES : (q + 1) * LANES]

    for t in range(tiles):
        source = measured[t].reshape(count, LANES)
        for c in range(coils):
            for q in range(radix3):
                start = c * pencil + q * per
                lines[start : start + per, t * LANES : (t + 1) * LANES] = source[
                    pl.ds(q * coils + c, per, stride=radix3 * coils), :
                ]
    high, low = split2(lines[...])
    for q in range(0, radix, 2):
        width = min(2, radix - q) * LANES
        part = order[:, q * LANES : q * LANES + width]
        picked = mm(high, part) + mm(low, part)
        for k in range(0, width, LANES):
            target[0, q + k // LANES] = picked[:, k : k + LANES]


def prepare_target(token, measured, sampled, radix3):
    _, pencil, coils, height = measured.shape
    radix = height // LANES
    count = pencil * coils
    return pl.pallas_call(
        partial(target_kernel, radix3),
        out_shape=(
            jax.ShapeDtypeStruct((2, radix, count, LANES), F32),
            jax.ShapeDtypeStruct((radix, pencil, LANES), F32),
        ),
        grid=(2,),
        in_specs=[pl.BlockSpec(memory_space=pltpu.SMEM)]
        + [
            pl.BlockSpec((1, pencil, coils, LANES), lambda i, t=t: (i, 0, 0, t))
            for t in range(radix)
        ]
        + [pl.BlockSpec((pencil, LANES), lambda i, t=t: (0, t)) for t in range(radix)],
        out_specs=(
            pl.BlockSpec((1, radix, count, LANES), lambda i: (i, 0, 0, 0)),
            pl.BlockSpec((radix, pencil, LANES), lambda i: (0, 0, 0)),
        ),
        scratch_shapes=[pltpu.VMEM((count, height), F32), pltpu.VMEM((height, height), BF16)],
        cost_estimate=pl.CostEstimate(
            flops=8 * count * height * height, bytes_accessed=16 * count * height, transcendentals=0
        ),
        compiler_params=pltpu.CompilerParams(vmem_limit_bytes=20 * MIB),
        name="target",
    )(token, *[measured] * radix, *[sampled] * radix)


def pairwise(groups):
    return groups <= 8 and groups & (groups - 1) == 0


def send(value):
    groups = value.shape[0]
    if not pairwise(groups):
        value = value.astype(jnp.float16)
        return [lax.all_to_all(value, "gz", split_axis=0, concat_axis=0, tiled=True)]
    return [value[0]] + [
        lax.ppermute(value[k].astype(jnp.float16), "gz", [(i, i ^ k) for i in range(groups)])
        for k in range(1, groups)
    ]


def receive(parts):
    if len(parts) == 1:
        return parts[0].astype(F32)
    return jnp.stack([part.astype(F32) for part in parts])


def after(value, *earlier):
    return lax.optimization_barrier((value, *earlier))[0]


def local(
    noisy_image, fresh_noise, coil_maps, measured, sampled, first_kernel, inner_kernels, last_kernel
):
    groups = lax.axis_size("gz")
    coils, _, rows, cols = coil_maps.shape
    height = measured.shape[3]
    radix, inner = cols // INNER, INNER
    per = inner // groups
    row_radix = height // LANES
    chunks = 2
    pencil = radix * per
    count = coils * pencil // chunks
    place = lax.axis_index("gz") if pairwise(groups) else 0
    lead = jnp.stack([lax.axis_index("col") == 0, place]).astype(jnp.int32)

    weights, scales = network_weights(
        first_kernel, inner_kernels[0], last_kernel, cols, height
    )
    top, bottom, side = halo(noisy_image)
    predicted, clean = run_network(noisy_image, top, bottom, side, edge_flags(), weights)
    other = swap_cores(clean)

    token = lead
    arrived = []
    for chunk in range(chunks):
        spectra = columns_forward(token, clean, other, coil_maps, scales, groups, chunk, chunks)
        spectra = send(spectra.reshape(groups, 2, count, rows))
        if chunk == 0:
            target, kept = prepare_target(after(lead, spectra[0]), measured, sampled, radix)
            token = after(lead, kept)
        arrived.append(spectra)

    back = []
    for chunk in range(chunks):
        lines = receive(after(arrived[chunk], *back[-1:]))
        if rows != LANES:
            lines = jnp.transpose(lines, (1, 2, 0, 3)).reshape(2, -1, row_radix, LANES)
            lines = jnp.transpose(lines, (2, 0, 1, 3))
        lines = rows_both_ways(lead, lines, kept, target, scales, chunk * (coils // chunks) * pencil)
        if rows != LANES:
            lines = jnp.transpose(lines, (1, 2, 0, 3)).reshape(2, -1, groups, rows)
            lines = jnp.transpose(lines, (2, 0, 1, 3))
        back.append(send(lines))

    gradient = []
    for chunk in range(chunks):
        lines = receive(after(back[chunk], *gradient))
        lines = lines.reshape(groups, 2, coils // chunks, radix, per, rows)
        gradient = columns_inverse(lead, lines, coil_maps, scales, chunk, chunks, gradient)

    own, away = gradient
    own = own + swap_cores(away)
    update = clean - STEP_GAIN * own
    return SCALE_NEXT * update + DIRECT_GAIN * predicted + NOISE_GAIN * fresh_noise


def solution(mesh):
    in_specs = (
        P("grp", "gz", "col"),
        P("grp", "gz", "col"),
        P("col", "grp", "gz", None),
        P("grp", "gz", "col", None),
        P("gz", "grp"),
        P(),
        P(),
        P(),
    )
    out_specs = P("grp", "gz", "col")
    return jax.shard_map(local, mesh=mesh, in_specs=in_specs, out_specs=out_specs, check_vma=False)
```

```python
import math
from functools import partial

import jax
import jax.numpy as jnp
import ml_dtypes
import numpy as np
from jax import lax
from jax.experimental import pallas as pl
from jax.experimental.pallas import tpu as pltpu
from jax.sharding import PartitionSpec as P

SCALE_NOW = 0.8
SIGMA_NOW = 0.6
STEP_GAIN = 1.0
SCALE_NEXT = 0.9
DIRECT_GAIN = 0.31622776601683794
NOISE_GAIN = 0.3

NOISY_MAX = 6.0
MAPS_MAX = 1.5
MEASURED_MAX = 2.4

F32 = jnp.float32
BF16 = jnp.bfloat16
LANES = 128
EDGE = 8
MIB = 1024 * 1024
INNER = 256


def ceil_to(value, step):
    return -(-value // step) * step


def tap_choice(rows, cols):
    choice = np.zeros(rows.shape + (9,), np.float32)
    for index in np.ndindex(rows.shape):
        a, b = rows[index], cols[index]
        if 0 <= a < 3 and 0 <= b < 3:
            choice[index + (3 * a + b,)] = 1.0
    return choice


def tap_choices():
    pair = np.eye(2, dtype=np.float32)
    first, last = [], []
    for c, r in np.ndindex(2, 2):
        s, d, x = np.meshgrid(*map(np.arange, (4, 4, 16)), indexing="ij")
        chosen = tap_choice(x - 5 - 2 * s - r, d - c)
        first.append(np.einsum("sdxt,hk->shdxtk", chosen, pair).reshape(512, 18))
        dr, dc = np.meshgrid(np.arange(4), np.arange(4), indexing="ij")
        chosen = tap_choice(r - dr + 2, c - dc + 2)
        last.append(np.einsum("yxt,hk->yxhtk", chosen, pair).reshape(32, 18))
    middle = []
    for cols, rows in (((0, 1), (0, 1)), ((-1, 2), (0, 1)), ((0, 1), (2, -1)), ((-1, 2), (2, -1))):
        for gamma in cols:
            for rho in rows:
                taps = []
                for c, r in np.ndindex(2, 2):
                    a, b = rho - r + 1, gamma - c + 1
                    taps.append(3 * a + b if 0 <= a < 3 and 0 <= b < 3 else None)
                middle.append(taps)
    return np.stack(first), middle, np.stack(last)


def weights_kernel(cols, height, first_taps, k2, last_taps, choice1, choice3, first, inner, last, scales):
    _, middle, _ = tap_choices()
    ch = k2.shape[1]
    k1 = jnp.concatenate([first_taps[t].astype(F32) for t in range(9)], axis=0).astype(BF16)
    k3 = jnp.concatenate([last_taps[t].astype(F32) for t in range(9)], axis=0).astype(BF16)
    parts = [mm(choice1[i], k1) for i in range(4)]
    first[...] = (0.5 * jnp.concatenate(parts, axis=1)).astype(BF16).reshape(first.shape)
    turned = [(0.5 * jnp.transpose(k2[t].astype(F32))).astype(BF16) for t in range(9)]
    zero = jnp.zeros((ch, ch), BF16)
    for p, taps in enumerate(middle):
        row = [zero if t is None else turned[t] for t in taps]
        inner[p * ch : (p + 1) * ch, :] = jnp.concatenate(row, axis=1)
    parts = [mm(choice3[i], k3) for i in range(4)]
    last[...] = jnp.concatenate(parts, axis=1).astype(BF16)

    def top(value, axes):
        for axis in axes:
            value = jnp.max(value, axis=axis, keepdims=True)
        return value

    gain1 = top(jnp.sum(jnp.abs(k1.astype(F32)), axis=0, keepdims=True), (1,))
    gain2 = sum(jnp.abs(k2[t].astype(F32)) for t in range(9))
    gain2 = top(jnp.sum(gain2, axis=1, keepdims=True), (0,))
    gain3 = jnp.sum(jnp.abs(k3.astype(F32)), axis=1, keepdims=True)
    odd = lax.rem(lax.broadcasted_iota(jnp.int32, gain3.shape, 0), 2) == 1
    gain3 = jnp.maximum(
        jnp.sum(jnp.where(odd, gain3, 0.0), axis=0, keepdims=True),
        jnp.sum(jnp.where(odd, 0.0, gain3), axis=0, keepdims=True),
    )
    predicted = 1.1 * NOISY_MAX * gain1 * gain2 * gain3
    clean = (NOISY_MAX + SIGMA_NOW * predicted) / SCALE_NOW
    spectra = 1.1 * math.sqrt(cols) * 2.0 * MAPS_MAX * clean
    lines = 1.1 * math.sqrt(height) * (spectra + math.sqrt(2.0) * MEASURED_MAX)
    rows = []
    for bound in (spectra, lines):
        rows += [60000.0 / bound, bound / 60000.0]
    scales[...] = jnp.concatenate([jnp.broadcast_to(r, (1, LANES)) for r in rows + rows], axis=0)


def network_weights(first_kernel, inner_kernel, last_kernel, cols, height):
    ch = inner_kernel.shape[1]
    choice1, _, choice3 = tap_choices()
    shapes = ((4, 128, 4 * ch), (16 * ch, 4 * ch), (32, 4 * ch))
    first, inner, last, scales = pl.pallas_call(
        partial(weights_kernel, cols, height),
        out_shape=[jax.ShapeDtypeStruct(d, BF16) for d in shapes]
        + [jax.ShapeDtypeStruct((8, LANES), F32)],
        cost_estimate=pl.CostEstimate(flops=10**7, bytes_accessed=10**6, transcendentals=0),
        compiler_params=pltpu.CompilerParams(vmem_limit_bytes=10 * MIB),
        name="weights",
    )(
        jnp.transpose(first_kernel, (0, 2, 1)),
        inner_kernel,
        last_kernel,
        jnp.asarray(choice1, BF16),
        jnp.asarray(choice3, BF16),
    )
    return (first, inner, last), scales


def split3(value):
    high = value.astype(BF16)
    rest = value - high.astype(F32)
    middle = rest.astype(BF16)
    return high, middle, (rest - middle.astype(F32)).astype(BF16)


def split2(value):
    high = value.astype(BF16)
    return high, (value - high.astype(F32)).astype(BF16)


def mm(lhs, rhs):
    return lax.dot_general(lhs, rhs, (((1,), (0,)), ((), ())), preferred_element_type=F32)


def mm_nt(lhs, rhs):
    return lax.dot_general(lhs, rhs, (((1,), (1,)), ((), ())), preferred_element_type=F32)


def network_kernel(
    flags, top, center, bottom, side, first, inner, last, pred, clean, tile, q, hid, hid_side, done, acc
):
    rows, cols = center.shape[1:]
    blocks = rows // 2 + 2
    groups = q.shape[1] // 8 - 1
    used = hid.shape[1]
    step = done.shape[0] // used

    for ch in range(2):
        tile[ch, 0:8, :] = top[ch, :, 0:cols]
        tile[ch, 8 : 8 + rows, :] = center[ch]
        tile[ch, 8 + rows : 16 + rows, :] = bottom[ch, :, 0:cols]
    edge = jnp.concatenate(
        [
            part
            for ch in range(2)
            for part in (top[ch, :, cols:], side[ch], bottom[ch, :, cols:])
        ],
        axis=0,
    ).astype(BF16)
    w = lax.broadcasted_iota(jnp.int32, (cols, 256), 0)
    k = lax.broadcasted_iota(jnp.int32, (cols, 256), 1)
    e = lax.broadcasted_iota(jnp.int32, (EDGE, 256), 0) + jnp.where(flags[2] != 0, cols, -EDGE)
    ke = lax.broadcasted_iota(jnp.int32, (EDGE, 256), 1)
    for d in range(4):
        sel = jnp.where(w == 2 * k - 3 + d, 1.0, 0.0).astype(BF16)
        sel_side = jnp.where(e == 2 * ke - 3 + d, 1.0, 0.0).astype(BF16)
        both = mm(tile[...].reshape(-1, cols).astype(BF16), sel)
        both += mm(edge, sel_side)
        for ch in range(2):
            q[4 * ch + d] = both[ch * (rows + 16) : (ch + 1) * (rows + 16)]

    end = cols // 2 + 1
    tail = end // 8 * 8
    lines = lax.broadcasted_iota(jnp.int32, (8, 256), 0)
    low = jnp.where((lines == 0) & (flags[2] != 0), 0.0, 1.0)
    high = jnp.where((lines == end - tail) & (flags[3] != 0), 0.0, 1.0)

    def silu_rows(half):
        h = half + half * jnp.tanh(half)
        pieces = []
        for start in range(0, h.shape[0], used):
            pieces += [
                h[start : start + 8] * low,
                h[start + 8 : start + tail],
                h[start + tail : start + tail + 8] * high,
            ]
            if tail + 8 < used:
                pieces.append(h[start + tail + 8 : start + used])
        return jnp.concatenate(pieces, axis=0)

    acc[...] = jnp.zeros(acc.shape, F32)
    hid[0] = jnp.zeros(hid.shape[1:], BF16)
    hid_side[0] = jnp.zeros(hid.shape[1:], BF16)

    def first_layer(t, carry):
        window = q[:, pl.ds(pl.multiple_of(8 * t, 8), 16), :].reshape(128, 256)
        window = jnp.transpose(window)[:used].astype(BF16)
        for s in range(4):
            h = silu_rows(mm(window, first[s]))
            place = 4 * t + s + 1
            hid[place] = h.astype(BF16)
            hid_side[place, :, 0:128] = pltpu.roll(h[:, 128:256], 1, 0).astype(BF16)
            hid_side[place, :, 128:256] = pltpu.roll(h[:, 0:128], used - 1, 0).astype(BF16)
        return carry

    lax.fori_loop(0, groups, first_layer, 0)

    for flag, j in ((0, 0), (1, blocks - 1)):

        @pl.when(flags[flag] != 0)
        def _(j=j):
            hid[j + 1] = jnp.zeros(hid.shape[1:], BF16)
            hid_side[j + 1] = jnp.zeros(hid_side.shape[1:], BF16)

    lane = lax.broadcasted_iota(jnp.int32, (step * used, 256), 1)
    below = lax.rem(lane, 128) < 64

    def next_layers(i, carry):
        j = step * i

        def around(ref, offset):
            return ref[pl.ds(j + offset, step)].reshape(step * used, 256)

        lhs = jnp.concatenate(
            [
                around(hid, 1),
                around(hid_side, 1),
                jnp.where(below, around(hid, 2), around(hid, 0)),
                jnp.where(below, around(hid_side, 2), around(hid_side, 0)),
            ],
            axis=1,
        )
        add_parts(j - step)
        done[...] = silu_rows(mm(lhs, inner[...])).astype(BF16)
        return carry

    def add_parts(j):
        for u in range(step):
            part = mm_nt(last[...], done[u * used : (u + 1) * used])
            row = j + u
            gone = ((row == 0) & (flags[0] != 0)) | ((row == blocks - 1) & (flags[1] != 0))
            part = part * jnp.where(gone, 0.0, 1.0)
            where = pl.ds(pl.multiple_of(16 * (row + step), 16), 32)
            for c in range(0, used, 128):
                width = min(128, used - c)
                acc[c // 128, where, 0:width] = acc[c // 128, where, 0:width] + part[:, c : c + width]

    done[...] = jnp.zeros(done.shape, BF16)
    lax.fori_loop(0, blocks // step, next_layers, 0)
    add_parts(blocks - step)

    def pixels(d):
        return jnp.concatenate(
            [
                jnp.concatenate(
                    [
                        acc[c, pl.ds(24 + 16 * step + 2 * d + ch, rows, stride=8), :]
                        for c in range(2)
                    ],
                    axis=1,
                )
                for ch in range(2)
            ],
            axis=0,
        )

    k = lax.broadcasted_iota(jnp.int32, (256, cols), 0)
    w = lax.broadcasted_iota(jnp.int32, (256, cols), 1)
    total = 0.0
    for d, other, shift in ((1, 3, 1), (2, 0, 255)):
        line = pixels(d) + pltpu.roll(pixels(other), shift, 1)
        sel = jnp.where(w == 2 * k - 3 + d, 1.0, 0.0).astype(BF16)
        both = mm(jnp.concatenate(split2(line), axis=0), sel)
        total += both[: 2 * rows] + both[2 * rows :]
    for ch in range(2):
        part = total[ch * rows : (ch + 1) * rows]
        pred[ch] = part
        clean[ch] = (center[ch] - SIGMA_NOW * part) / SCALE_NOW


def run_network(noisy, top, bottom, side, flags, weights):
    _, rows, cols = noisy.shape
    blocks = rows // 2 + 2
    groups = -(-blocks // 4)
    used = ceil_to(cols // 2 + 2, 16)
    step = max(u for u in (1, 2, 3, 6) if blocks % u == 0)
    vmem = pl.BlockSpec(memory_space=pltpu.VMEM)
    shape = jax.ShapeDtypeStruct(noisy.shape, F32)
    return pl.pallas_call(
        network_kernel,
        out_shape=(shape, shape),
        in_specs=[pl.BlockSpec(memory_space=pltpu.SMEM)] + [vmem] * 7,
        out_specs=(vmem, vmem),
        scratch_shapes=[
            pltpu.VMEM((2, rows + 16, cols), F32),
            pltpu.VMEM((8, 8 * groups + 8, 256), F32),
            pltpu.VMEM((4 * groups + 1, used, 256), BF16),
            pltpu.VMEM((4 * groups + 1, used, 256), BF16),
            pltpu.VMEM((step * used, 256), BF16),
            pltpu.VMEM((2, 16 * (blocks + step) + 16, 128), F32),
        ],
        cost_estimate=pl.CostEstimate(
            flops=20 * rows * cols * 64 * 64, bytes_accessed=24 * rows * cols, transcendentals=0
        ),
        compiler_params=pltpu.CompilerParams(vmem_limit_bytes=40 * MIB),
        name="network",
    )(flags, top, noisy, bottom, side, *weights)


def halo(noisy):
    gz = lax.axis_size("gz")
    _, rows, cols = noisy.shape
    left, right = noisy[:, :, :EDGE], noisy[:, :, cols - EDGE :]
    side = swap_cores(jnp.where(lax.axis_index("col") == 0, right, left))
    down = [(i, i + 1) for i in range(gz - 1)]
    lower = jnp.concatenate([noisy[:, rows - EDGE :], side[:, rows - EDGE :]], axis=2)
    upper = jnp.concatenate([noisy[:, :EDGE], side[:, :EDGE]], axis=2)
    top = lax.ppermute(lower, "gz", down)
    bottom = lax.ppermute(upper, "gz", [(b, a) for a, b in down])
    return top, bottom, side


def swap_cores(value):
    assert lax.axis_size("col") == 2
    return lax.ppermute(value, "col", [(0, 1), (1, 0)])


def edge_flags():
    row, col = lax.axis_index("gz"), lax.axis_index("col")
    last_row, last_col = lax.axis_size("gz") - 1, lax.axis_size("col") - 1
    return jnp.stack([row == 0, row == last_row, col == 0, col == last_col]).astype(jnp.int32)


def halves(matrix):
    high = matrix.astype(ml_dtypes.bfloat16)
    low = (matrix - high.astype(np.float64)).astype(ml_dtypes.bfloat16)
    return np.stack([high, low])


def fourier_parts(length, scale):
    index = np.arange(length)
    angle = 2.0 * np.pi * (np.outer(index, index) % length) / length
    return np.cos(angle) * scale, np.sin(angle) * scale


def turn_table(radix, inner):
    angle = 2.0 * np.pi * np.outer(np.arange(radix), np.arange(inner)) / (radix * inner)
    return np.stack([np.cos(angle), np.sin(angle)]).astype(np.float32)


def small_dft(values, sign):
    n = len(values)
    if n == 1:
        return values
    if n % 2 == 0:
        even = small_dft(values[0::2], sign)
        odd = small_dft(values[1::2], sign)
        low, high = [], []
        for q in range(n // 2):
            re, im = times_unit(odd[q], q, n, sign)
            low.append((even[q][0] + re, even[q][1] + im))
            high.append((even[q][0] - re, even[q][1] - im))
        return low + high
    if n == 3:
        (r0, i0), (r1, i1), (r2, i2) = values
        sr, si = r1 + r2, i1 + i2
        half = math.sqrt(3.0) / 2.0 * sign
        dr, di = half * (r1 - r2), half * (i1 - i2)
        tr, ti = r0 - 0.5 * sr, i0 - 0.5 * si
        return [(r0 + sr, i0 + si), (tr - di, ti + dr), (tr + di, ti - dr)]
    out = []
    for q in range(n):
        terms = [times_unit(v, a * q, n, sign) for a, v in enumerate(values)]
        out.append((sum(t[0] for t in terms), sum(t[1] for t in terms)))
    return out


def times_unit(value, power, n, sign):
    re, im = value
    power %= n
    if power == 0:
        return re, im
    if 4 * power == n:
        return (-im, re) if sign > 0 else (im, -re)
    if 2 * power == n:
        return -re, -im
    if 4 * power == 3 * n:
        return (im, -re) if sign > 0 else (-im, re)
    c = math.cos(2.0 * math.pi * power / n)
    s = sign * math.sin(2.0 * math.pi * power / n)
    return c * re - s * im, c * im + s * re


def turn(value, cos, sin, sign):
    re, im = value
    if sign > 0:
        return re * cos - im * sin, im * cos + re * sin
    return re * cos + im * sin, im * cos - re * sin


def beside(parts, axis):
    return jnp.concatenate([parts[0], parts[0], parts[1]], axis=axis)


def against(matrix, axis):
    return jnp.concatenate([matrix[0], matrix[1], matrix[0]], axis=axis)


def columns_forward_kernel(first, mine, other, maps, scales, matrix, table, out):
    radix, inner = table.shape[1:]
    coils = maps.shape[0]
    rows, cols = mine.shape[1:]
    groups = out.shape[0]
    per = inner // groups
    lead, me = first[0] != 0, first[1]
    image = [
        jnp.concatenate(
            [jnp.where(lead, mine[p], other[p]), jnp.where(lead, other[p], mine[p])], axis=1
        )
        * scales[0:1, 0:1]
        for p in range(2)
    ]
    turned = []
    for coil in range(coils):
        maps_real, maps_imag = maps[coil, 0], maps[coil, 1]
        coil_image = (
            maps_real * image[0] - maps_imag * image[1],
            maps_real * image[1] + maps_imag * image[0],
        )
        parts = [
            tuple(v[:, a * inner : (a + 1) * inner] for v in coil_image) for a in range(radix)
        ]
        parts = small_dft(parts, -1)
        turned.append(
            [
                turn(part, table[0, q : q + 1, :], table[1, q : q + 1, :], -1) if q else part
                for q, part in enumerate(parts)
            ]
        )
    for q in range(radix):
        data = jnp.concatenate([jnp.concatenate(turned[c][q], axis=1) for c in range(coils)], axis=0)
        result = mm_nt(against(matrix, 1), beside(split2(data), 1))
        for p in range(2):
            for g in range(groups):
                start = p * inner + g * per
                for c in range(coils):
                    out[lax.bitwise_xor(g, me), p, c, q] = result[start : start + per, c * rows : (c + 1) * rows]


def columns_forward(first, mine, other, maps, scales, groups, chunk, chunks):
    coils, _, rows, cols = maps.shape
    coils //= chunks
    inner = INNER
    radix = cols // inner
    c, s = fourier_parts(inner, 1.0 / math.sqrt(cols))
    matrix = halves(np.block([[c, s], [-s, c]]))
    table = turn_table(radix, inner)
    vmem = pl.BlockSpec(memory_space=pltpu.VMEM)
    per = inner // groups
    return pl.pallas_call(
        columns_forward_kernel,
        out_shape=jax.ShapeDtypeStruct((groups, 2, coils, radix, per, rows), F32),
        grid=(1,),
        in_specs=[
            pl.BlockSpec(memory_space=pltpu.SMEM),
            vmem,
            vmem,
            pl.BlockSpec((coils, 2, rows, cols), lambda i: (chunk, 0, 0, 0)),
            vmem,
            vmem,
            vmem,
        ],
        out_specs=pl.BlockSpec(
            (groups, 2, coils, radix, per, rows), lambda i: (0, 0, 0, 0, 0, 0)
        ),
        cost_estimate=pl.CostEstimate(
            flops=24 * coils * rows * cols * inner,
            bytes_accessed=16 * coils * rows * cols,
            transcendentals=0,
        ),
        compiler_params=pltpu.CompilerParams(vmem_limit_bytes=20 * MIB),
        name="columns_forward",
    )(first, mine, other, maps, scales, jnp.asarray(matrix), jnp.asarray(table))


def rows_kernel(place, data, kept, target, scales, forward, inverse, table, out, lines):
    radix = table.shape[1]
    count = data.shape[2]
    spots = [lax.bitwise_xor(a, place[1]) for a in range(radix)]
    parts = small_dft([(data[spot, 0], data[spot, 1]) for spot in spots], -1)
    for q, part in enumerate(parts):
        if q:
            part = turn(part, table[0, q : q + 1, :], table[1, q : q + 1, :], -1)
        for p in range(2):
            lines[q * count : (q + 1) * count, p * LANES : (p + 1) * LANES] = part[p]
    spectrum = mm(beside(split2(lines[...]), 1), against(forward, 0))
    keep = kept[...].reshape(radix * count, LANES) * scales[2:3, :]
    unit = scales[1:2, :]
    residual = jnp.concatenate(
        [
            keep
            * (spectrum[:, p * LANES : (p + 1) * LANES] * unit - target[p].reshape(-1, LANES))
            for p in range(2)
        ],
        axis=1,
    )
    lines[...] = mm(beside(split2(residual), 1), against(inverse, 0))
    back = []
    for q in range(radix):
        part = tuple(
            lines[q * count : (q + 1) * count, p * LANES : (p + 1) * LANES] for p in range(2)
        )
        if q:
            part = turn(part, table[0, q : q + 1, :], table[1, q : q + 1, :], 1)
        back.append(part)
    for spot, (re, im) in zip(spots, small_dft(back, 1)):
        out[spot, 0] = re
        out[spot, 1] = im


def rows_both_ways(place, data, kept, target, scales, first_line):
    radix, _, count, _ = data.shape
    pencil = kept.shape[1]
    c, s = fourier_parts(LANES, 1.0 / math.sqrt(radix * LANES))
    forward = halves(np.block([[c, -s], [s, c]]))
    inverse = halves(np.block([[c, s], [-s, c]]))
    table = turn_table(radix, LANES)
    block = max(b for b in range(8, 56, 8) if pencil % b == 0)
    offset, repeat = first_line // block, pencil // block
    vmem = pl.BlockSpec(memory_space=pltpu.VMEM)
    spec = pl.BlockSpec((radix, 2, block, LANES), lambda i: (0, 0, i, 0))
    return pl.pallas_call(
        rows_kernel,
        out_shape=jax.ShapeDtypeStruct(data.shape, F32),
        grid=(count // block,),
        in_specs=[
            pl.BlockSpec(memory_space=pltpu.SMEM),
            spec,
            pl.BlockSpec((radix, block, LANES), lambda i: (0, lax.rem(i + offset, repeat), 0)),
            pl.BlockSpec((2, radix, block, LANES), lambda i: (0, 0, i + offset, 0)),
            vmem,
            vmem,
            vmem,
            vmem,
        ],
        out_specs=spec,
        scratch_shapes=[pltpu.VMEM((radix * block, 2 * LANES), F32)],
        cost_estimate=pl.CostEstimate(
            flops=24 * radix * count * LANES * LANES,
            bytes_accessed=32 * radix * count * LANES,
            transcendentals=0,
        ),
        compiler_params=pltpu.CompilerParams(vmem_limit_bytes=12 * MIB),
        name="rows_both_ways",
    )(place, data, kept, target, scales, jnp.asarray(forward), jnp.asarray(inverse), jnp.asarray(table))


def columns_inverse_kernel(last, first, data, maps, scales, matrix, table, *refs):
    radix, inner = table.shape[1:]
    groups = data.shape[0]
    coils, _, rows, cols = maps.shape
    base, outs = (None, refs) if len(refs) == 1 else (refs[0], refs[1:])
    parts = []
    for q in range(radix):
        lines = jnp.concatenate(
            [
                jnp.transpose(
                    jnp.concatenate(
                        [
                            data[lax.bitwise_xor(g, first[1]), p, c, q]
                            for p in range(2)
                            for g in range(groups)
                        ], axis=0
                    )
                )
                for c in range(coils)
            ],
            axis=0,
        )
        result = mm(beside(split2(lines), 1), against(matrix, 0))
        part = (result[:, :inner], result[:, inner:])
        if q:
            part = turn(part, table[0, q : q + 1, :], table[1, q : q + 1, :], 1)
        parts.append(part)
    sums = [[], []]
    for a, (re, im) in enumerate(small_dft(parts, 1)):
        where = slice(a * inner, (a + 1) * inner)
        total = [0.0, 0.0]
        for c in range(coils):
            maps_real, maps_imag = maps[c, 0, :, where], maps[c, 1, :, where]
            x, y = re[c * rows : (c + 1) * rows], im[c * rows : (c + 1) * rows]
            total[0] += maps_real * x + maps_imag * y
            total[1] += maps_real * y - maps_imag * x
        for p in range(2):
            part = total[p] * scales[3:4, 0:1]
            sums[p].append(part if base is None else base[p, :, where] + part)
    lead = first[0] != 0
    for p in range(2):
        line = jnp.concatenate(sums[p], axis=1)
        if last:
            own, away = line[:, : cols // 2], line[:, cols // 2 :]
            outs[0][p] = jnp.where(lead, own, away)
            outs[1][p] = jnp.where(lead, away, own)
        else:
            outs[0][p] = line


def columns_inverse(first, data, maps, scales, chunk, chunks, base):
    groups, _, coils, radix, per, rows = data.shape
    cols = maps.shape[3]
    inner = cols // radix
    c, s = fourier_parts(inner, 1.0 / math.sqrt(cols))
    matrix = halves(np.block([[c, s], [-s, c]]))
    table = turn_table(radix, inner)
    vmem = pl.BlockSpec(memory_space=pltpu.VMEM)
    last = chunk == chunks - 1
    if last:
        shape = [jax.ShapeDtypeStruct((2, rows, cols // 2), F32)] * 2
    else:
        shape = [jax.ShapeDtypeStruct((2, rows, cols), F32)]
    return pl.pallas_call(
        partial(columns_inverse_kernel, last),
        out_shape=shape,
        grid=(1,),
        in_specs=[
            pl.BlockSpec(memory_space=pltpu.SMEM),
            vmem,
            pl.BlockSpec((coils, 2, rows, cols), lambda i: (chunk, 0, 0, 0)),
            vmem,
            vmem,
            vmem,
        ]
        + [vmem] * len(base),
        out_specs=[vmem] * len(shape),
        cost_estimate=pl.CostEstimate(
            flops=24 * coils * rows * cols * inner,
            bytes_accessed=16 * coils * rows * cols,
            transcendentals=0,
        ),
        compiler_params=pltpu.CompilerParams(vmem_limit_bytes=20 * MIB),
        name="columns_inverse",
    )(first, data, maps, scales, jnp.asarray(matrix), jnp.asarray(table), *base)


def target_kernel(radix3, token, *refs):
    tiles = (len(refs) - 4) // 2
    measured, sampled = refs[:tiles], refs[tiles : 2 * tiles]
    target, kept, lines, order = refs[2 * tiles :]
    radix, pencil, _ = kept.shape
    count, height = lines.shape
    coils = count // pencil
    per = pencil // radix3

    @pl.when(pl.program_id(0) == 0)
    def _():
        source = lax.broadcasted_iota(jnp.int32, (height, LANES), 0)
        place = lax.broadcasted_iota(jnp.int32, (height, LANES), 1)
        for q in range(radix):
            order[:, q * LANES : (q + 1) * LANES] = jnp.where(
                source == radix * place + q, 1.0, 0.0
            ).astype(BF16)
        for t in range(tiles):
            for q in range(radix3):
                lines[q * per : (q + 1) * per, t * LANES : (t + 1) * LANES] = sampled[t][
                    pl.ds(q, per, stride=radix3), :
                ].astype(F32)
        picked = mm(lines[0:pencil, :].astype(BF16), order[...])
        for q in range(radix):
            kept[q] = picked[:, q * LANES : (q + 1) * LANES]

    for t in range(tiles):
        source = measured[t].reshape(count, LANES)
        for c in range(coils):
            for q in range(radix3):
                start = c * pencil + q * per
                lines[start : start + per, t * LANES : (t + 1) * LANES] = source[
                    pl.ds(q * coils + c, per, stride=radix3 * coils), :
                ]
    high, low = split2(lines[...])
    for q in range(0, radix, 2):
        width = min(2, radix - q) * LANES
        part = order[:, q * LANES : q * LANES + width]
        picked = mm(high, part) + mm(low, part)
        for k in range(0, width, LANES):
            target[0, q + k // LANES] = picked[:, k : k + LANES]


def prepare_target(token, measured, sampled, radix3):
    _, pencil, coils, height = measured.shape
    radix = height // LANES
    count = pencil * coils
    return pl.pallas_call(
        partial(target_kernel, radix3),
        out_shape=(
            jax.ShapeDtypeStruct((2, radix, count, LANES), F32),
            jax.ShapeDtypeStruct((radix, pencil, LANES), F32),
        ),
        grid=(2,),
        in_specs=[pl.BlockSpec(memory_space=pltpu.SMEM)]
        + [
            pl.BlockSpec((1, pencil, coils, LANES), lambda i, t=t: (i, 0, 0, t))
            for t in range(radix)
        ]
        + [pl.BlockSpec((pencil, LANES), lambda i, t=t: (0, t)) for t in range(radix)],
        out_specs=(
            pl.BlockSpec((1, radix, count, LANES), lambda i: (i, 0, 0, 0)),
            pl.BlockSpec((radix, pencil, LANES), lambda i: (0, 0, 0)),
        ),
        scratch_shapes=[pltpu.VMEM((count, height), F32), pltpu.VMEM((height, height), BF16)],
        cost_estimate=pl.CostEstimate(
            flops=8 * count * height * height, bytes_accessed=16 * count * height, transcendentals=0
        ),
        compiler_params=pltpu.CompilerParams(vmem_limit_bytes=20 * MIB),
        name="target",
    )(token, *[measured] * radix, *[sampled] * radix)


def pairwise(groups):
    return groups <= 8 and groups & (groups - 1) == 0


def send(value):
    groups = value.shape[0]
    if not pairwise(groups):
        value = value.astype(jnp.float16)
        return [lax.all_to_all(value, "gz", split_axis=0, concat_axis=0, tiled=True)]
    return [value[0]] + [
        lax.ppermute(value[k].astype(jnp.float16), "gz", [(i, i ^ k) for i in range(groups)])
        for k in range(1, groups)
    ]


def receive(parts):
    if len(parts) == 1:
        return parts[0].astype(F32)
    return jnp.stack([part.astype(F32) for part in parts])


def after(value, *earlier):
    return lax.optimization_barrier((value, *earlier))[0]


def local(
    noisy_image, fresh_noise, coil_maps, measured, sampled, first_kernel, inner_kernels, last_kernel
):
    groups = lax.axis_size("gz")
    coils, _, rows, cols = coil_maps.shape
    height = measured.shape[3]
    radix, inner = cols // INNER, INNER
    per = inner // groups
    row_radix = height // LANES
    chunks = 2
    pencil = radix * per
    count = coils * pencil // chunks
    place = lax.axis_index("gz") if pairwise(groups) else 0
    lead = jnp.stack([lax.axis_index("col") == 0, place]).astype(jnp.int32)

    weights, scales = network_weights(
        first_kernel, inner_kernels[0], last_kernel, cols, height
    )
    top, bottom, side = halo(noisy_image)
    predicted, clean = run_network(noisy_image, top, bottom, side, edge_flags(), weights)
    other = swap_cores(clean)

    token = lead
    arrived = []
    for chunk in range(chunks):
        spectra = columns_forward(token, clean, other, coil_maps, scales, groups, chunk, chunks)
        spectra = send(spectra.reshape(groups, 2, count, rows))
        if chunk == 0:
            target, kept = prepare_target(after(lead, spectra[0]), measured, sampled, radix)
            token = after(lead, kept)
        arrived.append(spectra)

    back = []
    for chunk in range(chunks):
        lines = receive(after(arrived[chunk], *back[-1:]))
        if rows != LANES:
            lines = jnp.transpose(lines, (1, 2, 0, 3)).reshape(2, -1, row_radix, LANES)
            lines = jnp.transpose(lines, (2, 0, 1, 3))
        lines = rows_both_ways(lead, lines, kept, target, scales, chunk * (coils // chunks) * pencil)
        if rows != LANES:
            lines = jnp.transpose(lines, (1, 2, 0, 3)).reshape(2, -1, groups, rows)
            lines = jnp.transpose(lines, (2, 0, 1, 3))
        back.append(send(lines))

    gradient = []
    for chunk in range(chunks):
        lines = receive(after(back[chunk], *gradient))
        lines = lines.reshape(groups, 2, coils // chunks, radix, per, rows)
        gradient = columns_inverse(lead, lines, coil_maps, scales, chunk, chunks, gradient)

    own, away = gradient
    own = own + swap_cores(away)
    update = clean - STEP_GAIN * own
    return SCALE_NEXT * update + DIRECT_GAIN * predicted + NOISE_GAIN * fresh_noise


def solution(mesh):
    in_specs = (
        P("grp", "gz", "col"),
        P("grp", "gz", "col"),
        P("col", "grp", "gz", None),
        P("grp", "gz", "col", None),
        P("gz", "grp"),
        P(),
        P(),
        P(),
    )
    out_specs = P("grp", "gz", "col")
    return jax.shard_map(local, mesh=mesh, in_specs=in_specs, out_specs=out_specs, check_vma=False)
```

```python
import math
from functools import partial

import jax
import jax.numpy as jnp
import ml_dtypes
import numpy as np
from jax import lax
from jax.experimental import pallas as pl
from jax.experimental.pallas import tpu as pltpu
from jax.sharding import PartitionSpec as P

SCALE_NOW = 0.8
SIGMA_NOW = 0.6
STEP_GAIN = 1.0
SCALE_NEXT = 0.9
DIRECT_GAIN = 0.31622776601683794
NOISE_GAIN = 0.3

NOISY_MAX = 6.0
MAPS_MAX = 1.5
MEASURED_MAX = 2.4

F32 = jnp.float32
BF16 = jnp.bfloat16
LANES = 128
EDGE = 8
MIB = 1024 * 1024
INNER = 256


def ceil_to(value, step):
    return -(-value // step) * step


def tap_choice(rows, cols):
    choice = np.zeros(rows.shape + (9,), np.float32)
    for index in np.ndindex(rows.shape):
        a, b = rows[index], cols[index]
        if 0 <= a < 3 and 0 <= b < 3:
            choice[index + (3 * a + b,)] = 1.0
    return choice


def tap_choices():
    pair = np.eye(2, dtype=np.float32)
    first, last = [], []
    for c, r in np.ndindex(2, 2):
        s, d, x = np.meshgrid(*map(np.arange, (4, 4, 16)), indexing="ij")
        chosen = tap_choice(x - 5 - 2 * s - r, d - c)
        first.append(np.einsum("sdxt,hk->shdxtk", chosen, pair).reshape(512, 18))
        dr, dc = np.meshgrid(np.arange(4), np.arange(4), indexing="ij")
        chosen = tap_choice(r - dr + 2, c - dc + 2)
        last.append(np.einsum("yxt,hk->yxhtk", chosen, pair).reshape(32, 18))
    middle = []
    for cols, rows in (((0, 1), (0, 1)), ((-1, 2), (0, 1)), ((0, 1), (2, -1)), ((-1, 2), (2, -1))):
        for gamma in cols:
            for rho in rows:
                taps = []
                for c, r in np.ndindex(2, 2):
                    a, b = rho - r + 1, gamma - c + 1
                    taps.append(3 * a + b if 0 <= a < 3 and 0 <= b < 3 else None)
                middle.append(taps)
    return np.stack(first), middle, np.stack(last)


def weights_kernel(cols, height, first_taps, k2, last_taps, choice1, choice3, first, inner, last, scales):
    _, middle, _ = tap_choices()
    ch = k2.shape[1]
    k1 = jnp.concatenate([first_taps[t].astype(F32) for t in range(9)], axis=0).astype(BF16)
    k3 = jnp.concatenate([last_taps[t].astype(F32) for t in range(9)], axis=0).astype(BF16)
    parts = [mm(choice1[i], k1) for i in range(4)]
    first[...] = (0.5 * jnp.concatenate(parts, axis=1)).astype(BF16).reshape(first.shape)
    turned = [(0.5 * jnp.transpose(k2[t].astype(F32))).astype(BF16) for t in range(9)]
    zero = jnp.zeros((ch, ch), BF16)
    for p, taps in enumerate(middle):
        row = [zero if t is None else turned[t] for t in taps]
        inner[p * ch : (p + 1) * ch, :] = jnp.concatenate(row, axis=1)
    parts = [mm(choice3[i], k3) for i in range(4)]
    last[...] = jnp.concatenate(parts, axis=1).astype(BF16)

    def top(value, axes):
        for axis in axes:
            value = jnp.max(value, axis=axis, keepdims=True)
        return value

    gain1 = top(jnp.sum(jnp.abs(k1.astype(F32)), axis=0, keepdims=True), (1,))
    gain2 = sum(jnp.abs(k2[t].astype(F32)) for t in range(9))
    gain2 = top(jnp.sum(gain2, axis=1, keepdims=True), (0,))
    gain3 = jnp.sum(jnp.abs(k3.astype(F32)), axis=1, keepdims=True)
    odd = lax.rem(lax.broadcasted_iota(jnp.int32, gain3.shape, 0), 2) == 1
    gain3 = jnp.maximum(
        jnp.sum(jnp.where(odd, gain3, 0.0), axis=0, keepdims=True),
        jnp.sum(jnp.where(odd, 0.0, gain3), axis=0, keepdims=True),
    )
    predicted = 1.1 * NOISY_MAX * gain1 * gain2 * gain3
    clean = (NOISY_MAX + SIGMA_NOW * predicted) / SCALE_NOW
    spectra = 1.1 * math.sqrt(cols) * 2.0 * MAPS_MAX * clean
    lines = 1.1 * math.sqrt(height) * (spectra + math.sqrt(2.0) * MEASURED_MAX)
    rows = []
    for bound in (spectra, lines):
        rows += [60000.0 / bound, bound / 60000.0]
    scales[...] = jnp.concatenate([jnp.broadcast_to(r, (1, LANES)) for r in rows + rows], axis=0)


def network_weights(first_kernel, inner_kernel, last_kernel, cols, height):
    ch = inner_kernel.shape[1]
    choice1, _, choice3 = tap_choices()
    shapes = ((4, 128, 4 * ch), (16 * ch, 4 * ch), (32, 4 * ch))
    first, inner, last, scales = pl.pallas_call(
        partial(weights_kernel, cols, height),
        out_shape=[jax.ShapeDtypeStruct(d, BF16) for d in shapes]
        + [jax.ShapeDtypeStruct((8, LANES), F32)],
        cost_estimate=pl.CostEstimate(flops=10**7, bytes_accessed=10**6, transcendentals=0),
        compiler_params=pltpu.CompilerParams(vmem_limit_bytes=10 * MIB),
        name="weights",
    )(
        jnp.transpose(first_kernel, (0, 2, 1)),
        inner_kernel,
        last_kernel,
        jnp.asarray(choice1, BF16),
        jnp.asarray(choice3, BF16),
    )
    return (first, inner, last), scales


def split2(value):
    high = value.astype(BF16)
    return high, (value - high.astype(F32)).astype(BF16)


def mm(lhs, rhs):
    return lax.dot_general(lhs, rhs, (((1,), (0,)), ((), ())), preferred_element_type=F32)


def mm_nt(lhs, rhs):
    return lax.dot_general(lhs, rhs, (((1,), (1,)), ((), ())), preferred_element_type=F32)


def network_kernel(
    flags, top, center, bottom, side, first, inner, last, pred, clean, tile, q, hid, hid_side, done, acc
):
    rows, cols = center.shape[1:]
    blocks = rows // 2 + 2
    groups = q.shape[1] // 8 - 1
    used = hid.shape[1]
    step = done.shape[0] // used

    for ch in range(2):
        tile[ch, 0:8, :] = top[ch, :, 0:cols]
        tile[ch, 8 : 8 + rows, :] = center[ch]
        tile[ch, 8 + rows : 16 + rows, :] = bottom[ch, :, 0:cols]
    edge = jnp.concatenate(
        [
            part
            for ch in range(2)
            for part in (top[ch, :, cols:], side[ch], bottom[ch, :, cols:])
        ],
        axis=0,
    ).astype(BF16)
    w = lax.broadcasted_iota(jnp.int32, (cols, 256), 0)
    k = lax.broadcasted_iota(jnp.int32, (cols, 256), 1)
    e = lax.broadcasted_iota(jnp.int32, (EDGE, 256), 0) + jnp.where(flags[2] != 0, cols, -EDGE)
    ke = lax.broadcasted_iota(jnp.int32, (EDGE, 256), 1)
    for d in range(4):
        sel = jnp.where(w == 2 * k - 3 + d, 1.0, 0.0).astype(BF16)
        sel_side = jnp.where(e == 2 * ke - 3 + d, 1.0, 0.0).astype(BF16)
        both = mm(tile[...].reshape(-1, cols).astype(BF16), sel)
        both += mm(edge, sel_side)
        for ch in range(2):
            q[4 * ch + d] = both[ch * (rows + 16) : (ch + 1) * (rows + 16)]

    end = cols // 2 + 1
    tail = end // 8 * 8
    lines = lax.broadcasted_iota(jnp.int32, (8, 256), 0)
    low = jnp.where((lines == 0) & (flags[2] != 0), 0.0, 1.0)
    high = jnp.where((lines == end - tail) & (flags[3] != 0), 0.0, 1.0)

    def silu_rows(half):
        h = half + half * jnp.tanh(half)
        pieces = []
        for start in range(0, h.shape[0], used):
            pieces += [
                h[start : start + 8] * low,
                h[start + 8 : start + tail],
                h[start + tail : start + tail + 8] * high,
            ]
            if tail + 8 < used:
                pieces.append(h[start + tail + 8 : start + used])
        return jnp.concatenate(pieces, axis=0)

    acc[...] = jnp.zeros(acc.shape, F32)
    hid[0] = jnp.zeros(hid.shape[1:], BF16)
    hid_side[0] = jnp.zeros(hid.shape[1:], BF16)

    def first_layer(t, carry):
        window = q[:, pl.ds(pl.multiple_of(8 * t, 8), 16), :].reshape(128, 256)
        window = jnp.transpose(window)[:used].astype(BF16)
        for s in range(4):
            h = silu_rows(mm(window, first[s]))
            place = 4 * t + s + 1
            hid[place] = h.astype(BF16)
            hid_side[place, :, 0:128] = pltpu.roll(h[:, 128:256], 1, 0).astype(BF16)
            hid_side[place, :, 128:256] = pltpu.roll(h[:, 0:128], used - 1, 0).astype(BF16)
        return carry

    lax.fori_loop(0, groups, first_layer, 0)

    for flag, j in ((0, 0), (1, blocks - 1)):

        @pl.when(flags[flag] != 0)
        def _(j=j):
            hid[j + 1] = jnp.zeros(hid.shape[1:], BF16)
            hid_side[j + 1] = jnp.zeros(hid_side.shape[1:], BF16)

    lane = lax.broadcasted_iota(jnp.int32, (step * used, 256), 1)
    below = lax.rem(lane, 128) < 64

    def next_layers(i, carry):
        j = step * i

        def around(ref, offset):
            return ref[pl.ds(j + offset, step)].reshape(step * used, 256)

        lhs = jnp.concatenate(
            [
                around(hid, 1),
                around(hid_side, 1),
                jnp.where(below, around(hid, 2), around(hid, 0)),
                jnp.where(below, around(hid_side, 2), around(hid_side, 0)),
            ],
            axis=1,
        )
        add_parts(j - step)
        done[...] = silu_rows(mm(lhs, inner[...])).astype(BF16)
        return carry

    def add_parts(j):
        for u in range(step):
            part = mm_nt(last[...], done[u * used : (u + 1) * used])
            row = j + u
            gone = ((row == 0) & (flags[0] != 0)) | ((row == blocks - 1) & (flags[1] != 0))
            part = part * jnp.where(gone, 0.0, 1.0)
            where = pl.ds(pl.multiple_of(16 * (row + step), 16), 32)
            for c in range(0, used, 128):
                width = min(128, used - c)
                acc[c // 128, where, 0:width] = acc[c // 128, where, 0:width] + part[:, c : c + width]

    done[...] = jnp.zeros(done.shape, BF16)
    lax.fori_loop(0, blocks // step, next_layers, 0)
    add_parts(blocks - step)

    def pixels(d):
        return jnp.concatenate(
            [
                jnp.concatenate(
                    [
                        acc[c, pl.ds(24 + 16 * step + 2 * d + ch, rows, stride=8), :]
                        for c in range(2)
                    ],
                    axis=1,
                )
                for ch in range(2)
            ],
            axis=0,
        )

    k = lax.broadcasted_iota(jnp.int32, (256, cols), 0)
    w = lax.broadcasted_iota(jnp.int32, (256, cols), 1)
    total = 0.0
    for d, other, shift in ((1, 3, 1), (2, 0, 255)):
        line = pixels(d) + pltpu.roll(pixels(other), shift, 1)
        sel = jnp.where(w == 2 * k - 3 + d, 1.0, 0.0).astype(BF16)
        both = mm(jnp.concatenate(split2(line), axis=0), sel)
        total += both[: 2 * rows] + both[2 * rows :]
    for ch in range(2):
        part = total[ch * rows : (ch + 1) * rows]
        pred[ch] = part
        clean[ch] = (center[ch] - SIGMA_NOW * part) / SCALE_NOW


def run_network(noisy, top, bottom, side, flags, weights):
    _, rows, cols = noisy.shape
    blocks = rows // 2 + 2
    groups = -(-blocks // 4)
    used = ceil_to(cols // 2 + 2, 16)
    step = max(u for u in (1, 2, 3, 6) if blocks % u == 0)
    vmem = pl.BlockSpec(memory_space=pltpu.VMEM)
    shape = jax.ShapeDtypeStruct(noisy.shape, F32)
    return pl.pallas_call(
        network_kernel,
        out_shape=(shape, shape),
        in_specs=[pl.BlockSpec(memory_space=pltpu.SMEM)] + [vmem] * 7,
        out_specs=(vmem, vmem),
        scratch_shapes=[
            pltpu.VMEM((2, rows + 16, cols), F32),
            pltpu.VMEM((8, 8 * groups + 8, 256), F32),
            pltpu.VMEM((4 * groups + 1, used, 256), BF16),
            pltpu.VMEM((4 * groups + 1, used, 256), BF16),
            pltpu.VMEM((step * used, 256), BF16),
            pltpu.VMEM((2, 16 * (blocks + step) + 16, 128), F32),
        ],
        cost_estimate=pl.CostEstimate(
            flops=20 * rows * cols * 64 * 64, bytes_accessed=24 * rows * cols, transcendentals=0
        ),
        compiler_params=pltpu.CompilerParams(vmem_limit_bytes=40 * MIB),
        name="network",
    )(flags, top, noisy, bottom, side, *weights)


def halo(noisy):
    gz = lax.axis_size("gz")
    _, rows, cols = noisy.shape
    left, right = noisy[:, :, :EDGE], noisy[:, :, cols - EDGE :]
    side = swap_cores(jnp.where(lax.axis_index("col") == 0, right, left))
    down = [(i, i + 1) for i in range(gz - 1)]
    lower = jnp.concatenate([noisy[:, rows - EDGE :], side[:, rows - EDGE :]], axis=2)
    upper = jnp.concatenate([noisy[:, :EDGE], side[:, :EDGE]], axis=2)
    top = lax.ppermute(lower, "gz", down)
    bottom = lax.ppermute(upper, "gz", [(b, a) for a, b in down])
    return top, bottom, side


def swap_cores(value):
    assert lax.axis_size("col") == 2
    return lax.ppermute(value, "col", [(0, 1), (1, 0)])


def edge_flags():
    row, col = lax.axis_index("gz"), lax.axis_index("col")
    last_row, last_col = lax.axis_size("gz") - 1, lax.axis_size("col") - 1
    return jnp.stack([row == 0, row == last_row, col == 0, col == last_col]).astype(jnp.int32)


def halves(matrix):
    high = matrix.astype(ml_dtypes.bfloat16)
    low = (matrix - high.astype(np.float64)).astype(ml_dtypes.bfloat16)
    return np.stack([high, low])


def fourier_parts(length, scale):
    index = np.arange(length)
    angle = 2.0 * np.pi * (np.outer(index, index) % length) / length
    return np.cos(angle) * scale, np.sin(angle) * scale


def turn_table(radix, inner):
    angle = 2.0 * np.pi * np.outer(np.arange(radix), np.arange(inner)) / (radix * inner)
    return np.stack([np.cos(angle), np.sin(angle)]).astype(np.float32)


def small_dft(values, sign):
    n = len(values)
    if n == 1:
        return values
    if n % 2 == 0:
        even = small_dft(values[0::2], sign)
        odd = small_dft(values[1::2], sign)
        low, high = [], []
        for q in range(n // 2):
            re, im = times_unit(odd[q], q, n, sign)
            low.append((even[q][0] + re, even[q][1] + im))
            high.append((even[q][0] - re, even[q][1] - im))
        return low + high
    if n == 3:
        (r0, i0), (r1, i1), (r2, i2) = values
        sr, si = r1 + r2, i1 + i2
        half = math.sqrt(3.0) / 2.0 * sign
        dr, di = half * (r1 - r2), half * (i1 - i2)
        tr, ti = r0 - 0.5 * sr, i0 - 0.5 * si
        return [(r0 + sr, i0 + si), (tr - di, ti + dr), (tr + di, ti - dr)]
    out = []
    for q in range(n):
        terms = [times_unit(v, a * q, n, sign) for a, v in enumerate(values)]
        out.append((sum(t[0] for t in terms), sum(t[1] for t in terms)))
    return out


def times_unit(value, power, n, sign):
    re, im = value
    power %= n
    if power == 0:
        return re, im
    if 4 * power == n:
        return (-im, re) if sign > 0 else (im, -re)
    if 2 * power == n:
        return -re, -im
    if 4 * power == 3 * n:
        return (im, -re) if sign > 0 else (-im, re)
    c = math.cos(2.0 * math.pi * power / n)
    s = sign * math.sin(2.0 * math.pi * power / n)
    return c * re - s * im, c * im + s * re


def turn(value, cos, sin, sign):
    re, im = value
    if sign > 0:
        return re * cos - im * sin, im * cos + re * sin
    return re * cos + im * sin, im * cos - re * sin


def beside(parts, axis):
    return jnp.concatenate([parts[0], parts[0], parts[1]], axis=axis)


def against(matrix, axis):
    return jnp.concatenate([matrix[0], matrix[1], matrix[0]], axis=axis)


def columns_forward_kernel(first, mine, other, maps, scales, matrix, table, out):
    radix, inner = table.shape[1:]
    coils = maps.shape[0]
    rows, _ = mine.shape[1:]
    groups = out.shape[0]
    per = inner // groups
    lead, me = first[0] != 0, first[1]
    image = [
        jnp.concatenate(
            [jnp.where(lead, mine[p], other[p]), jnp.where(lead, other[p], mine[p])], axis=1
        )
        * scales[0:1, 0:1]
        for p in range(2)
    ]
    turned = []
    for coil in range(coils):
        maps_real, maps_imag = maps[coil, 0], maps[coil, 1]
        coil_image = (
            maps_real * image[0] - maps_imag * image[1],
            maps_real * image[1] + maps_imag * image[0],
        )
        parts = [
            tuple(v[:, a * inner : (a + 1) * inner] for v in coil_image) for a in range(radix)
        ]
        parts = small_dft(parts, -1)
        turned.append(
            [
                turn(part, table[0, q : q + 1, :], table[1, q : q + 1, :], -1) if q else part
                for q, part in enumerate(parts)
            ]
        )
    for q in range(radix):
        data = jnp.concatenate([jnp.concatenate(turned[c][q], axis=1) for c in range(coils)], axis=0)
        result = mm_nt(against(matrix, 1), beside(split2(data), 1))
        for p in range(2):
            for g in range(groups):
                start = p * inner + g * per
                for c in range(coils):
                    out[lax.bitwise_xor(g, me), p, c, q] = result[start : start + per, c * rows : (c + 1) * rows]


def columns_forward(first, mine, other, maps, scales, groups, chunk, chunks):
    coils, _, rows, cols = maps.shape
    coils //= chunks
    inner = INNER
    radix = cols // inner
    c, s = fourier_parts(inner, 1.0 / math.sqrt(cols))
    matrix = halves(np.block([[c, s], [-s, c]]))
    table = turn_table(radix, inner)
    vmem = pl.BlockSpec(memory_space=pltpu.VMEM)
    per = inner // groups
    return pl.pallas_call(
        columns_forward_kernel,
        out_shape=jax.ShapeDtypeStruct((groups, 2, coils, radix, per, rows), F32),
        grid=(1,),
        in_specs=[
            pl.BlockSpec(memory_space=pltpu.SMEM),
            vmem,
            vmem,
            pl.BlockSpec((coils, 2, rows, cols), lambda i: (chunk, 0, 0, 0)),
            vmem,
            vmem,
            vmem,
        ],
        out_specs=pl.BlockSpec(
            (groups, 2, coils, radix, per, rows), lambda i: (0, 0, 0, 0, 0, 0)
        ),
        cost_estimate=pl.CostEstimate(
            flops=24 * coils * rows * cols * inner,
            bytes_accessed=16 * coils * rows * cols,
            transcendentals=0,
        ),
        compiler_params=pltpu.CompilerParams(vmem_limit_bytes=20 * MIB),
        name="columns_forward",
    )(first, mine, other, maps, scales, jnp.asarray(matrix), jnp.asarray(table))


def rows_kernel(place, data, kept, target, scales, forward, inverse, table, out, lines):
    radix = table.shape[1]
    count = data.shape[2]
    spots = [lax.bitwise_xor(a, place[1]) for a in range(radix)]
    parts = small_dft([(data[spot, 0], data[spot, 1]) for spot in spots], -1)
    for q, part in enumerate(parts):
        if q:
            part = turn(part, table[0, q : q + 1, :], table[1, q : q + 1, :], -1)
        for p in range(2):
            lines[q * count : (q + 1) * count, p * LANES : (p + 1) * LANES] = part[p]
    spectrum = mm(beside(split2(lines[...]), 1), against(forward, 0))
    keep = kept[...].reshape(radix * count, LANES) * scales[2:3, :]
    unit = scales[1:2, :]
    residual = jnp.concatenate(
        [
            keep
            * (spectrum[:, p * LANES : (p + 1) * LANES] * unit - target[p].reshape(-1, LANES))
            for p in range(2)
        ],
        axis=1,
    )
    lines[...] = mm(beside(split2(residual), 1), against(inverse, 0))
    back = []
    for q in range(radix):
        part = tuple(
            lines[q * count : (q + 1) * count, p * LANES : (p + 1) * LANES] for p in range(2)
        )
        if q:
            part = turn(part, table[0, q : q + 1, :], table[1, q : q + 1, :], 1)
        back.append(part)
    for spot, (re, im) in zip(spots, small_dft(back, 1)):
        out[spot, 0] = re
        out[spot, 1] = im


def rows_both_ways(place, data, kept, target, scales, first_line):
    radix, _, count, _ = data.shape
    pencil = kept.shape[1]
    c, s = fourier_parts(LANES, 1.0 / math.sqrt(radix * LANES))
    forward = halves(np.block([[c, -s], [s, c]]))
    inverse = halves(np.block([[c, s], [-s, c]]))
    table = turn_table(radix, LANES)
    block = max(b for b in range(8, 56, 8) if pencil % b == 0)
    offset, repeat = first_line // block, pencil // block
    vmem = pl.BlockSpec(memory_space=pltpu.VMEM)
    spec = pl.BlockSpec((radix, 2, block, LANES), lambda i: (0, 0, i, 0))
    return pl.pallas_call(
        rows_kernel,
        out_shape=jax.ShapeDtypeStruct(data.shape, F32),
        grid=(count // block,),
        in_specs=[
            pl.BlockSpec(memory_space=pltpu.SMEM),
            spec,
            pl.BlockSpec((radix, block, LANES), lambda i: (0, lax.rem(i + offset, repeat), 0)),
            pl.BlockSpec((2, radix, block, LANES), lambda i: (0, 0, i + offset, 0)),
            vmem,
            vmem,
            vmem,
            vmem,
        ],
        out_specs=spec,
        scratch_shapes=[pltpu.VMEM((radix * block, 2 * LANES), F32)],
        cost_estimate=pl.CostEstimate(
            flops=24 * radix * count * LANES * LANES,
            bytes_accessed=32 * radix * count * LANES,
            transcendentals=0,
        ),
        compiler_params=pltpu.CompilerParams(vmem_limit_bytes=12 * MIB),
        name="rows_both_ways",
    )(place, data, kept, target, scales, jnp.asarray(forward), jnp.asarray(inverse), jnp.asarray(table))


def columns_inverse_kernel(last, first, data, maps, scales, matrix, table, *refs):
    radix, inner = table.shape[1:]
    groups = data.shape[0]
    coils, _, rows, cols = maps.shape
    base, outs = (None, refs) if len(refs) == 1 else (refs[0], refs[1:])
    parts = []
    for q in range(radix):
        lines = jnp.concatenate(
            [
                jnp.transpose(
                    jnp.concatenate(
                        [
                            data[lax.bitwise_xor(g, first[1]), p, c, q]
                            for p in range(2)
                            for g in range(groups)
                        ], axis=0
                    )
                )
                for c in range(coils)
            ],
            axis=0,
        )
        result = mm(beside(split2(lines), 1), against(matrix, 0))
        part = (result[:, :inner], result[:, inner:])
        if q:
            part = turn(part, table[0, q : q + 1, :], table[1, q : q + 1, :], 1)
        parts.append(part)
    sums = [[], []]
    for a, (re, im) in enumerate(small_dft(parts, 1)):
        where = slice(a * inner, (a + 1) * inner)
        total = [0.0, 0.0]
        for c in range(coils):
            maps_real, maps_imag = maps[c, 0, :, where], maps[c, 1, :, where]
            x, y = re[c * rows : (c + 1) * rows], im[c * rows : (c + 1) * rows]
            total[0] += maps_real * x + maps_imag * y
            total[1] += maps_real * y - maps_imag * x
        for p in range(2):
            part = total[p] * scales[3:4, 0:1]
            sums[p].append(part if base is None else base[p, :, where] + part)
    lead = first[0] != 0
    for p in range(2):
        line = jnp.concatenate(sums[p], axis=1)
        if last:
            own, away = line[:, : cols // 2], line[:, cols // 2 :]
            outs[0][p] = jnp.where(lead, own, away)
            outs[1][p] = jnp.where(lead, away, own)
        else:
            outs[0][p] = line


def columns_inverse(first, data, maps, scales, chunk, chunks, base):
    _, _, coils, radix, _, rows = data.shape
    cols = maps.shape[3]
    inner = cols // radix
    c, s = fourier_parts(inner, 1.0 / math.sqrt(cols))
    matrix = halves(np.block([[c, s], [-s, c]]))
    table = turn_table(radix, inner)
    vmem = pl.BlockSpec(memory_space=pltpu.VMEM)
    last = chunk == chunks - 1
    if last:
        shape = [jax.ShapeDtypeStruct((2, rows, cols // 2), F32)] * 2
    else:
        shape = [jax.ShapeDtypeStruct((2, rows, cols), F32)]
    return pl.pallas_call(
        partial(columns_inverse_kernel, last),
        out_shape=shape,
        grid=(1,),
        in_specs=[
            pl.BlockSpec(memory_space=pltpu.SMEM),
            vmem,
            pl.BlockSpec((coils, 2, rows, cols), lambda i: (chunk, 0, 0, 0)),
            vmem,
            vmem,
            vmem,
        ]
        + [vmem] * len(base),
        out_specs=[vmem] * len(shape),
        cost_estimate=pl.CostEstimate(
            flops=24 * coils * rows * cols * inner,
            bytes_accessed=16 * coils * rows * cols,
            transcendentals=0,
        ),
        compiler_params=pltpu.CompilerParams(vmem_limit_bytes=20 * MIB),
        name="columns_inverse",
    )(first, data, maps, scales, jnp.asarray(matrix), jnp.asarray(table), *base)


def target_kernel(radix3, token, *refs):
    tiles = (len(refs) - 4) // 2
    measured, sampled = refs[:tiles], refs[tiles : 2 * tiles]
    target, kept, lines, order = refs[2 * tiles :]
    radix, pencil, _ = kept.shape
    count, height = lines.shape
    coils = count // pencil
    per = pencil // radix3

    @pl.when(pl.program_id(0) == 0)
    def _():
        source = lax.broadcasted_iota(jnp.int32, (height, LANES), 0)
        place = lax.broadcasted_iota(jnp.int32, (height, LANES), 1)
        for q in range(radix):
            order[:, q * LANES : (q + 1) * LANES] = jnp.where(
                source == radix * place + q, 1.0, 0.0
            ).astype(BF16)
        for t in range(tiles):
            for q in range(radix3):
                lines[q * per : (q + 1) * per, t * LANES : (t + 1) * LANES] = sampled[t][
                    pl.ds(q, per, stride=radix3), :
                ].astype(F32)
        picked = mm(lines[0:pencil, :].astype(BF16), order[...])
        for q in range(radix):
            kept[q] = picked[:, q * LANES : (q + 1) * LANES]

    for t in range(tiles):
        source = measured[t].reshape(count, LANES)
        for c in range(coils):
            for q in range(radix3):
                start = c * pencil + q * per
                lines[start : start + per, t * LANES : (t + 1) * LANES] = source[
                    pl.ds(q * coils + c, per, stride=radix3 * coils), :
                ]
    high, low = split2(lines[...])
    for q in range(0, radix, 2):
        width = min(2, radix - q) * LANES
        part = order[:, q * LANES : q * LANES + width]
        picked = mm(high, part) + mm(low, part)
        for k in range(0, width, LANES):
            target[0, q + k // LANES] = picked[:, k : k + LANES]


def prepare_target(token, measured, sampled, radix3):
    _, pencil, coils, height = measured.shape
    radix = height // LANES
    count = pencil * coils
    return pl.pallas_call(
        partial(target_kernel, radix3),
        out_shape=(
            jax.ShapeDtypeStruct((2, radix, count, LANES), F32),
            jax.ShapeDtypeStruct((radix, pencil, LANES), F32),
        ),
        grid=(2,),
        in_specs=[pl.BlockSpec(memory_space=pltpu.SMEM)]
        + [
            pl.BlockSpec((1, pencil, coils, LANES), lambda i, t=t: (i, 0, 0, t))
            for t in range(radix)
        ]
        + [pl.BlockSpec((pencil, LANES), lambda i, t=t: (0, t)) for t in range(radix)],
        out_specs=(
            pl.BlockSpec((1, radix, count, LANES), lambda i: (i, 0, 0, 0)),
            pl.BlockSpec((radix, pencil, LANES), lambda i: (0, 0, 0)),
        ),
        scratch_shapes=[pltpu.VMEM((count, height), F32), pltpu.VMEM((height, height), BF16)],
        cost_estimate=pl.CostEstimate(
            flops=8 * count * height * height, bytes_accessed=16 * count * height, transcendentals=0
        ),
        compiler_params=pltpu.CompilerParams(vmem_limit_bytes=20 * MIB),
        name="target",
    )(token, *[measured] * radix, *[sampled] * radix)


def pairwise(groups):
    return groups <= 8 and groups & (groups - 1) == 0


def send(value):
    groups = value.shape[0]
    if not pairwise(groups):
        value = value.astype(jnp.float16)
        return [lax.all_to_all(value, "gz", split_axis=0, concat_axis=0, tiled=True)]
    return [value[0]] + [
        lax.ppermute(value[k].astype(jnp.float16), "gz", [(i, i ^ k) for i in range(groups)])
        for k in range(1, groups)
    ]


def receive(parts):
    if len(parts) == 1:
        return parts[0].astype(F32)
    return jnp.stack([part.astype(F32) for part in parts])


def after(value, *earlier):
    return lax.optimization_barrier((value, *earlier))[0]


def local(
    noisy_image, fresh_noise, coil_maps, measured, sampled, first_kernel, inner_kernels, last_kernel
):
    groups = lax.axis_size("gz")
    coils, _, rows, cols = coil_maps.shape
    height = measured.shape[3]
    radix, inner = cols // INNER, INNER
    per = inner // groups
    row_radix = height // LANES
    chunks = 2
    pencil = radix * per
    count = coils * pencil // chunks
    place = lax.axis_index("gz") if pairwise(groups) else 0
    lead = jnp.stack([lax.axis_index("col") == 0, place]).astype(jnp.int32)

    weights, scales = network_weights(
        first_kernel, inner_kernels[0], last_kernel, cols, height
    )
    top, bottom, side = halo(noisy_image)
    predicted, clean = run_network(noisy_image, top, bottom, side, edge_flags(), weights)
    other = swap_cores(clean)

    token = lead
    arrived = []
    for chunk in range(chunks):
        spectra = columns_forward(token, clean, other, coil_maps, scales, groups, chunk, chunks)
        spectra = send(spectra.reshape(groups, 2, count, rows))
        token = after(lead, spectra[0])
        arrived.append(spectra)
    target, kept = prepare_target(token, measured, sampled, radix)

    back = []
    for chunk in range(chunks):
        lines = receive(after(arrived[chunk], token))
        if rows != LANES:
            lines = jnp.transpose(lines, (1, 2, 0, 3)).reshape(2, -1, row_radix, LANES)
            lines = jnp.transpose(lines, (2, 0, 1, 3))
        lines = rows_both_ways(lead, lines, kept, target, scales, chunk * (coils // chunks) * pencil)
        if rows != LANES:
            lines = jnp.transpose(lines, (1, 2, 0, 3)).reshape(2, -1, groups, rows)
            lines = jnp.transpose(lines, (2, 0, 1, 3))
        token = lines[0]
        back.append(send(lines))

    gradient = []
    for chunk in range(chunks):
        lines = receive(after(back[chunk], *gradient))
        lines = lines.reshape(groups, 2, coils // chunks, radix, per, rows)
        gradient = columns_inverse(lead, lines, coil_maps, scales, chunk, chunks, gradient)

    own, away = gradient
    own = own + swap_cores(away)
    update = clean - STEP_GAIN * own
    return SCALE_NEXT * update + DIRECT_GAIN * predicted + NOISE_GAIN * fresh_noise


def solution(mesh):
    in_specs = (
        P("grp", "gz", "col"),
        P("grp", "gz", "col"),
        P("col", "grp", "gz", None),
        P("grp", "gz", "col", None),
        P("gz", "grp"),
        P(),
        P(),
        P(),
    )
    out_specs = P("grp", "gz", "col")

    return jax.shard_map(local, mesh=mesh, in_specs=in_specs, out_specs=out_specs, check_vma=False)
```

```python
import math
from functools import partial

import jax
import jax.numpy as jnp
import ml_dtypes
import numpy as np
from jax import lax
from jax.experimental import pallas as pl
from jax.experimental.pallas import tpu as pltpu
from jax.sharding import PartitionSpec as P

SCALE_NOW = 0.8
SIGMA_NOW = 0.6
STEP_GAIN = 1.0
SCALE_NEXT = 0.9
DIRECT_GAIN = 0.31622776601683794
NOISE_GAIN = 0.3

NOISY_MAX = 6.0
MAPS_MAX = 1.5
MEASURED_MAX = 2.4

F32 = jnp.float32
BF16 = jnp.bfloat16
LANES = 128
EDGE = 8
MIB = 1024 * 1024
INNER = 256


def ceil_to(value, step):
    return -(-value // step) * step


def tap_choice(rows, cols):
    choice = np.zeros(rows.shape + (9,), np.float32)
    for index in np.ndindex(rows.shape):
        a, b = rows[index], cols[index]
        if 0 <= a < 3 and 0 <= b < 3:
            choice[index + (3 * a + b,)] = 1.0
    return choice


def tap_choices():
    pair = np.eye(2, dtype=np.float32)
    first, last = [], []
    for c, r in np.ndindex(2, 2):
        s, d, x = np.meshgrid(*map(np.arange, (4, 4, 16)), indexing="ij")
        chosen = tap_choice(x - 5 - 2 * s - r, d - c)
        first.append(np.einsum("sdxt,hk->shdxtk", chosen, pair).reshape(512, 18))
        dr, dc = np.meshgrid(np.arange(4), np.arange(4), indexing="ij")
        chosen = tap_choice(r - dr + 2, c - dc + 2)
        last.append(np.einsum("yxt,hk->yxhtk", chosen, pair).reshape(32, 18))
    middle = []
    for cols, rows in (((0, 1), (0, 1)), ((-1, 2), (0, 1)), ((0, 1), (2, -1)), ((-1, 2), (2, -1))):
        for gamma in cols:
            for rho in rows:
                taps = []
                for c, r in np.ndindex(2, 2):
                    a, b = rho - r + 1, gamma - c + 1
                    taps.append(3 * a + b if 0 <= a < 3 and 0 <= b < 3 else None)
                middle.append(taps)
    return np.stack(first), middle, np.stack(last)


def weights_kernel(cols, height, first_taps, k2, last_taps, choice, first, inner, last, scales):
    _, middle, _ = tap_choices()
    ch = k2.shape[1]
    k1 = jnp.concatenate([first_taps[t].astype(F32) for t in range(9)], axis=0).astype(BF16)
    k3 = jnp.concatenate([last_taps[t].astype(F32) for t in range(9)], axis=0).astype(BF16)
    parts = [mm(choice[i, 0:512], k1) for i in range(4)]
    first[...] = (0.5 * jnp.concatenate(parts, axis=1)).astype(BF16).reshape(first.shape)
    turned = [(0.5 * jnp.transpose(k2[t].astype(F32))).astype(BF16) for t in range(9)]
    zero = jnp.zeros((ch, ch), BF16)
    for p, taps in enumerate(middle):
        row = [zero if t is None else turned[t] for t in taps]
        inner[p * ch : (p + 1) * ch, :] = jnp.concatenate(row, axis=1)
    parts = [mm(choice[i, 512:544], k3) for i in range(4)]
    last[...] = jnp.concatenate(parts, axis=1).astype(BF16)

    def top(value, axes):
        for axis in axes:
            value = jnp.max(value, axis=axis, keepdims=True)
        return value

    gain1 = top(jnp.sum(jnp.abs(k1.astype(F32)), axis=0, keepdims=True), (1,))
    gain2 = sum(jnp.abs(k2[t].astype(F32)) for t in range(9))
    gain2 = top(jnp.sum(gain2, axis=1, keepdims=True), (0,))
    gain3 = jnp.sum(jnp.abs(k3.astype(F32)), axis=1, keepdims=True)
    odd = lax.rem(lax.broadcasted_iota(jnp.int32, gain3.shape, 0), 2) == 1
    gain3 = jnp.maximum(
        jnp.sum(jnp.where(odd, gain3, 0.0), axis=0, keepdims=True),
        jnp.sum(jnp.where(odd, 0.0, gain3), axis=0, keepdims=True),
    )
    predicted = 1.1 * NOISY_MAX * gain1 * gain2 * gain3
    clean = (NOISY_MAX + SIGMA_NOW * predicted) / SCALE_NOW
    spectra = 1.1 * math.sqrt(cols) * 2.0 * MAPS_MAX * clean
    lines = 1.1 * math.sqrt(height) * (spectra + math.sqrt(2.0) * MEASURED_MAX)
    rows = []
    for bound in (spectra, lines):
        rows += [60000.0 / bound, bound / 60000.0]
    scales[...] = jnp.concatenate([jnp.broadcast_to(r, (1, LANES)) for r in rows + rows], axis=0)


def network_weights(first_kernel, inner_kernel, last_kernel, cols, height):
    ch = inner_kernel.shape[1]
    choice1, _, choice3 = tap_choices()
    shapes = ((4, 128, 4 * ch), (16 * ch, 4 * ch), (32, 4 * ch))
    first, inner, last, scales = pl.pallas_call(
        partial(weights_kernel, cols, height),
        out_shape=[jax.ShapeDtypeStruct(d, BF16) for d in shapes]
        + [jax.ShapeDtypeStruct((8, LANES), F32)],
        cost_estimate=pl.CostEstimate(flops=10**7, bytes_accessed=10**6, transcendentals=0),
        compiler_params=pltpu.CompilerParams(vmem_limit_bytes=10 * MIB),
        name="weights",
    )(
        jnp.transpose(first_kernel, (0, 2, 1)),
        inner_kernel,
        last_kernel,
        jnp.asarray(np.concatenate([choice1, choice3], axis=1), BF16),
    )
    return (first, inner, last), scales


def split2(value):
    high = value.astype(BF16)
    return high, (value - high.astype(F32)).astype(BF16)


def mm(lhs, rhs):
    return lax.dot_general(lhs, rhs, (((1,), (0,)), ((), ())), preferred_element_type=F32)


def mm_nt(lhs, rhs):
    return lax.dot_general(lhs, rhs, (((1,), (1,)), ((), ())), preferred_element_type=F32)


def network_kernel(
    flags, top, center, bottom, side, first, inner, last, pred, clean, tile, q, hid, hid_side, done, acc
):
    rows, cols = center.shape[1:]
    blocks = rows // 2 + 2
    used = hid.shape[1]
    step = done.shape[0] // used

    for ch in range(2):
        tile[ch, 0:8, :] = top[ch, :, 0:cols]
        tile[ch, 8 : 8 + rows, :] = center[ch]
        tile[ch, 8 + rows : 16 + rows, :] = bottom[ch, :, 0:cols]
    edge = jnp.concatenate(
        [
            part
            for ch in range(2)
            for part in (top[ch, :, cols:], side[ch], bottom[ch, :, cols:])
        ],
        axis=0,
    ).astype(BF16)
    w = lax.broadcasted_iota(jnp.int32, (cols, 256), 0)
    k = lax.broadcasted_iota(jnp.int32, (cols, 256), 1)
    e = lax.broadcasted_iota(jnp.int32, (EDGE, 256), 0) + jnp.where(flags[2] != 0, cols, -EDGE)
    ke = lax.broadcasted_iota(jnp.int32, (EDGE, 256), 1)
    for d in range(4):
        sel = jnp.where(w == 2 * k - 3 + d, 1.0, 0.0).astype(BF16)
        sel_side = jnp.where(e == 2 * ke - 3 + d, 1.0, 0.0).astype(BF16)
        both = mm(tile[...].reshape(-1, cols).astype(BF16), sel)
        both += mm(edge, sel_side)
        for ch in range(2):
            q[4 * ch + d, 0 : rows + 16] = both[ch * (rows + 16) : (ch + 1) * (rows + 16)]
            q[4 * ch + d, rows + 16 :] = jnp.zeros((8, 256), F32)

    end = cols // 2 + 1
    tail = end // 8 * 8
    lines = lax.broadcasted_iota(jnp.int32, (8, 256), 0)
    low = jnp.where((lines == 0) & (flags[2] != 0), 0.0, 1.0)
    high = jnp.where((lines == end - tail) & (flags[3] != 0), 0.0, 1.0)

    def silu_rows(half):
        h = half + half * jnp.tanh(half)
        pieces = []
        for start in range(0, h.shape[0], used):
            pieces += [
                h[start : start + 8] * low,
                h[start + 8 : start + tail],
                h[start + tail : start + tail + 8] * high,
            ]
            if tail + 8 < used:
                pieces.append(h[start + tail + 8 : start + used])
        return jnp.concatenate(pieces, axis=0)

    acc[...] = jnp.zeros(acc.shape, F32)
    hid[0] = jnp.zeros(hid.shape[1:], BF16)
    hid_side[0] = jnp.zeros(hid.shape[1:], BF16)

    def first_layer(pair, carry):
        windows = []
        for t in (2 * pair, 2 * pair + 1):
            window = q[:, pl.ds(pl.multiple_of(8 * t, 8), 16), :].reshape(128, 256)
            windows.append(jnp.transpose(window)[:used].astype(BF16))
        for n, window in enumerate(windows):
            for s in range(4):
                h = silu_rows(mm(window, first[s]))
                place = 8 * pair + 4 * n + s + 1
                hid[place] = h.astype(BF16)
                hid_side[place, :, 0:128] = pltpu.roll(h[:, 128:256], 1, 0).astype(BF16)
                hid_side[place, :, 128:256] = pltpu.roll(h[:, 0:128], used - 1, 0).astype(BF16)
        return carry

    lax.fori_loop(0, (hid.shape[0] - 1) // 8, first_layer, 0)

    for flag, j in ((0, 0), (1, blocks - 1)):

        @pl.when(flags[flag] != 0)
        def _(j=j):
            hid[j + 1] = jnp.zeros(hid.shape[1:], BF16)
            hid_side[j + 1] = jnp.zeros(hid_side.shape[1:], BF16)

    lane = lax.broadcasted_iota(jnp.int32, (step * used, 256), 1)
    below = lax.rem(lane, 128) < 64

    def next_layers(i, carry):
        j = step * i

        def around(ref, offset):
            return ref[pl.ds(j + offset, step)].reshape(step * used, 256)

        lhs = jnp.concatenate(
            [
                around(hid, 1),
                around(hid_side, 1),
                jnp.where(below, around(hid, 2), around(hid, 0)),
                jnp.where(below, around(hid_side, 2), around(hid_side, 0)),
            ],
            axis=1,
        )
        add_parts(j - step)
        done[...] = silu_rows(mm(lhs, inner[...])).astype(BF16)
        return carry

    def add_parts(j):
        for u in range(step):
            part = mm_nt(last[...], done[u * used : (u + 1) * used])
            row = j + u
            gone = ((row == 0) & (flags[0] != 0)) | ((row == blocks - 1) & (flags[1] != 0))
            part = part * jnp.where(gone, 0.0, 1.0)
            where = pl.ds(pl.multiple_of(16 * (row + step), 16), 32)
            for c in range(0, used, 128):
                width = min(128, used - c)
                acc[c // 128, where, 0:width] = acc[c // 128, where, 0:width] + part[:, c : c + width]

    done[...] = jnp.zeros(done.shape, BF16)
    lax.fori_loop(0, blocks // step, next_layers, 0)
    add_parts(blocks - step)

    def pixels(d):
        return jnp.concatenate(
            [
                jnp.concatenate(
                    [
                        acc[c, pl.ds(24 + 16 * step + 2 * d + ch, rows, stride=8), :]
                        for c in range(2)
                    ],
                    axis=1,
                )
                for ch in range(2)
            ],
            axis=0,
        )

    k = lax.broadcasted_iota(jnp.int32, (256, cols), 0)
    w = lax.broadcasted_iota(jnp.int32, (256, cols), 1)
    total = 0.0
    for d, other, shift in ((1, 3, 1), (2, 0, 255)):
        line = pixels(d) + pltpu.roll(pixels(other), shift, 1)
        sel = jnp.where(w == 2 * k - 3 + d, 1.0, 0.0).astype(BF16)
        both = mm(jnp.concatenate(split2(line), axis=0), sel)
        total += both[: 2 * rows] + both[2 * rows :]
    for ch in range(2):
        part = total[ch * rows : (ch + 1) * rows]
        pred[ch] = part
        clean[ch] = (center[ch] - SIGMA_NOW * part) / SCALE_NOW


def run_network(noisy, top, bottom, side, flags, weights):
    _, rows, cols = noisy.shape
    blocks = rows // 2 + 2
    pairs = -(-blocks // 8)
    used = ceil_to(cols // 2 + 2, 16)
    step = max(u for u in (1, 2, 3, 6) if blocks % u == 0)
    vmem = pl.BlockSpec(memory_space=pltpu.VMEM)
    shape = jax.ShapeDtypeStruct(noisy.shape, F32)
    return pl.pallas_call(
        network_kernel,
        out_shape=(shape, shape),
        in_specs=[pl.BlockSpec(memory_space=pltpu.SMEM)] + [vmem] * 7,
        out_specs=(vmem, vmem),
        scratch_shapes=[
            pltpu.VMEM((2, rows + 16, cols), F32),
            pltpu.VMEM((8, rows + 24, 256), F32),
            pltpu.VMEM((8 * pairs + 1, used, 256), BF16),
            pltpu.VMEM((8 * pairs + 1, used, 256), BF16),
            pltpu.VMEM((step * used, 256), BF16),
            pltpu.VMEM((2, 16 * (blocks + step) + 16, 128), F32),
        ],
        cost_estimate=pl.CostEstimate(
            flops=20 * rows * cols * 64 * 64, bytes_accessed=24 * rows * cols, transcendentals=0
        ),
        compiler_params=pltpu.CompilerParams(vmem_limit_bytes=40 * MIB),
        name="network",
    )(flags, top, noisy, bottom, side, *weights)


def halo(noisy):
    gz = lax.axis_size("gz")
    _, rows, cols = noisy.shape
    left, right = noisy[:, :, :EDGE], noisy[:, :, cols - EDGE :]
    side = swap_cores(jnp.where(lax.axis_index("col") == 0, right, left))
    down = [(i, i + 1) for i in range(gz - 1)]
    lower = jnp.concatenate([noisy[:, rows - EDGE :], side[:, rows - EDGE :]], axis=2)
    upper = jnp.concatenate([noisy[:, :EDGE], side[:, :EDGE]], axis=2)
    top = lax.ppermute(lower, "gz", down)
    bottom = lax.ppermute(upper, "gz", [(b, a) for a, b in down])
    return top, bottom, side


def swap_cores(value):
    assert lax.axis_size("col") == 2
    return lax.ppermute(value, "col", [(0, 1), (1, 0)])


def edge_flags():
    row, col = lax.axis_index("gz"), lax.axis_index("col")
    last_row, last_col = lax.axis_size("gz") - 1, lax.axis_size("col") - 1
    return jnp.stack([row == 0, row == last_row, col == 0, col == last_col]).astype(jnp.int32)


def halves(matrix):
    high = matrix.astype(ml_dtypes.bfloat16)
    low = (matrix - high.astype(np.float64)).astype(ml_dtypes.bfloat16)
    return np.stack([high, low])


def fourier_parts(length, scale):
    index = np.arange(length)
    angle = 2.0 * np.pi * (np.outer(index, index) % length) / length
    return np.cos(angle) * scale, np.sin(angle) * scale


def turn_table(radix, inner):
    angle = 2.0 * np.pi * np.outer(np.arange(radix), np.arange(inner)) / (radix * inner)
    return np.stack([np.cos(angle), np.sin(angle)]).astype(np.float32)


def small_dft(values, sign):
    n = len(values)
    if n == 1:
        return values
    if n % 2 == 0:
        even = small_dft(values[0::2], sign)
        odd = small_dft(values[1::2], sign)
        low, high = [], []
        for q in range(n // 2):
            re, im = times_unit(odd[q], q, n, sign)
            low.append((even[q][0] + re, even[q][1] + im))
            high.append((even[q][0] - re, even[q][1] - im))
        return low + high
    if n == 3:
        (r0, i0), (r1, i1), (r2, i2) = values
        sr, si = r1 + r2, i1 + i2
        half = math.sqrt(3.0) / 2.0 * sign
        dr, di = half * (r1 - r2), half * (i1 - i2)
        tr, ti = r0 - 0.5 * sr, i0 - 0.5 * si
        return [(r0 + sr, i0 + si), (tr - di, ti + dr), (tr + di, ti - dr)]
    out = []
    for q in range(n):
        terms = [times_unit(v, a * q, n, sign) for a, v in enumerate(values)]
        out.append((sum(t[0] for t in terms), sum(t[1] for t in terms)))
    return out


def times_unit(value, power, n, sign):
    re, im = value
    power %= n
    if power == 0:
        return re, im
    if 4 * power == n:
        return (-im, re) if sign > 0 else (im, -re)
    if 2 * power == n:
        return -re, -im
    if 4 * power == 3 * n:
        return (im, -re) if sign > 0 else (-im, re)
    c = math.cos(2.0 * math.pi * power / n)
    s = sign * math.sin(2.0 * math.pi * power / n)
    return c * re - s * im, c * im + s * re


def turn(value, cos, sin, sign):
    re, im = value
    if sign > 0:
        return re * cos - im * sin, im * cos + re * sin
    return re * cos + im * sin, im * cos - re * sin


def beside(parts, axis):
    return jnp.concatenate([parts[0], parts[0], parts[1]], axis=axis)


def against(matrix, axis):
    return jnp.concatenate([matrix[0], matrix[1], matrix[0]], axis=axis)


def columns_forward_kernel(first, mine, other, maps, scales, matrix, table, out):
    radix, inner = table.shape[1:]
    coils = maps.shape[0]
    rows, _ = mine.shape[1:]
    groups = out.shape[0]
    per = inner // groups
    lead, me = first[0] != 0, first[1]
    image = [
        jnp.concatenate(
            [jnp.where(lead, mine[p], other[p]), jnp.where(lead, other[p], mine[p])], axis=1
        )
        * scales[0:1, 0:1]
        for p in range(2)
    ]
    turned = []
    for coil in range(coils):
        maps_real, maps_imag = maps[coil, 0], maps[coil, 1]
        coil_image = (
            maps_real * image[0] - maps_imag * image[1],
            maps_real * image[1] + maps_imag * image[0],
        )
        parts = [
            tuple(v[:, a * inner : (a + 1) * inner] for v in coil_image) for a in range(radix)
        ]
        parts = small_dft(parts, -1)
        turned.append(
            [
                turn(part, table[0, q : q + 1, :], table[1, q : q + 1, :], -1) if q else part
                for q, part in enumerate(parts)
            ]
        )
    for q in range(radix):
        data = jnp.concatenate([jnp.concatenate(turned[c][q], axis=1) for c in range(coils)], axis=0)
        result = mm_nt(against(matrix, 1), beside(split2(data), 1))
        for p in range(2):
            for g in range(groups):
                start = p * inner + g * per
                for c in range(coils):
                    out[lax.bitwise_xor(g, me), p, c, q] = result[start : start + per, c * rows : (c + 1) * rows]


def columns_forward(first, mine, other, maps, scales, groups, chunk, chunks):
    coils, _, rows, cols = maps.shape
    coils //= chunks
    inner = INNER
    radix = cols // inner
    c, s = fourier_parts(inner, 1.0 / math.sqrt(cols))
    matrix = halves(np.block([[c, s], [-s, c]]))
    table = turn_table(radix, inner)
    vmem = pl.BlockSpec(memory_space=pltpu.VMEM)
    per = inner // groups
    return pl.pallas_call(
        columns_forward_kernel,
        out_shape=jax.ShapeDtypeStruct((groups, 2, coils, radix, per, rows), F32),
        grid=(1,),
        in_specs=[
            pl.BlockSpec(memory_space=pltpu.SMEM),
            vmem,
            vmem,
            pl.BlockSpec((coils, 2, rows, cols), lambda i: (chunk, 0, 0, 0)),
            vmem,
            vmem,
            vmem,
        ],
        out_specs=pl.BlockSpec(
            (groups, 2, coils, radix, per, rows), lambda i: (0, 0, 0, 0, 0, 0)
        ),
        cost_estimate=pl.CostEstimate(
            flops=24 * coils * rows * cols * inner,
            bytes_accessed=16 * coils * rows * cols,
            transcendentals=0,
        ),
        compiler_params=pltpu.CompilerParams(vmem_limit_bytes=20 * MIB),
        name="columns_forward",
    )(first, mine, other, maps, scales, jnp.asarray(matrix), jnp.asarray(table))


def rows_kernel(place, data, kept, target, scales, forward, inverse, table, out, lines):
    radix = table.shape[1]
    count = data.shape[2]
    spots = [lax.bitwise_xor(a, place[1]) for a in range(radix)]
    parts = small_dft([(data[spot, 0], data[spot, 1]) for spot in spots], -1)
    for q, part in enumerate(parts):
        if q:
            part = turn(part, table[0, q : q + 1, :], table[1, q : q + 1, :], -1)
        for p in range(2):
            lines[q * count : (q + 1) * count, p * LANES : (p + 1) * LANES] = part[p]
    spectrum = mm(beside(split2(lines[...]), 1), against(forward, 0))
    keep = kept[...].reshape(radix * count, LANES) * scales[2:3, :]
    unit = scales[1:2, :]
    residual = jnp.concatenate(
        [
            keep
            * (spectrum[:, p * LANES : (p + 1) * LANES] * unit - target[p].reshape(-1, LANES))
            for p in range(2)
        ],
        axis=1,
    )
    lines[...] = mm(beside(split2(residual), 1), against(inverse, 0))
    back = []
    for q in range(radix):
        part = tuple(
            lines[q * count : (q + 1) * count, p * LANES : (p + 1) * LANES] for p in range(2)
        )
        if q:
            part = turn(part, table[0, q : q + 1, :], table[1, q : q + 1, :], 1)
        back.append(part)
    for spot, (re, im) in zip(spots, small_dft(back, 1)):
        out[spot, 0] = re
        out[spot, 1] = im


def rows_both_ways(place, data, kept, target, scales, first_line):
    radix, _, count, _ = data.shape
    pencil = kept.shape[1]
    c, s = fourier_parts(LANES, 1.0 / math.sqrt(radix * LANES))
    forward = halves(np.block([[c, -s], [s, c]]))
    inverse = halves(np.block([[c, s], [-s, c]]))
    table = turn_table(radix, LANES)
    block = max(b for b in range(8, 104, 8) if pencil % b == 0)
    offset, repeat = first_line // block, pencil // block
    vmem = pl.BlockSpec(memory_space=pltpu.VMEM)
    spec = pl.BlockSpec((radix, 2, block, LANES), lambda i: (0, 0, i, 0))
    return pl.pallas_call(
        rows_kernel,
        out_shape=jax.ShapeDtypeStruct(data.shape, F32),
        grid=(count // block,),
        in_specs=[
            pl.BlockSpec(memory_space=pltpu.SMEM),
            spec,
            pl.BlockSpec((radix, block, LANES), lambda i: (0, lax.rem(i + offset, repeat), 0)),
            pl.BlockSpec((2, radix, block, LANES), lambda i: (0, 0, i + offset, 0)),
            vmem,
            vmem,
            vmem,
            vmem,
        ],
        out_specs=spec,
        scratch_shapes=[pltpu.VMEM((radix * block, 2 * LANES), F32)],
        cost_estimate=pl.CostEstimate(
            flops=24 * radix * count * LANES * LANES,
            bytes_accessed=32 * radix * count * LANES,
            transcendentals=0,
        ),
        compiler_params=pltpu.CompilerParams(vmem_limit_bytes=12 * MIB),
        name="rows_both_ways",
    )(place, data, kept, target, scales, jnp.asarray(forward), jnp.asarray(inverse), jnp.asarray(table))


def columns_inverse_kernel(last, first, data, maps, scales, matrix, table, *refs):
    radix, inner = table.shape[1:]
    groups = data.shape[0]
    coils, _, rows, cols = maps.shape
    base, outs = (None, refs) if len(refs) == 1 else (refs[0], refs[1:])
    parts = []
    for q in range(radix):
        lines = jnp.concatenate(
            [
                jnp.transpose(
                    jnp.concatenate(
                        [
                            data[lax.bitwise_xor(g, first[1]), p, c, q]
                            for p in range(2)
                            for g in range(groups)
                        ], axis=0
                    )
                )
                for c in range(coils)
            ],
            axis=0,
        )
        result = mm(beside(split2(lines), 1), against(matrix, 0))
        part = (result[:, :inner], result[:, inner:])
        if q:
            part = turn(part, table[0, q : q + 1, :], table[1, q : q + 1, :], 1)
        parts.append(part)
    sums = [[], []]
    for a, (re, im) in enumerate(small_dft(parts, 1)):
        where = slice(a * inner, (a + 1) * inner)
        total = [0.0, 0.0]
        for c in range(coils):
            maps_real, maps_imag = maps[c, 0, :, where], maps[c, 1, :, where]
            x, y = re[c * rows : (c + 1) * rows], im[c * rows : (c + 1) * rows]
            total[0] += maps_real * x + maps_imag * y
            total[1] += maps_real * y - maps_imag * x
        for p in range(2):
            part = total[p] * scales[3:4, 0:1]
            sums[p].append(part if base is None else base[p, :, where] + part)
    lead = first[0] != 0
    for p in range(2):
        line = jnp.concatenate(sums[p], axis=1)
        if last:
            own, away = line[:, : cols // 2], line[:, cols // 2 :]
            outs[0][p] = jnp.where(lead, own, away)
            outs[1][p] = jnp.where(lead, away, own)
        else:
            outs[0][p] = line


def columns_inverse(first, data, maps, scales, chunk, chunks, base):
    _, _, coils, radix, _, rows = data.shape
    cols = maps.shape[3]
    inner = cols // radix
    c, s = fourier_parts(inner, 1.0 / math.sqrt(cols))
    matrix = halves(np.block([[c, s], [-s, c]]))
    table = turn_table(radix, inner)
    vmem = pl.BlockSpec(memory_space=pltpu.VMEM)
    last = chunk == chunks - 1
    if last:
        shape = [jax.ShapeDtypeStruct((2, rows, cols // 2), F32)] * 2
    else:
        shape = [jax.ShapeDtypeStruct((2, rows, cols), F32)]
    return pl.pallas_call(
        partial(columns_inverse_kernel, last),
        out_shape=shape,
        grid=(1,),
        in_specs=[
            pl.BlockSpec(memory_space=pltpu.SMEM),
            vmem,
            pl.BlockSpec((coils, 2, rows, cols), lambda i: (chunk, 0, 0, 0)),
            vmem,
            vmem,
            vmem,
        ]
        + [vmem] * len(base),
        out_specs=[vmem] * len(shape),
        cost_estimate=pl.CostEstimate(
            flops=24 * coils * rows * cols * inner,
            bytes_accessed=16 * coils * rows * cols,
            transcendentals=0,
        ),
        compiler_params=pltpu.CompilerParams(vmem_limit_bytes=20 * MIB),
        name="columns_inverse",
    )(first, data, maps, scales, jnp.asarray(matrix), jnp.asarray(table), *base)


def target_kernel(radix3, token, *refs):
    tiles = (len(refs) - 4) // 2
    measured, sampled = refs[:tiles], refs[tiles : 2 * tiles]
    target, kept, lines, order = refs[2 * tiles :]
    radix, pencil, _ = kept.shape
    count, height = lines.shape
    coils = count // pencil
    per = pencil // radix3

    @pl.when(pl.program_id(0) == 0)
    def _():
        source = lax.broadcasted_iota(jnp.int32, (height, LANES), 0)
        place = lax.broadcasted_iota(jnp.int32, (height, LANES), 1)
        for q in range(radix):
            order[:, q * LANES : (q + 1) * LANES] = jnp.where(
                source == radix * place + q, 1.0, 0.0
            ).astype(BF16)
        for t in range(tiles):
            for q in range(radix3):
                lines[q * per : (q + 1) * per, t * LANES : (t + 1) * LANES] = sampled[t][
                    pl.ds(q, per, stride=radix3), :
                ].astype(F32)
        picked = mm(lines[0:pencil, :].astype(BF16), order[...])
        for q in range(radix):
            kept[q] = picked[:, q * LANES : (q + 1) * LANES]

    for t in range(tiles):
        source = measured[t].reshape(count, LANES)
        for c in range(coils):
            for q in range(radix3):
                start = c * pencil + q * per
                lines[start : start + per, t * LANES : (t + 1) * LANES] = source[
                    pl.ds(q * coils + c, per, stride=radix3 * coils), :
                ]
    both = jnp.concatenate(split2(lines[...]), axis=0)
    for q in range(0, radix, 2):
        width = min(2, radix - q) * LANES
        part = order[:, q * LANES : q * LANES + width]
        picked = mm(both, part)
        picked = picked[:count] + picked[count:]
        for k in range(0, width, LANES):
            target[0, q + k // LANES] = picked[:, k : k + LANES]


def prepare_target(token, measured, sampled, radix3):
    _, pencil, coils, height = measured.shape
    radix = height // LANES
    count = pencil * coils
    return pl.pallas_call(
        partial(target_kernel, radix3),
        out_shape=(
            jax.ShapeDtypeStruct((2, radix, count, LANES), F32),
            jax.ShapeDtypeStruct((radix, pencil, LANES), F32),
        ),
        grid=(2,),
        in_specs=[pl.BlockSpec(memory_space=pltpu.SMEM)]
        + [
            pl.BlockSpec((1, pencil, coils, LANES), lambda i, t=t: (i, 0, 0, t))
            for t in range(radix)
        ]
        + [pl.BlockSpec((pencil, LANES), lambda i, t=t: (0, t)) for t in range(radix)],
        out_specs=(
            pl.BlockSpec((1, radix, count, LANES), lambda i: (i, 0, 0, 0)),
            pl.BlockSpec((radix, pencil, LANES), lambda i: (0, 0, 0)),
        ),
        scratch_shapes=[pltpu.VMEM((count, height), F32), pltpu.VMEM((height, height), BF16)],
        cost_estimate=pl.CostEstimate(
            flops=8 * count * height * height, bytes_accessed=16 * count * height, transcendentals=0
        ),
        compiler_params=pltpu.CompilerParams(vmem_limit_bytes=20 * MIB),
        name="target",
    )(token, *[measured] * radix, *[sampled] * radix)


def pairwise(groups):
    return groups <= 8 and groups & (groups - 1) == 0


def send(value):
    groups = value.shape[0]
    if not pairwise(groups):
        value = value.astype(jnp.float16)
        return [lax.all_to_all(value, "gz", split_axis=0, concat_axis=0, tiled=True)]
    return [value[0]] + [
        lax.ppermute(value[k].astype(jnp.float16), "gz", [(i, i ^ k) for i in range(groups)])
        for k in range(1, groups)
    ]


def receive(parts):
    if len(parts) == 1:
        return parts[0].astype(F32)
    return jnp.stack([part.astype(F32) for part in parts])


def after(value, *earlier):
    return lax.optimization_barrier((value, *earlier))[0]


def local(
    noisy_image, fresh_noise, coil_maps, measured, sampled, first_kernel, inner_kernels, last_kernel
):
    groups = lax.axis_size("gz")
    coils, _, rows, cols = coil_maps.shape
    height = measured.shape[3]
    radix, inner = cols // INNER, INNER
    per = inner // groups
    row_radix = height // LANES
    chunks = 2
    pencil = radix * per
    count = coils * pencil // chunks
    place = lax.axis_index("gz") if pairwise(groups) else 0
    lead = jnp.stack([lax.axis_index("col") == 0, place]).astype(jnp.int32)

    weights, scales = network_weights(
        first_kernel, inner_kernels[0], last_kernel, cols, height
    )
    top, bottom, side = halo(noisy_image)
    predicted, clean = run_network(noisy_image, top, bottom, side, edge_flags(), weights)
    other = swap_cores(clean)

    token = lead
    arrived = []
    for chunk in range(chunks):
        spectra = columns_forward(token, clean, other, coil_maps, scales, groups, chunk, chunks)
        spectra = send(spectra.reshape(groups, 2, count, rows))
        token = after(lead, spectra[0])
        arrived.append(spectra)
    target, kept = prepare_target(token, measured, sampled, radix)

    back = []
    for chunk in range(chunks):
        lines = receive(after(arrived[chunk], token))
        if rows != LANES:
            lines = jnp.transpose(lines, (1, 2, 0, 3)).reshape(2, -1, row_radix, LANES)
            lines = jnp.transpose(lines, (2, 0, 1, 3))
        lines = rows_both_ways(lead, lines, kept, target, scales, chunk * (coils // chunks) * pencil)
        if rows != LANES:
            lines = jnp.transpose(lines, (1, 2, 0, 3)).reshape(2, -1, groups, rows)
            lines = jnp.transpose(lines, (2, 0, 1, 3))
        token = lines[0]
        back.append(send(lines))

    gradient = []
    for chunk in range(chunks):
        lines = receive(after(back[chunk], *gradient))
        lines = lines.reshape(groups, 2, coils // chunks, radix, per, rows)
        gradient = columns_inverse(lead, lines, coil_maps, scales, chunk, chunks, gradient)

    own, away = gradient
    own = own + swap_cores(away)
    update = clean - STEP_GAIN * own
    return SCALE_NEXT * update + DIRECT_GAIN * predicted + NOISE_GAIN * fresh_noise


def solution(mesh):
    in_specs = (
        P("grp", "gz", "col"),
        P("grp", "gz", "col"),
        P("col", "grp", "gz", None),
        P("grp", "gz", "col", None),
        P("gz", "grp"),
        P(),
        P(),
        P(),
    )
    out_specs = P("grp", "gz", "col")

    return jax.shard_map(local, mesh=mesh, in_specs=in_specs, out_specs=out_specs, check_vma=False)
```

```python
import math
from functools import partial

import jax
import jax.numpy as jnp
import ml_dtypes
import numpy as np
from jax import lax
from jax.experimental import pallas as pl
from jax.experimental.pallas import tpu as pltpu
from jax.sharding import PartitionSpec as P

SCALE_NOW = 0.8
SIGMA_NOW = 0.6
STEP_GAIN = 1.0
SCALE_NEXT = 0.9
DIRECT_GAIN = 0.31622776601683794
NOISE_GAIN = 0.3

NOISY_MAX = 6.0
MAPS_MAX = 1.5
MEASURED_MAX = 2.4

F32 = jnp.float32
BF16 = jnp.bfloat16
LANES = 128
EDGE = 8
MIB = 1024 * 1024
INNER = 256


def ceil_to(value, step):
    return -(-value // step) * step


def tap_choice(rows, cols):
    choice = np.zeros(rows.shape + (9,), np.float32)
    for index in np.ndindex(rows.shape):
        a, b = rows[index], cols[index]
        if 0 <= a < 3 and 0 <= b < 3:
            choice[index + (3 * a + b,)] = 1.0
    return choice


def tap_choices():
    pair = np.eye(2, dtype=np.float32)
    first, last = [], []
    for c, r in np.ndindex(2, 2):
        s, d, x = np.meshgrid(*map(np.arange, (4, 4, 16)), indexing="ij")
        chosen = tap_choice(x - 5 - 2 * s - r, d - c)
        first.append(np.einsum("sdxt,hk->shdxtk", chosen, pair).reshape(512, 18))
        dr, dc = np.meshgrid(np.arange(4), np.arange(4), indexing="ij")
        chosen = tap_choice(r - dr + 2, c - dc + 2)
        last.append(np.einsum("yxt,hk->yxhtk", chosen, pair).reshape(32, 18))
    middle = []
    for cols, rows in (((0, 1), (0, 1)), ((-1, 2), (0, 1)), ((0, 1), (2, -1)), ((-1, 2), (2, -1))):
        for gamma in cols:
            for rho in rows:
                taps = []
                for c, r in np.ndindex(2, 2):
                    a, b = rho - r + 1, gamma - c + 1
                    taps.append(3 * a + b if 0 <= a < 3 and 0 <= b < 3 else None)
                middle.append(taps)
    return np.stack(first), middle, np.stack(last)


def weights_kernel(cols, height, first_taps, k2, last_taps, choice, first, inner, last, scales):
    _, middle, _ = tap_choices()
    ch = k2.shape[1]
    k1 = jnp.concatenate([first_taps[t].astype(F32) for t in range(9)], axis=0).astype(BF16)
    k3 = jnp.concatenate([last_taps[t].astype(F32) for t in range(9)], axis=0).astype(BF16)
    parts = [mm(choice[i, 0:512], k1) for i in range(4)]
    first[...] = (0.5 * jnp.concatenate(parts, axis=1)).astype(BF16).reshape(first.shape)
    turned = [(0.5 * jnp.transpose(k2[t].astype(F32))).astype(BF16) for t in range(9)]
    zero = jnp.zeros((ch, ch), BF16)
    for p, taps in enumerate(middle):
        row = [zero if t is None else turned[t] for t in taps]
        inner[p * ch : (p + 1) * ch, :] = jnp.concatenate(row, axis=1)
    parts = [mm(choice[i, 512:544], k3) for i in range(4)]
    last[...] = jnp.concatenate(parts, axis=1).astype(BF16)

    def top(value, axes):
        for axis in axes:
            value = jnp.max(value, axis=axis, keepdims=True)
        return value

    gain1 = top(jnp.sum(jnp.abs(k1.astype(F32)), axis=0, keepdims=True), (1,))
    gain2 = sum(jnp.abs(k2[t].astype(F32)) for t in range(9))
    gain2 = top(jnp.sum(gain2, axis=1, keepdims=True), (0,))
    gain3 = jnp.sum(jnp.abs(k3.astype(F32)), axis=1, keepdims=True)
    odd = lax.rem(lax.broadcasted_iota(jnp.int32, gain3.shape, 0), 2) == 1
    gain3 = jnp.maximum(
        jnp.sum(jnp.where(odd, gain3, 0.0), axis=0, keepdims=True),
        jnp.sum(jnp.where(odd, 0.0, gain3), axis=0, keepdims=True),
    )
    predicted = 1.1 * NOISY_MAX * gain1 * gain2 * gain3
    clean = (NOISY_MAX + SIGMA_NOW * predicted) / SCALE_NOW
    spectra = 1.1 * math.sqrt(cols) * 2.0 * MAPS_MAX * clean
    lines = 1.1 * math.sqrt(height) * (spectra + math.sqrt(2.0) * MEASURED_MAX)
    rows = []
    for bound in (spectra, lines):
        rows += [60000.0 / bound, bound / 60000.0]
    scales[...] = jnp.concatenate([jnp.broadcast_to(r, (1, LANES)) for r in rows + rows], axis=0)


def network_weights(first_kernel, inner_kernel, last_kernel, cols, height):
    ch = inner_kernel.shape[1]
    choice1, _, choice3 = tap_choices()
    shapes = ((4, 128, 4 * ch), (16 * ch, 4 * ch), (32, 4 * ch))
    first, inner, last, scales = pl.pallas_call(
        partial(weights_kernel, cols, height),
        out_shape=[jax.ShapeDtypeStruct(d, BF16) for d in shapes]
        + [jax.ShapeDtypeStruct((8, LANES), F32)],
        cost_estimate=pl.CostEstimate(flops=10**7, bytes_accessed=10**6, transcendentals=0),
        compiler_params=pltpu.CompilerParams(vmem_limit_bytes=10 * MIB),
        name="weights",
    )(
        jnp.transpose(first_kernel, (0, 2, 1)),
        inner_kernel,
        last_kernel,
        jnp.asarray(np.concatenate([choice1, choice3], axis=1), BF16),
    )
    return (first, inner, last), scales


def split2(value):
    high = value.astype(BF16)
    return high, (value - high.astype(F32)).astype(BF16)


def mm(lhs, rhs):
    return lax.dot_general(lhs, rhs, (((1,), (0,)), ((), ())), preferred_element_type=F32)


def mm_nt(lhs, rhs):
    return lax.dot_general(lhs, rhs, (((1,), (1,)), ((), ())), preferred_element_type=F32)


def network_kernel(
    flags, top, center, bottom, side, first, inner, last, pred, clean, tile, q, hid, hid_side, done, acc
):
    rows, cols = center.shape[1:]
    blocks = rows // 2 + 2
    used = hid.shape[1]
    step = done.shape[0] // used

    for ch in range(2):
        tile[ch, 0:8, :] = top[ch, :, 0:cols]
        tile[ch, 8 : 8 + rows, :] = center[ch]
        tile[ch, 8 + rows : 16 + rows, :] = bottom[ch, :, 0:cols]
    edge = jnp.concatenate(
        [
            part
            for ch in range(2)
            for part in (top[ch, :, cols:], side[ch], bottom[ch, :, cols:])
        ],
        axis=0,
    ).astype(BF16)
    w = lax.broadcasted_iota(jnp.int32, (cols, 256), 0)
    k = lax.broadcasted_iota(jnp.int32, (cols, 256), 1)
    e = lax.broadcasted_iota(jnp.int32, (EDGE, 256), 0) + jnp.where(flags[2] != 0, cols, -EDGE)
    ke = lax.broadcasted_iota(jnp.int32, (EDGE, 256), 1)
    for d in range(4):
        sel = jnp.where(w == 2 * k - 3 + d, 1.0, 0.0).astype(BF16)
        sel_side = jnp.where(e == 2 * ke - 3 + d, 1.0, 0.0).astype(BF16)
        both = mm(tile[...].reshape(-1, cols).astype(BF16), sel)
        both += mm(edge, sel_side)
        for ch in range(2):
            q[4 * ch + d, 0 : rows + 16] = both[ch * (rows + 16) : (ch + 1) * (rows + 16)]
            q[4 * ch + d, rows + 16 :] = jnp.zeros((8, 256), F32)

    end = cols // 2 + 1
    tail = end // 8 * 8
    lines = lax.broadcasted_iota(jnp.int32, (8, 256), 0)
    low = jnp.where((lines == 0) & (flags[2] != 0), 0.0, 1.0)
    high = jnp.where((lines == end - tail) & (flags[3] != 0), 0.0, 1.0)

    def silu_rows(half):
        h = half + half * jnp.tanh(half)
        pieces = []
        for start in range(0, h.shape[0], used):
            pieces += [
                h[start : start + 8] * low,
                h[start + 8 : start + tail],
                h[start + tail : start + tail + 8] * high,
            ]
            if tail + 8 < used:
                pieces.append(h[start + tail + 8 : start + used])
        return jnp.concatenate(pieces, axis=0)

    acc[...] = jnp.zeros(acc.shape, F32)
    hid[0] = jnp.zeros(hid.shape[1:], BF16)
    hid_side[0] = jnp.zeros(hid.shape[1:], BF16)

    def first_layer(pair, carry):
        windows = []
        for t in (2 * pair, 2 * pair + 1):
            window = q[:, pl.ds(pl.multiple_of(8 * t, 8), 16), :].reshape(128, 256)
            windows.append(jnp.transpose(window)[:used].astype(BF16))
        for n, window in enumerate(windows):
            for s in range(4):
                h = silu_rows(mm(window, first[s]))
                place = 8 * pair + 4 * n + s + 1
                hid[place] = h.astype(BF16)
                hid_side[place, :, 0:128] = pltpu.roll(h[:, 128:256], 1, 0).astype(BF16)
                hid_side[place, :, 128:256] = pltpu.roll(h[:, 0:128], used - 1, 0).astype(BF16)
        return carry

    lax.fori_loop(0, (hid.shape[0] - 1) // 8, first_layer, 0)

    for flag, j in ((0, 0), (1, blocks - 1)):

        @pl.when(flags[flag] != 0)
        def _(j=j):
            hid[j + 1] = jnp.zeros(hid.shape[1:], BF16)
            hid_side[j + 1] = jnp.zeros(hid_side.shape[1:], BF16)

    lane = lax.broadcasted_iota(jnp.int32, (step * used, 256), 1)
    below = lax.rem(lane, 128) < 64

    def next_layers(i, carry):
        j = step * i

        def around(ref, offset):
            return ref[pl.ds(j + offset, step)].reshape(step * used, 256)

        lhs = jnp.concatenate(
            [
                around(hid, 1),
                around(hid_side, 1),
                jnp.where(below, around(hid, 2), around(hid, 0)),
                jnp.where(below, around(hid_side, 2), around(hid_side, 0)),
            ],
            axis=1,
        )
        add_parts(j - step)
        done[...] = silu_rows(mm(lhs, inner[...])).astype(BF16)
        return carry

    def add_parts(j):
        for u in range(step):
            part = mm_nt(last[...], done[u * used : (u + 1) * used])
            row = j + u
            gone = ((row == 0) & (flags[0] != 0)) | ((row == blocks - 1) & (flags[1] != 0))
            part = part * jnp.where(gone, 0.0, 1.0)
            where = pl.ds(pl.multiple_of(16 * (row + step), 16), 32)
            for c in range(0, used, 128):
                width = min(128, used - c)
                acc[c // 128, where, 0:width] = acc[c // 128, where, 0:width] + part[:, c : c + width]

    done[...] = jnp.zeros(done.shape, BF16)
    lax.fori_loop(0, blocks // step, next_layers, 0)
    add_parts(blocks - step)

    def pixels(d):
        return jnp.concatenate(
            [
                jnp.concatenate(
                    [
                        acc[c, pl.ds(24 + 16 * step + 2 * d + ch, rows, stride=8), :]
                        for c in range(2)
                    ],
                    axis=1,
                )
                for ch in range(2)
            ],
            axis=0,
        )

    k = lax.broadcasted_iota(jnp.int32, (256, cols), 0)
    w = lax.broadcasted_iota(jnp.int32, (256, cols), 1)
    total = 0.0
    for d, other, shift in ((1, 3, 1), (2, 0, 255)):
        line = pixels(d) + pltpu.roll(pixels(other), shift, 1)
        sel = jnp.where(w == 2 * k - 3 + d, 1.0, 0.0).astype(BF16)
        both = mm(jnp.concatenate(split2(line), axis=0), sel)
        total += both[: 2 * rows] + both[2 * rows :]
    for ch in range(2):
        part = total[ch * rows : (ch + 1) * rows]
        pred[ch] = part
        clean[ch] = (center[ch] - SIGMA_NOW * part) / SCALE_NOW


def run_network(noisy, top, bottom, side, flags, weights):
    _, rows, cols = noisy.shape
    blocks = rows // 2 + 2
    pairs = -(-blocks // 8)
    used = ceil_to(cols // 2 + 2, 16)
    step = max(u for u in (1, 2, 3, 6) if blocks % u == 0)
    vmem = pl.BlockSpec(memory_space=pltpu.VMEM)
    shape = jax.ShapeDtypeStruct(noisy.shape, F32)
    return pl.pallas_call(
        network_kernel,
        out_shape=(shape, shape),
        in_specs=[pl.BlockSpec(memory_space=pltpu.SMEM)] + [vmem] * 7,
        out_specs=(vmem, vmem),
        scratch_shapes=[
            pltpu.VMEM((2, rows + 16, cols), F32),
            pltpu.VMEM((8, rows + 24, 256), F32),
            pltpu.VMEM((8 * pairs + 1, used, 256), BF16),
            pltpu.VMEM((8 * pairs + 1, used, 256), BF16),
            pltpu.VMEM((step * used, 256), BF16),
            pltpu.VMEM((2, 16 * (blocks + step) + 16, 128), F32),
        ],
        cost_estimate=pl.CostEstimate(
            flops=20 * rows * cols * 64 * 64, bytes_accessed=24 * rows * cols, transcendentals=0
        ),
        compiler_params=pltpu.CompilerParams(vmem_limit_bytes=40 * MIB),
        name="network",
    )(flags, top, noisy, bottom, side, *weights)


def halo(noisy):
    gz = lax.axis_size("gz")
    _, rows, cols = noisy.shape
    left, right = noisy[:, :, :EDGE], noisy[:, :, cols - EDGE :]
    side = swap_cores(jnp.where(lax.axis_index("col") == 0, right, left))
    down = [(i, i + 1) for i in range(gz - 1)]
    lower = jnp.concatenate([noisy[:, rows - EDGE :], side[:, rows - EDGE :]], axis=2)
    upper = jnp.concatenate([noisy[:, :EDGE], side[:, :EDGE]], axis=2)
    top = lax.ppermute(lower, "gz", down)
    bottom = lax.ppermute(upper, "gz", [(b, a) for a, b in down])
    return top, bottom, side


def swap_cores(value):
    assert lax.axis_size("col") == 2
    return lax.ppermute(value, "col", [(0, 1), (1, 0)])


def edge_flags():
    row, col = lax.axis_index("gz"), lax.axis_index("col")
    last_row, last_col = lax.axis_size("gz") - 1, lax.axis_size("col") - 1
    return jnp.stack([row == 0, row == last_row, col == 0, col == last_col]).astype(jnp.int32)


def halves(matrix):
    high = matrix.astype(ml_dtypes.bfloat16)
    low = (matrix - high.astype(np.float64)).astype(ml_dtypes.bfloat16)
    return np.stack([high, low])


def fourier_parts(length, scale):
    index = np.arange(length)
    angle = 2.0 * np.pi * (np.outer(index, index) % length) / length
    return np.cos(angle) * scale, np.sin(angle) * scale


def turn_table(radix, inner):
    angle = 2.0 * np.pi * np.outer(np.arange(radix), np.arange(inner)) / (radix * inner)
    return np.stack([np.cos(angle), np.sin(angle)]).astype(np.float32)


def small_dft(values, sign):
    n = len(values)
    if n == 1:
        return values
    if n % 2 == 0:
        even = small_dft(values[0::2], sign)
        odd = small_dft(values[1::2], sign)
        low, high = [], []
        for q in range(n // 2):
            re, im = times_unit(odd[q], q, n, sign)
            low.append((even[q][0] + re, even[q][1] + im))
            high.append((even[q][0] - re, even[q][1] - im))
        return low + high
    if n == 3:
        (r0, i0), (r1, i1), (r2, i2) = values
        sr, si = r1 + r2, i1 + i2
        half = math.sqrt(3.0) / 2.0 * sign
        dr, di = half * (r1 - r2), half * (i1 - i2)
        tr, ti = r0 - 0.5 * sr, i0 - 0.5 * si
        return [(r0 + sr, i0 + si), (tr - di, ti + dr), (tr + di, ti - dr)]
    out = []
    for q in range(n):
        terms = [times_unit(v, a * q, n, sign) for a, v in enumerate(values)]
        out.append((sum(t[0] for t in terms), sum(t[1] for t in terms)))
    return out


def times_unit(value, power, n, sign):
    re, im = value
    power %= n
    if power == 0:
        return re, im
    if 4 * power == n:
        return (-im, re) if sign > 0 else (im, -re)
    if 2 * power == n:
        return -re, -im
    if 4 * power == 3 * n:
        return (im, -re) if sign > 0 else (-im, re)
    c = math.cos(2.0 * math.pi * power / n)
    s = sign * math.sin(2.0 * math.pi * power / n)
    return c * re - s * im, c * im + s * re


def turn(value, cos, sin, sign):
    re, im = value
    if sign > 0:
        return re * cos - im * sin, im * cos + re * sin
    return re * cos + im * sin, im * cos - re * sin


def beside(parts, axis):
    return jnp.concatenate([parts[0], parts[0], parts[1]], axis=axis)


def against(matrix, axis):
    return jnp.concatenate([matrix[0], matrix[1], matrix[0]], axis=axis)


def columns_forward_kernel(first, mine, other, maps, scales, matrix, table, out):
    radix, inner = table.shape[1:]
    coils = maps.shape[0]
    rows, _ = mine.shape[1:]
    groups = out.shape[0]
    per = inner // groups
    lead, me = first[0] != 0, first[1]
    image = [
        jnp.concatenate(
            [jnp.where(lead, mine[p], other[p]), jnp.where(lead, other[p], mine[p])], axis=1
        )
        * scales[0:1, 0:1]
        for p in range(2)
    ]
    turned = []
    for coil in range(coils):
        maps_real, maps_imag = maps[coil, 0], maps[coil, 1]
        coil_image = (
            maps_real * image[0] - maps_imag * image[1],
            maps_real * image[1] + maps_imag * image[0],
        )
        parts = [
            tuple(v[:, a * inner : (a + 1) * inner] for v in coil_image) for a in range(radix)
        ]
        parts = small_dft(parts, -1)
        turned.append(
            [
                turn(part, table[0, q : q + 1, :], table[1, q : q + 1, :], -1) if q else part
                for q, part in enumerate(parts)
            ]
        )
    for q in range(radix):
        data = jnp.concatenate([jnp.concatenate(turned[c][q], axis=1) for c in range(coils)], axis=0)
        result = mm_nt(against(matrix, 1), beside(split2(data), 1))
        for p in range(2):
            for g in range(groups):
                start = p * inner + g * per
                for c in range(coils):
                    out[lax.bitwise_xor(g, me), p, c, q] = result[start : start + per, c * rows : (c + 1) * rows]


def columns_forward(first, mine, other, maps, scales, groups, chunk, chunks):
    coils, _, rows, cols = maps.shape
    coils //= chunks
    inner = INNER
    radix = cols // inner
    c, s = fourier_parts(inner, 1.0 / math.sqrt(cols))
    matrix = halves(np.block([[c, s], [-s, c]]))
    table = turn_table(radix, inner)
    vmem = pl.BlockSpec(memory_space=pltpu.VMEM)
    per = inner // groups
    return pl.pallas_call(
        columns_forward_kernel,
        out_shape=jax.ShapeDtypeStruct((groups, 2, coils, radix, per, rows), F32),
        grid=(1,),
        in_specs=[
            pl.BlockSpec(memory_space=pltpu.SMEM),
            vmem,
            vmem,
            pl.BlockSpec((coils, 2, rows, cols), lambda i: (chunk, 0, 0, 0)),
            vmem,
            vmem,
            vmem,
        ],
        out_specs=pl.BlockSpec(
            (groups, 2, coils, radix, per, rows), lambda i: (0, 0, 0, 0, 0, 0)
        ),
        cost_estimate=pl.CostEstimate(
            flops=24 * coils * rows * cols * inner,
            bytes_accessed=16 * coils * rows * cols,
            transcendentals=0,
        ),
        compiler_params=pltpu.CompilerParams(vmem_limit_bytes=20 * MIB),
        name="columns_forward",
    )(first, mine, other, maps, scales, jnp.asarray(matrix), jnp.asarray(table))


def rows_kernel(place, data, kept, target, scales, forward, inverse, table, out, lines):
    radix = table.shape[1]
    count = data.shape[2]
    spots = [lax.bitwise_xor(a, place[1]) for a in range(radix)]
    parts = small_dft([(data[spot, 0], data[spot, 1]) for spot in spots], -1)
    for q, part in enumerate(parts):
        if q:
            part = turn(part, table[0, q : q + 1, :], table[1, q : q + 1, :], -1)
        for p in range(2):
            lines[q * count : (q + 1) * count, p * LANES : (p + 1) * LANES] = part[p]
    spectrum = mm(beside(split2(lines[...]), 1), against(forward, 0))
    keep = kept[...].reshape(radix * count, LANES) * scales[2:3, :]
    unit = scales[1:2, :]
    residual = jnp.concatenate(
        [
            keep
            * (spectrum[:, p * LANES : (p + 1) * LANES] * unit - target[p].reshape(-1, LANES))
            for p in range(2)
        ],
        axis=1,
    )
    lines[...] = mm(beside(split2(residual), 1), against(inverse, 0))
    back = []
    for q in range(radix):
        part = tuple(
            lines[q * count : (q + 1) * count, p * LANES : (p + 1) * LANES] for p in range(2)
        )
        if q:
            part = turn(part, table[0, q : q + 1, :], table[1, q : q + 1, :], 1)
        back.append(part)
    for spot, (re, im) in zip(spots, small_dft(back, 1)):
        out[spot, 0] = re
        out[spot, 1] = im


def rows_both_ways(place, data, kept, target, scales, first_line):
    radix, _, count, _ = data.shape
    pencil = kept.shape[1]
    c, s = fourier_parts(LANES, 1.0 / math.sqrt(radix * LANES))
    forward = halves(np.block([[c, -s], [s, c]]))
    inverse = halves(np.block([[c, s], [-s, c]]))
    table = turn_table(radix, LANES)
    block = max(b for b in range(8, 104, 8) if pencil % b == 0)
    offset, repeat = first_line // block, pencil // block
    vmem = pl.BlockSpec(memory_space=pltpu.VMEM)
    spec = pl.BlockSpec((radix, 2, block, LANES), lambda i: (0, 0, i, 0))
    return pl.pallas_call(
        rows_kernel,
        out_shape=jax.ShapeDtypeStruct(data.shape, F32),
        grid=(count // block,),
        in_specs=[
            pl.BlockSpec(memory_space=pltpu.SMEM),
            spec,
            pl.BlockSpec((radix, block, LANES), lambda i: (0, lax.rem(i + offset, repeat), 0)),
            pl.BlockSpec((2, radix, block, LANES), lambda i: (0, 0, i + offset, 0)),
            vmem,
            vmem,
            vmem,
            vmem,
        ],
        out_specs=spec,
        scratch_shapes=[pltpu.VMEM((radix * block, 2 * LANES), F32)],
        cost_estimate=pl.CostEstimate(
            flops=24 * radix * count * LANES * LANES,
            bytes_accessed=32 * radix * count * LANES,
            transcendentals=0,
        ),
        compiler_params=pltpu.CompilerParams(vmem_limit_bytes=12 * MIB),
        name="rows_both_ways",
    )(place, data, kept, target, scales, jnp.asarray(forward), jnp.asarray(inverse), jnp.asarray(table))


def columns_inverse_kernel(last, first, data, maps, scales, matrix, table, *refs):
    radix, inner = table.shape[1:]
    groups = data.shape[0]
    coils, _, rows, cols = maps.shape
    base, outs = (None, refs) if len(refs) == 1 else (refs[0], refs[1:])
    parts = []
    for q in range(radix):
        lines = jnp.concatenate(
            [
                jnp.transpose(
                    jnp.concatenate(
                        [
                            data[lax.bitwise_xor(g, first[1]), p, c, q]
                            for p in range(2)
                            for g in range(groups)
                        ], axis=0
                    )
                )
                for c in range(coils)
            ],
            axis=0,
        )
        result = mm(beside(split2(lines), 1), against(matrix, 0))
        part = (result[:, :inner], result[:, inner:])
        if q:
            part = turn(part, table[0, q : q + 1, :], table[1, q : q + 1, :], 1)
        parts.append(part)
    sums = [[], []]
    for a, (re, im) in enumerate(small_dft(parts, 1)):
        where = slice(a * inner, (a + 1) * inner)
        total = [0.0, 0.0]
        for c in range(coils):
            maps_real, maps_imag = maps[c, 0, :, where], maps[c, 1, :, where]
            x, y = re[c * rows : (c + 1) * rows], im[c * rows : (c + 1) * rows]
            total[0] += maps_real * x + maps_imag * y
            total[1] += maps_real * y - maps_imag * x
        for p in range(2):
            part = total[p] * scales[3:4, 0:1]
            sums[p].append(part if base is None else base[p, :, where] + part)
    lead = first[0] != 0
    for p in range(2):
        line = jnp.concatenate(sums[p], axis=1)
        if last:
            own, away = line[:, : cols // 2], line[:, cols // 2 :]
            outs[0][p] = jnp.where(lead, own, away)
            outs[1][p] = jnp.where(lead, away, own)
        else:
            outs[0][p] = line


def columns_inverse(first, data, maps, scales, chunk, chunks, base):
    _, _, coils, radix, _, rows = data.shape
    cols = maps.shape[3]
    inner = cols // radix
    c, s = fourier_parts(inner, 1.0 / math.sqrt(cols))
    matrix = halves(np.block([[c, s], [-s, c]]))
    table = turn_table(radix, inner)
    vmem = pl.BlockSpec(memory_space=pltpu.VMEM)
    last = chunk == chunks - 1
    if last:
        shape = [jax.ShapeDtypeStruct((2, rows, cols // 2), F32)] * 2
    else:
        shape = [jax.ShapeDtypeStruct((2, rows, cols), F32)]
    return pl.pallas_call(
        partial(columns_inverse_kernel, last),
        out_shape=shape,
        grid=(1,),
        in_specs=[
            pl.BlockSpec(memory_space=pltpu.SMEM),
            vmem,
            pl.BlockSpec((coils, 2, rows, cols), lambda i: (chunk, 0, 0, 0)),
            vmem,
            vmem,
            vmem,
        ]
        + [vmem] * len(base),
        out_specs=[vmem] * len(shape),
        cost_estimate=pl.CostEstimate(
            flops=24 * coils * rows * cols * inner,
            bytes_accessed=16 * coils * rows * cols,
            transcendentals=0,
        ),
        compiler_params=pltpu.CompilerParams(vmem_limit_bytes=20 * MIB),
        name="columns_inverse",
    )(first, data, maps, scales, jnp.asarray(matrix), jnp.asarray(table), *base)


def target_kernel(radix3, token, *refs):
    tiles = (len(refs) - 4) // 2
    measured, sampled = refs[:tiles], refs[tiles : 2 * tiles]
    target, kept, lines, order = refs[2 * tiles :]
    radix, pencil, _ = kept.shape
    count, height = lines.shape
    coils = count // pencil
    per = pencil // radix3
    size = order.shape[0]
    span = size // radix

    def reordered(value):
        pieces = [mm(value[:, k : k + size], order[...]) for k in range(0, height, size)]
        if value.shape[0] > count:
            pieces = [piece[:count] + piece[count:] for piece in pieces]
        return [
            jnp.concatenate([piece[:, q * span : (q + 1) * span] for piece in pieces], axis=1)
            for q in range(radix)
        ]

    @pl.when(pl.program_id(0) == 0)
    def _():
        source = lax.broadcasted_iota(jnp.int32, order.shape, 0)
        place = lax.broadcasted_iota(jnp.int32, order.shape, 1)
        place = radix * lax.rem(place, span) + lax.div(place, span)
        order[...] = jnp.where(source == place, 1.0, 0.0).astype(BF16)
        for t in range(tiles):
            for q in range(radix3):
                lines[q * per : (q + 1) * per, t * LANES : (t + 1) * LANES] = sampled[t][
                    pl.ds(q, per, stride=radix3), :
                ].astype(F32)
        for q, part in enumerate(reordered(lines[0:pencil, :].astype(BF16))):
            kept[q] = part

    for t in range(tiles):
        source = measured[t].reshape(count, LANES)
        for c in range(coils):
            for q in range(radix3):
                start = c * pencil + q * per
                lines[start : start + per, t * LANES : (t + 1) * LANES] = source[
                    pl.ds(q * coils + c, per, stride=radix3 * coils), :
                ]
    both = jnp.concatenate(split2(lines[...]), axis=0)
    for q, part in enumerate(reordered(both)):
        target[0, q] = part


def prepare_target(token, measured, sampled, radix3):
    _, pencil, coils, height = measured.shape
    radix = height // LANES
    count = pencil * coils
    return pl.pallas_call(
        partial(target_kernel, radix3),
        out_shape=(
            jax.ShapeDtypeStruct((2, radix, count, LANES), F32),
            jax.ShapeDtypeStruct((radix, pencil, LANES), F32),
        ),
        grid=(2,),
        in_specs=[pl.BlockSpec(memory_space=pltpu.SMEM)]
        + [
            pl.BlockSpec((1, pencil, coils, LANES), lambda i, t=t: (i, 0, 0, t))
            for t in range(radix)
        ]
        + [pl.BlockSpec((pencil, LANES), lambda i, t=t: (0, t)) for t in range(radix)],
        out_specs=(
            pl.BlockSpec((1, radix, count, LANES), lambda i: (i, 0, 0, 0)),
            pl.BlockSpec((radix, pencil, LANES), lambda i: (0, 0, 0)),
        ),
        scratch_shapes=[pltpu.VMEM((count, height), F32), pltpu.VMEM((INNER, INNER), BF16)],
        cost_estimate=pl.CostEstimate(
            flops=8 * count * height * height, bytes_accessed=16 * count * height, transcendentals=0
        ),
        compiler_params=pltpu.CompilerParams(vmem_limit_bytes=20 * MIB),
        name="target",
    )(token, *[measured] * radix, *[sampled] * radix)


def pairwise(groups):
    return groups <= 8 and groups & (groups - 1) == 0


def send(value):
    groups = value.shape[0]
    if not pairwise(groups):
        value = value.astype(jnp.float16)
        return [lax.all_to_all(value, "gz", split_axis=0, concat_axis=0, tiled=True)]
    blocks = [value[0]]
    for k in range(1, groups):
        half = value[k].astype(jnp.float16)
        blocks.append(lax.ppermute(half, "gz", [(i, i ^ k) for i in range(groups)]))
    return blocks


def receive(parts):
    if len(parts) == 1:
        return parts[0].astype(F32)
    return jnp.stack([part.astype(F32) for part in parts])


def after(value, *earlier):
    return lax.optimization_barrier((value, *earlier))[0]


def local(
    noisy_image, fresh_noise, coil_maps, measured, sampled, first_kernel, inner_kernels, last_kernel
):
    groups = lax.axis_size("gz")
    coils, _, rows, cols = coil_maps.shape
    height = measured.shape[3]
    radix, inner = cols // INNER, INNER
    per = inner // groups
    row_radix = height // LANES
    chunks = 2
    pencil = radix * per
    count = coils * pencil // chunks
    place = lax.axis_index("gz") if pairwise(groups) else 0
    lead = jnp.stack([lax.axis_index("col") == 0, place]).astype(jnp.int32)

    weights, scales = network_weights(
        first_kernel, inner_kernels[0], last_kernel, cols, height
    )
    top, bottom, side = halo(noisy_image)
    predicted, clean = run_network(noisy_image, top, bottom, side, edge_flags(), weights)
    other = swap_cores(clean)

    token = lead
    arrived = []
    for chunk in range(chunks):
        spectra = columns_forward(token, clean, other, coil_maps, scales, groups, chunk, chunks)
        spectra = send(spectra.reshape(groups, 2, count, rows))
        token = after(lead, spectra[0])
        arrived.append(spectra)
    target, kept = prepare_target(token, measured, sampled, radix)

    back = []
    for chunk in range(chunks):
        lines = receive(arrived[chunk])
        if rows != LANES:
            lines = jnp.transpose(lines, (1, 2, 0, 3)).reshape(2, -1, row_radix, LANES)
            lines = jnp.transpose(lines, (2, 0, 1, 3))
        lines = rows_both_ways(lead, lines, kept, target, scales, chunk * (coils // chunks) * pencil)
        if rows != LANES:
            lines = jnp.transpose(lines, (1, 2, 0, 3)).reshape(2, -1, groups, rows)
            lines = jnp.transpose(lines, (2, 0, 1, 3))
        token = lines[0]
        back.append(send(lines))

    gradient = []
    for chunk in range(chunks):
        lines = receive(after(back[chunk], *gradient))
        lines = lines.reshape(groups, 2, coils // chunks, radix, per, rows)
        gradient = columns_inverse(lead, lines, coil_maps, scales, chunk, chunks, gradient)

    own, away = gradient
    own = own + swap_cores(away)
    update = clean - STEP_GAIN * own
    return SCALE_NEXT * update + DIRECT_GAIN * predicted + NOISE_GAIN * fresh_noise


def solution(mesh):
    in_specs = (
        P("grp", "gz", "col"),
        P("grp", "gz", "col"),
        P("col", "grp", "gz", None),
        P("grp", "gz", "col", None),
        P("gz", "grp"),
        P(),
        P(),
        P(),
    )
    out_specs = P("grp", "gz", "col")

    return jax.shard_map(local, mesh=mesh, in_specs=in_specs, out_specs=out_specs, check_vma=False)
```
